32 devices in a mesh: stream: 2 (over x), group: 8 (over z, y), dp: 2 (over core).
Axes of the slice: x: 2, y: 2, z: 4, core: 2. Of those that a mesh axis runs over, the one named last changes fastest.
Arguments:
- tokens: bfloat16 [2, 8192, 768], P('stream', ('group', 'dp')), may hold values from -6 to 6
- cotangent: bfloat16 [2, 8192, 768], P('stream', ('group', 'dp')), may hold values from -6 to 6
- box_bins: int32 [2, 2, 16, 512], P(None, None, ('group', 'dp')), may hold values from 0 to 127
- segment_ids: int32 [2, 16, 512], P(None, ('group', 'dp')), may hold values from 0 to 63, never falling along the last dimension, each value on 1 to 16 neighbouring positions
- key_mask: int32 [2, 16, 512], P(None, ('group', 'dp')), may hold values from 0 to 1, as said below
- ln1_gain: float32 [2, 768], P('stream'), may hold values from 0.5 to 1.5
- ln1_bias: float32 [2, 768], P('stream'), may hold values from -1.75 to 1.75
- w_qkv: bfloat16 [2, 768, 2304], P('stream'), may hold values from -0.21875 to 0.21875
- bias_q: float32 [2, 768], P('stream'), may hold values from -1.75 to 1.75
- bias_v: float32 [2, 768], P('stream'), may hold values from -1.75 to 1.75
- w_out: bfloat16 [2, 768, 768], P('stream'), may hold values from -1.75 to 1.75
- bias_out: float32 [2, 768], P('stream'), may hold values from -1.75 to 1.75
- ln2_gain: float32 [2, 768], P('stream'), may hold values from 0.5 to 1.5
- ln2_bias: float32 [2, 768], P('stream'), may hold values from -1.75 to 1.75
- w_in: bfloat16 [2, 768, 3072], P('stream'), may hold values from -0.21875 to 0.21875
- bias_in: float32 [2, 3072], P('stream'), may hold values from -3 to 3
- w_back: bfloat16 [2, 3072, 768], P('stream'), may hold values from -0.109375 to 0.109375
- bias_back: float32 [2, 768], P('stream'), may hold values from -1.75 to 1.75
- rel_table: float32 [2, 4608], P('stream'), may hold values from -3 to 3
Outputs:
- output: bfloat16 [2, 8192, 768], P('stream', ('group', 'dp'))
- g_tokens: bfloat16 [2, 8192, 768], P('stream', ('group', 'dp'))
- g_ln1_gain: float32 [2, 768], P('stream', 'dp')
- g_ln1_bias: float32 [2, 768], P('stream', 'dp')
- g_w_qkv: float32 [2, 768, 2304], P('stream', 'dp')
- g_bias_q: float32 [2, 768], P('stream', 'dp')
- g_bias_v: float32 [2, 768], P('stream', 'dp')
- g_w_out: float32 [2, 768, 768], P('stream', 'dp')
- g_bias_out: float32 [2, 768], P('stream', 'dp')
- g_ln2_gain: float32 [2, 768], P('stream', 'dp')
- g_ln2_bias: float32 [2, 768], P('stream', 'dp')
- g_w_in: float32 [2, 768, 3072], P('stream', 'dp')
- g_bias_in: float32 [2, 3072], P('stream', 'dp')
- g_w_back: float32 [2, 3072, 768], P('stream', 'dp')
- g_bias_back: float32 [2, 768], P('stream', 'dp')
- g_rel_table: float32 [2, 4608], P('stream', 'dp')
The draws below stay inside these ranges and needn't reach their ends.
Inputs may be any that keep to these rules, and one draw needn't show every extreme that they name: `key_mask`: the first token of every page is 1 in each stream. `segment_ids`: within a page the segment number never falls, every one of the 64 segments is present, each with 1 to 16 tokens.
All inputs are finite; a program needn't handle non-finite values.
Results may differ from the reference program's by a relative error of at most 0.012.
Values may be sent and summed in bfloat16 or wider, within the bound.
No kernel may reach another device: no remote copies, remote signals or barrier semaphores. Data moves between devices by JAX's collectives and lax.ppermute only.
A program may use at most 256 MiB of HBM per device.

```python
import math
import jax
import jax.numpy as jnp
import numpy as np
from jax import lax

D = 768
HEADS = 12
FF = 3072
BINS = 128
SEGS = 64
PAGE = 512
PAGES = 16
TOKENS = 8192


def draw_key_mask(key, part):
    levels = jax.random.randint(key, (2, PAGES, PAGE), 0, 8)
    places = lax.broadcasted_iota(jnp.int32, (2, PAGES, PAGE), 2)
    return jnp.where(places == 0, 1, jnp.minimum(levels, 1)).astype(jnp.int32)


def touch_ends(values, stream_key, least, largest):
    dims = values.shape
    spot = [jax.random.randint(jax.random.fold_in(stream_key, axis), (), 0, dims[axis]) for axis in range(len(dims))]
    values = values.at[tuple(spot)].set(least)
    longest = dims.index(max(dims))
    spot[longest] = (spot[longest] + 1) % dims[longest]
    return values.at[tuple(spot)].set(largest)


def spiked(entries, key, source, target, blocks, factor):
    owner, partner = [(jnp.arange(entries.shape[dim]) // (entries.shape[dim] // blocks)).reshape([-1 if axis == dim else 1 for axis in range(entries.ndim)]) for dim in (source, target)]
    chosen = jax.random.permutation(key, blocks)[partner]
    strong = (owner == chosen) | (owner == (partner + blocks // 2) % blocks)
    return jnp.where(strong, factor * entries, entries)


def block_levels(key, extent, split, least, high):
    factor_of = 1.0
    for dim, parts in split:
        draws = jax.random.uniform(jax.random.fold_in(jax.random.fold_in(key, 6), dim), (parts,), jnp.float32, least / len(split), high / len(split))
        factor_of = factor_of * jnp.repeat(jnp.exp(draws), extent[dim] // parts).reshape((-1,) + (1,) * (len(extent) - 1 - dim))
    return factor_of


def profile(amount, total, limit, lean):
    weights = [(1 << 20) // math.isqrt(grade ** lean) + 1 for grade in range(2, amount + 1)]
    rest, given = total - limit - (amount - 1), [1] * (amount - 1)
    while rest > 0:
        movable = [i for i in range(amount - 1) if given[i] < limit]
        whole, budget = sum([weights[i] for i in movable]), rest
        for i in movable:
            extra = min(limit - given[i], max(1, budget * weights[i] // whole), rest)
            given[i] = given[i] + extra
            rest = rest - extra
    return np.array([limit] + given)


def uneven_parts(rng, amount, total, most, lean):
    if amount == 2:
        one = jax.random.randint(rng, (), max(1, total - most), min(most, total - 1) + 1)
        return jnp.stack([one, total - one])
    lengths = jnp.asarray(profile(amount, total, most, lean), jnp.int32)
    twos = (amount - 1) // 2
    donor, sink = lengths[1:1 + 2 * twos:2], lengths[2:2 + 2 * twos:2]
    margin = jnp.minimum(donor - 1, most - sink)
    passed = jax.random.randint(jax.random.fold_in(rng, 1), (twos,), 0, 1 << 20) % (margin + 1)
    lengths = lengths.at[1:1 + 2 * twos:2].set(donor - passed).at[2:2 + 2 * twos:2].set(sink + passed)
    return lengths[jax.random.permutation(jax.random.fold_in(rng, 2), amount)]


def normal_values(stream_key, dims, deviation, most, shards=(), dtype=jnp.bfloat16):
    values = deviation * jax.random.normal(stream_key, dims, jnp.float32)
    if shards:
        values = values * block_levels(stream_key, dims, shards, -0.22, 0.18)
    return jnp.clip(values, -most, most).astype(dtype)


def heavy_noise(key, dims, width, bound, cuts, heavy, dtype=jnp.bfloat16):
    drawn = width * jax.random.normal(key, dims, jnp.float32)
    if cuts:
        drawn = drawn * block_levels(key, dims, cuts, -0.22, 0.18)
    return jnp.clip(spiked(drawn, jax.random.fold_in(key, 3), *heavy), -bound, bound).astype(dtype)


def setup_inputs(seed: int = 0) -> dict:
    arg_keys = jax.random.split(jax.random.key(seed), 20)
    return {
        "tokens": normal_values(arg_keys[0], (2, TOKENS, D), 1.0, 6.0, ((0, 2), (1, 16))),
        "cotangent": heavy_noise(arg_keys[1], (2, TOKENS, D), 1.0, 6.0, ((0, 2), (1, 16)), (1, 2, 16, 2.0)),
        "box_bins": touch_ends(jax.random.randint(arg_keys[2], (2, 2, PAGES, PAGE), 0, BINS), jax.random.fold_in(arg_keys[2], 1), 0, BINS - 1).astype(jnp.int32),
        "segment_ids": jax.vmap(lambda own: jnp.searchsorted(jnp.cumsum(uneven_parts(own, SEGS, PAGE, 2 * PAGE // SEGS, 2)), jnp.arange(PAGE), side="right"))(jax.random.split(arg_keys[3], 2 * PAGES)).reshape((2, PAGES, PAGE)).astype(jnp.int32),
        "key_mask": draw_key_mask(jax.random.fold_in(arg_keys[19], 71), 0),
        "ln1_gain": jnp.clip(1.0 + 0.1 * jax.random.normal(arg_keys[5], (2, D), jnp.float32), 0.5, 1.5),
        "ln1_bias": normal_values(arg_keys[6], (2, D), 0.3, 1.75, ((0, 2),), jnp.float32),
        "w_qkv": normal_values(arg_keys[7], (2, D, 3 * D), D ** -0.5, 0.21875, ((0, 2),)),
        "bias_q": normal_values(arg_keys[8], (2, D), 0.3, 1.75, ((0, 2),), jnp.float32),
        "bias_v": normal_values(arg_keys[9], (2, D), 0.3, 1.75, ((0, 2),), jnp.float32),
        "w_out": normal_values(arg_keys[10], (2, D, D), (D // 64) ** -0.5, 1.75, ((0, 2),)),
        "bias_out": normal_values(arg_keys[11], (2, D), 0.3, 1.75, ((0, 2),), jnp.float32),
        "ln2_gain": jnp.clip(1.0 + 0.1 * jax.random.normal(arg_keys[12], (2, D), jnp.float32), 0.5, 1.5),
        "ln2_bias": normal_values(arg_keys[13], (2, D), 0.3, 1.75, ((0, 2),), jnp.float32),
        "w_in": normal_values(arg_keys[14], (2, D, FF), D ** -0.5, 0.21875, ((0, 2),)),
        "bias_in": normal_values(arg_keys[15], (2, FF), 0.5, 3.0, ((0, 2),), jnp.float32),
        "w_back": normal_values(arg_keys[16], (2, FF, D), FF ** -0.5, 0.109375, ((0, 2),)),
        "bias_back": normal_values(arg_keys[17], (2, D), 0.3, 1.75, ((0, 2),), jnp.float32),
        "rel_table": normal_values(arg_keys[18], (2, 3 * HEADS * BINS), 0.5, 3.0, ((0, 2),), jnp.float32),
    }


@jax.custom_vjp
def low(v):
    return lax.optimization_barrier(v.astype(jnp.bfloat16)).astype(jnp.float32)

@jax.custom_vjp
def low_back(v):
    return v

def low_keep(v):
    return (low(v), None)

def low_pass(kept, grad):
    return (grad,)

def back_keep(v):
    return (v, None)

def back_low(kept, grad):
    return (low(grad),)
low.defvjp(low_keep, low_pass)
low_back.defvjp(back_keep, back_low)
EPSILON = 1e-05
NEGATIVE = -1000000000.0
HIGHEST = lax.Precision.HIGHEST

def norm_rows(values, gain_row, shift_row):
    center = values - lax.optimization_barrier(jnp.mean(values, axis=-1, keepdims=True))
    spread = lax.optimization_barrier(jnp.mean(center * center, axis=-1, keepdims=True))
    return center * lax.rsqrt(spread + EPSILON) * gain_row + shift_row

def exact_gelu(values):
    return jax.nn.gelu(values, approximate=False)

def branch_inputs(rows_in, gain_first, shift_first, pack_weight, query_bias, value_bias):
    model_width = rows_in.shape[1]
    normed = low(norm_rows(rows_in, gain_first, shift_first))
    packed = jnp.dot(normed, pack_weight, precision=HIGHEST)
    queries = low(low_back(packed[:, :model_width] + query_bias))
    key_rows = low(low_back(packed[:, model_width:2 * model_width]))
    value_rows = low(low_back(packed[:, 2 * model_width:] + value_bias))
    return (queries, key_rows, value_rows)

def attend(queries, key_rows, value_rows, table_low, query_codes, key_codes, key_live):
    length, model_width = queries.shape
    head_size = model_width // HEADS
    half_bins = BINS // 2
    query_heads = queries.reshape(length, HEADS, head_size)
    key_heads = key_rows.reshape(length, HEADS, head_size)
    value_heads = value_rows.reshape(length, HEADS, head_size)
    scores = jnp.einsum('ihd,jhd->hij', query_heads, key_heads, precision=HIGHEST) * head_size ** (-0.5)
    for code_axis in range(3):
        offset_index = jnp.clip(query_codes[code_axis][:, None] - key_codes[code_axis][None, :], -half_bins, half_bins - 1) + half_bins
        scores = scores + table_low[code_axis][:, offset_index]
    scores = low_back(scores)
    scores = jnp.where(key_live[None, None, :] > 0, scores, NEGATIVE)
    row_top = lax.optimization_barrier(jnp.max(scores, axis=-1, keepdims=True))
    weights = jnp.exp(scores - row_top)
    soft_weights = weights / lax.optimization_barrier(jnp.sum(weights, axis=-1, keepdims=True))
    context = jnp.einsum('hij,jhd->ihd', low(soft_weights), value_heads, precision=HIGHEST)
    return context.reshape(length, model_width)

def finish(rows_in, context, out_weight, out_bias, gain_second, shift_second, in_weight, in_bias, back_weight, back_bias):
    context = low(low_back(context))
    middle = rows_in + low_back(jnp.dot(context, out_weight, precision=HIGHEST) + out_bias)
    normed = low(norm_rows(middle, gain_second, shift_second))
    pre_active = low_back(jnp.dot(normed, in_weight, precision=HIGHEST) + in_bias)
    active = low(exact_gelu(pre_active))
    return middle + low_back(jnp.dot(active, back_weight, precision=HIGHEST) + back_bias)

def reference(tokens, cotangent, box_bins, segment_ids, key_mask, ln1_gain, ln1_bias, w_qkv, bias_q, bias_v, w_out, bias_out, ln2_gain, ln2_bias, w_in, bias_in, w_back, bias_back, rel_table):
    params = tuple((array.astype(jnp.float32) for array in (ln1_gain, ln1_bias, w_qkv, bias_q, bias_v, w_out, bias_out, ln2_gain, ln2_bias, w_in, bias_in, w_back, bias_back, rel_table)))
    token_pages = jnp.transpose(tokens.astype(jnp.float32).reshape(2, PAGES, PAGE, D), (1, 0, 2, 3))
    cot_pages = jnp.transpose(cotangent.astype(jnp.float32).reshape(2, PAGES, PAGE, D), (1, 0, 2, 3))
    all_codes = jnp.concatenate([box_bins, segment_ids[:, None]], axis=1)
    code_pages = jnp.transpose(all_codes, (2, 0, 1, 3))
    live_pages = jnp.transpose(key_mask, (1, 0, 2))

    def page_step(running, page_slab):
        page_tokens, page_cot, page_codes, page_live = page_slab

        def forward(rows_pair, weights):
            gain_first, shift_first, pack_weight, query_bias, value_bias, out_weight, out_bias, gain_second, shift_second, in_weight, in_bias, back_weight, back_bias, table_all = weights
            projected = [branch_inputs(rows_pair[stream], gain_first[stream], shift_first[stream], pack_weight[stream], query_bias[stream], value_bias[stream]) for stream in range(2)]
            results = []
            for stream in range(2):
                partner = 1 - stream
                table_low = low(table_all[stream]).reshape(3, HEADS, BINS)
                context = attend(projected[stream][0], projected[partner][1], projected[partner][2], table_low, page_codes[stream], page_codes[partner], page_live[partner])
                results.append(finish(rows_pair[stream], context, out_weight[stream], out_bias[stream], gain_second[stream], shift_second[stream], in_weight[stream], in_bias[stream], back_weight[stream], back_bias[stream]))
            return jnp.stack(results)
        result, pullback = jax.vjp(forward, page_tokens, params)
        d_rows, d_params = pullback(page_cot)
        running = jax.tree.map(lambda summed, addend: summed + addend, running, d_params)
        return (running, (result, d_rows))
    zeros = tuple((jnp.zeros_like(array) for array in params))
    grads, (result_pages, grad_pages) = lax.scan(page_step, zeros, (token_pages, cot_pages, code_pages, live_pages))
    output = jnp.transpose(result_pages, (1, 0, 2, 3)).reshape(2, TOKENS, D).astype(jnp.bfloat16)
    g_tokens = jnp.transpose(grad_pages, (1, 0, 2, 3)).reshape(2, TOKENS, D).astype(jnp.bfloat16)
    return (output, g_tokens, grads[0], grads[1], grads[2], grads[3], grads[4], grads[5], grads[6], grads[7], grads[8], grads[9], grads[10], grads[11], grads[12], grads[13])
```

```python
import jax
import jax.numpy as jnp
from jax import lax
from jax.sharding import PartitionSpec as P

HEADS = 12
BINS = 128
PAGE = 512


EPSILON = 1e-05
NEGATIVE = -1000000000.0
HIGHEST = lax.Precision.HIGHEST


def partner_2(shard, axis, distance):
    return lax.ppermute(shard, axis, [(i, i ^ 1 << distance) for i in range(lax.axis_size(axis))])


def norm_rows(values, gain_row, shift_row):
    center = values - jnp.mean(values, axis=-1, keepdims=True)
    spread = jnp.mean(center * center, axis=-1, keepdims=True)
    return center * lax.rsqrt(spread + EPSILON) * gain_row + shift_row


def exact_gelu(values):
    return jax.nn.gelu(values, approximate=False)


def cross_rows(left_side, right_side):
    return lax.dot_general(
        left_side, right_side, (((0,), (0,)), ((), ())), preferred_element_type=jnp.float32
    )


def times_back(left_side, right_side):
    return lax.dot_general(
        left_side, right_side, (((1,), (1,)), ((), ())), preferred_element_type=jnp.float32
    )


def one_hot_codes(code_values):
    levels = lax.broadcasted_iota(jnp.int32, code_values.shape + (BINS,), len(code_values.shape))
    return (code_values[..., None] == levels).astype(jnp.bfloat16)


def offset_select():
    half_bins = BINS // 2
    first_code = lax.broadcasted_iota(jnp.int32, (BINS, BINS, BINS), 0)
    second_code = lax.broadcasted_iota(jnp.int32, (BINS, BINS, BINS), 1)
    entry_index = lax.broadcasted_iota(jnp.int32, (BINS, BINS, BINS), 2)
    offset_index = jnp.clip(first_code - second_code, -half_bins, half_bins - 1) + half_bins
    return offset_index == entry_index


def query_side(query_hot, tiles):
    pieces = [
        jnp.einsum(
            "jo,pos->pjs",
            query_hot[code_axis],
            tiles[code_axis],
            preferred_element_type=jnp.float32,
        )
        for code_axis in range(3)
    ]
    return jnp.concatenate(pieces, axis=2).astype(jnp.bfloat16)


def page_scores(queries, key_rows, query_hot, key_side, key_live, tiles):
    length, model_width = queries.shape
    query_heads = queries.reshape(length, HEADS, model_width // HEADS)
    key_heads = key_rows.reshape(length, HEADS, model_width // HEADS)
    plain = jnp.einsum("ihd,jhd->hij", query_heads, key_heads, preferred_element_type=jnp.float32)
    extra = jnp.einsum(
        "hic,jc->hij", query_side(query_hot, tiles), key_side, preferred_element_type=jnp.float32
    )
    scores = plain * (model_width // HEADS) ** (-0.5) + extra
    return jnp.where(key_live[None, None, :] > 0, scores, NEGATIVE)


def regroup(grad_rows, data_count, group_count):
    leading = grad_rows.shape[0]
    shaped = grad_rows.reshape(
        (data_count, group_count, leading // (data_count * group_count)) + grad_rows.shape[1:]
    )
    return jnp.swapaxes(shaped, 0, 1).reshape(grad_rows.shape)


RING = 8
RING_ORDER = (0, 2, 4, 6, 7, 5, 3, 1)


def plain_totals(grads, data_count, group_count):
    totals = []
    for grad_rows in grads:
        ordered = regroup(grad_rows, data_count, group_count)
        share = lax.psum_scatter(ordered, ("group", "dp"), scatter_dimension=0, tiled=True)
        whole = lax.all_gather(share.astype(jnp.bfloat16), "group", axis=0, tiled=True)
        totals.append(whole.astype(jnp.float32))
    return tuple(totals)


def ring_send(chunk):
    pairs = []
    for place in range(RING):
        ahead = RING_ORDER[(place + 1) % RING]
        behind = RING_ORDER[(place - 1) % RING]
        pairs.append((RING_ORDER[place] * 2, ahead * 2))
        pairs.append((RING_ORDER[place] * 2 + 1, behind * 2 + 1))
    return lax.ppermute(chunk, ("group", "dp"), pairs)


def ring_place():
    group = lax.axis_index("group")
    place = jnp.int32(0)
    for position, member in enumerate(RING_ORDER):
        place = jnp.where(group == member, position, place)
    return jnp.where(lax.axis_index("dp") == 0, place, (RING - place) % RING)


def ring_sum(halves):
    dp = lax.axis_index("dp")
    place = ring_place()
    own = lax.dynamic_index_in_dim(halves, dp, 0, keepdims=False)
    other = lax.dynamic_index_in_dim(halves, 1 - dp, 0, keepdims=False)
    met = lax.ppermute(other, "dp", [(0, 1), (1, 0)])

    def part(step):
        index = (place + step + 2 * RING) % RING
        return lax.dynamic_index_in_dim(own, index, 0, keepdims=False).astype(
            jnp.float32
        ) + lax.dynamic_index_in_dim(met, index, 0, keepdims=False).astype(jnp.float32)

    held = part(0).astype(jnp.bfloat16)
    for step in range(1, RING):
        came = ring_send(held)
        held = (came.astype(jnp.float32) + part(-step)).astype(jnp.bfloat16)
    chunks = [held]
    for step in range(1, RING):
        held = ring_send(held)
        chunks.append(held)
    return chunks, [(place + 1 - step + RING) % RING for step in range(RING)]


def split_columns(grad_rows, width):
    rows, columns = grad_rows.shape
    shaped = grad_rows.astype(jnp.bfloat16).reshape(2, RING, rows // (2 * RING), columns // width, width)
    return jnp.swapaxes(shaped, 2, 3).reshape(2, RING, -1, width)


def join_columns(pieces, indices, columns):
    width = pieces[0].shape[-1]
    blocks = columns // width
    rows = pieces[0].shape[0] // blocks
    whole = jnp.zeros((RING * rows, columns), jnp.float32)
    for piece, index in zip(pieces, indices):
        flat = jnp.swapaxes(piece.reshape(blocks, rows, width), 0, 1).reshape(rows, columns)
        whole = lax.dynamic_update_slice(whole, flat.astype(jnp.float32), (index * rows, 0))
    return whole


def ring_totals(grads):
    width = grads[2].shape[0]
    wide = lambda index: split_columns(grads[index], width)
    feed = jnp.concatenate([wide(11), wide(9)], axis=2)
    small_indices = [index for index in range(14) if grads[index].ndim == 1]
    small = jnp.concatenate([grads[index].reshape(2, -1) for index in small_indices], axis=1)
    spare = -small.shape[1] % (RING * 16 * width)
    small = jnp.pad(small, ((0, 0), (0, spare))).astype(jnp.bfloat16).reshape(2, RING, -1, width)
    rest = jnp.concatenate([wide(2), wide(5), small], axis=2)
    feed_chunks, feed_indices = ring_sum(feed)
    rest_chunks, rest_indices = ring_sum(rest)
    totals = [None] * 14
    half = feed_chunks[0].shape[0] // 2
    totals[11] = join_columns([c[:half] for c in feed_chunks], feed_indices, grads[11].shape[1])
    totals[9] = join_columns([c[half:] for c in feed_chunks], feed_indices, grads[9].shape[1])
    first = wide(2).shape[2]
    second = first + wide(5).shape[2]
    totals[2] = join_columns([c[:first] for c in rest_chunks], rest_indices, grads[2].shape[1])
    totals[5] = join_columns([c[first:second] for c in rest_chunks], rest_indices, grads[5].shape[1])
    small_total = join_columns([c[second:] for c in rest_chunks], rest_indices, width).reshape(-1)
    start = 0
    for index in small_indices:
        length = grads[index].shape[0] // 2
        totals[index] = small_total[start : start + length]
        start += length
    return tuple(totals)


def on_device(
    tokens,
    cotangent,
    box_bins,
    segment_ids,
    key_mask,
    ln1_gain,
    ln1_bias,
    w_qkv,
    bias_q,
    bias_v,
    w_out,
    bias_out,
    ln2_gain,
    ln2_bias,
    w_in,
    bias_in,
    w_back,
    bias_back,
    rel_table,
):
    stream = lax.axis_index("stream")
    partner = 1 - stream
    inputs = tokens[0].astype(jnp.float32)
    row_count, model_width = inputs.shape
    page_count = row_count // PAGE
    head_size = model_width // HEADS
    score_scale = head_size ** (-0.5)
    all_codes = jnp.concatenate([box_bins, segment_ids[:, None]], axis=1)
    own_codes = jnp.transpose(
        lax.dynamic_index_in_dim(all_codes, stream, 0, keepdims=False), (1, 0, 2)
    )
    far_codes = jnp.transpose(
        lax.dynamic_index_in_dim(all_codes, partner, 0, keepdims=False), (1, 0, 2)
    )
    query_hot = one_hot_codes(own_codes)
    far_hot = one_hot_codes(far_codes)
    key_side = jnp.concatenate([far_hot[:, 0], far_hot[:, 1], far_hot[:, 2]], axis=2)
    key_live = lax.dynamic_index_in_dim(key_mask, partner, 0, keepdims=False)
    select_mask = offset_select()
    table_low = rel_table[0].astype(jnp.bfloat16).reshape(3 * HEADS, BINS)
    tiles = jnp.einsum(
        "cr,abr->cab",
        table_low,
        select_mask.astype(jnp.bfloat16),
        preferred_element_type=jnp.float32,
    )
    tiles = tiles.astype(jnp.bfloat16).reshape(3, HEADS, BINS, BINS)
    normed_first = norm_rows(inputs, ln1_gain[0], ln1_bias[0]).astype(jnp.bfloat16)
    packed = jnp.dot(normed_first, w_qkv[0], preferred_element_type=jnp.float32)
    queries = (packed[:, :model_width] + bias_q[0]).astype(jnp.bfloat16)
    key_rows = packed[:, model_width : 2 * model_width].astype(jnp.bfloat16)
    value_rows = (packed[:, 2 * model_width :] + bias_v[0]).astype(jnp.bfloat16)
    arrived = partner_2(jnp.stack([key_rows, value_rows]), "stream", 0)
    far_keys = arrived[0].reshape(page_count, PAGE, model_width)
    far_values = arrived[1].reshape(page_count, PAGE, model_width)
    query_pages = queries.reshape(page_count, PAGE, model_width)

    def attend_page(page_slab):
        page_queries, page_keys, page_values, page_hot, page_side, page_live = page_slab
        scores = page_scores(page_queries, page_keys, page_hot, page_side, page_live, tiles)
        row_top = jnp.max(scores, axis=-1, keepdims=True)
        weights = jnp.exp(scores - row_top)
        total_sum = jnp.sum(weights, axis=-1, keepdims=True)
        soft_weights = (weights / total_sum).astype(jnp.bfloat16)
        value_heads = page_values.reshape(PAGE, HEADS, head_size)
        context = jnp.einsum(
            "hij,jhd->ihd", soft_weights, value_heads, preferred_element_type=jnp.float32
        )
        return (
            context.reshape(PAGE, model_width).astype(jnp.bfloat16),
            (row_top + jnp.log(total_sum))[..., 0],
        )

    context_pages, log_total = lax.map(
        attend_page, (query_pages, far_keys, far_values, query_hot, key_side, key_live)
    )
    context = context_pages.reshape(row_count, model_width)
    middle = inputs + jnp.dot(context, w_out[0], preferred_element_type=jnp.float32) + bias_out[0]
    normed_second = norm_rows(middle, ln2_gain[0], ln2_bias[0]).astype(jnp.bfloat16)
    pre_active = jnp.dot(normed_second, w_in[0], preferred_element_type=jnp.float32) + bias_in[0]
    active = exact_gelu(pre_active).astype(jnp.bfloat16)
    output = (
        middle + jnp.dot(active, w_back[0], preferred_element_type=jnp.float32) + bias_back[0]
    ).astype(jnp.bfloat16)
    upstream = cotangent[0]
    upstream_wide = upstream.astype(jnp.float32)
    g_bias_back = jnp.sum(upstream_wide, axis=0)
    g_w_back = cross_rows(active, upstream)
    d_active = times_back(upstream, w_back[0])
    _, gelu_pull = jax.vjp(exact_gelu, pre_active)
    d_pre = gelu_pull(d_active)[0].astype(jnp.bfloat16)
    g_bias_in = jnp.sum(d_pre.astype(jnp.float32), axis=0)
    g_w_in = cross_rows(normed_second, d_pre)
    d_normed_second = times_back(d_pre, w_in[0])
    _, second_pull = jax.vjp(norm_rows, middle, ln2_gain[0], ln2_bias[0])
    d_second_part, g_ln2_gain, g_ln2_bias = second_pull(d_normed_second)
    d_middle = upstream_wide + d_second_part
    d_branch = d_middle.astype(jnp.bfloat16)
    g_bias_out = jnp.sum(d_branch.astype(jnp.float32), axis=0)
    g_w_out = cross_rows(context, d_branch)
    d_context = times_back(d_branch, w_out[0]).astype(jnp.bfloat16)

    def page_back(page_slab):
        (
            page_queries,
            page_keys,
            page_values,
            page_hot,
            page_side,
            page_live,
            page_total,
            page_grad,
        ) = page_slab
        scores = page_scores(page_queries, page_keys, page_hot, page_side, page_live, tiles)
        soft_weights = jnp.exp(scores - page_total[..., None])
        query_heads = page_queries.reshape(PAGE, HEADS, head_size)
        key_heads = page_keys.reshape(PAGE, HEADS, head_size)
        value_heads = page_values.reshape(PAGE, HEADS, head_size)
        grad_heads = page_grad.reshape(PAGE, HEADS, head_size)
        d_weights = jnp.einsum(
            "ihd,jhd->hij", grad_heads, value_heads, preferred_element_type=jnp.float32
        )
        centre = jnp.sum(soft_weights * d_weights, axis=-1, keepdims=True)
        d_scores = (soft_weights * (d_weights - centre)).astype(jnp.bfloat16)
        d_queries = (
            jnp.einsum("hij,jhd->ihd", d_scores, key_heads, preferred_element_type=jnp.float32)
            * score_scale
        )
        d_keys = (
            jnp.einsum("hij,ihd->jhd", d_scores, query_heads, preferred_element_type=jnp.float32)
            * score_scale
        )
        d_values = jnp.einsum(
            "hij,ihd->jhd",
            soft_weights.astype(jnp.bfloat16),
            grad_heads,
            preferred_element_type=jnp.float32,
        )
        spread_rows = jnp.einsum(
            "hij,jc->hic", d_scores, page_side, preferred_element_type=jnp.float32
        )
        hot_wide = page_hot.astype(jnp.float32)
        tile_grads = jnp.stack(
            [
                jnp.einsum(
                    "mx,umt->uxt",
                    hot_wide[code_axis],
                    spread_rows[:, :, code_axis * BINS : (code_axis + 1) * BINS],
                    precision=HIGHEST,
                )
                for code_axis in range(3)
            ]
        )
        return (
            d_queries.reshape(PAGE, model_width).astype(jnp.bfloat16),
            d_keys.reshape(PAGE, model_width).astype(jnp.bfloat16),
            d_values.reshape(PAGE, model_width).astype(jnp.bfloat16),
            tile_grads,
        )

    d_query_pages, d_far_keys, d_far_values, tile_pages = lax.map(
        page_back,
        (
            query_pages,
            far_keys,
            far_values,
            query_hot,
            key_side,
            key_live,
            log_total,
            d_context.reshape(page_count, PAGE, model_width),
        ),
    )
    returned = partner_2(
        jnp.stack(
            [
                d_far_keys.reshape(row_count, model_width),
                d_far_values.reshape(row_count, model_width),
            ]
        ),
        "stream",
        0,
    )
    d_queries = d_query_pages.reshape(row_count, model_width)
    d_packed = jnp.concatenate([d_queries, returned[0], returned[1]], axis=1)
    g_w_qkv = cross_rows(normed_first, d_packed)
    g_bias_q = jnp.sum(d_queries.astype(jnp.float32), axis=0)
    g_bias_v = jnp.sum(returned[1].astype(jnp.float32), axis=0)
    d_normed_first = times_back(d_packed, w_qkv[0])
    _, first_pull = jax.vjp(norm_rows, inputs, ln1_gain[0], ln1_bias[0])
    d_first_part, g_ln1_gain, g_ln1_bias = first_pull(d_normed_first)
    g_tokens = (d_middle + d_first_part).astype(jnp.bfloat16)
    tile_sum = jnp.sum(tile_pages, axis=0).reshape(3 * HEADS, BINS, BINS)
    g_rel_table = jnp.einsum(
        "cab,abr->cr", tile_sum, select_mask.astype(jnp.float32), precision=HIGHEST
    ).reshape(-1)
    grads = (
        g_ln1_gain,
        g_ln1_bias,
        g_w_qkv,
        g_bias_q,
        g_bias_v,
        g_w_out,
        g_bias_out,
        g_ln2_gain,
        g_ln2_bias,
        g_w_in,
        g_bias_in,
        g_w_back,
        g_bias_back,
        g_rel_table,
    )
    group_count = lax.axis_size("group")
    data_count = lax.axis_size("dp")
    if group_count == RING and data_count == 2:
        totals = ring_totals(grads)
    else:
        totals = plain_totals(grads, data_count, group_count)
    finals = tuple((summed[None] for summed in totals))
    return (output[None], g_tokens[None]) + finals


def solution(mesh):
    placed = (
        P("stream", ("group", "dp"), None),
        P("stream", ("group", "dp"), None),
        P(None, None, ("group", "dp"), None),
        P(None, ("group", "dp"), None),
        P(None, ("group", "dp"), None),
        P("stream", None),
        P("stream", None),
        P("stream", None, None),
        P("stream", None),
        P("stream", None),
        P("stream", None, None),
        P("stream", None),
        P("stream", None),
        P("stream", None),
        P("stream", None, None),
        P("stream", None),
        P("stream", None, None),
        P("stream", None),
        P("stream", None),
    )
    return jax.shard_map(
        on_device,
        mesh=mesh,
        in_specs=placed,
        out_specs=(
            P("stream", ("group", "dp"), None),
            P("stream", ("group", "dp"), None),
            P("stream", "dp"),
            P("stream", "dp"),
            P("stream", "dp", None),
            P("stream", "dp"),
            P("stream", "dp"),
            P("stream", "dp", None),
            P("stream", "dp"),
            P("stream", "dp"),
            P("stream", "dp"),
            P("stream", "dp", None),
            P("stream", "dp"),
            P("stream", "dp", None),
            P("stream", "dp"),
            P("stream", "dp"),
        ),
        check_vma=False,
    )
```

```python
import functools
import jax
import jax.numpy as jnp
from jax import lax
from jax.experimental import pallas as pl
from jax.experimental.pallas import tpu as pltpu
from jax.sharding import PartitionSpec as P

EPSILON = 1e-05
STRIP = 64
HEADS = 12
BINS = 128
GROUPS = 3
NEGATIVE = -1000000000.0
HIGHEST = lax.Precision.HIGHEST
RING = 8
RING_ORDER = (0, 2, 4, 6, 7, 5, 3, 1)
ROOT_HALF = 0.7071067811865476
DENSITY = 0.3989422804014327


def dot_plain(a, b):
    return lax.dot_general(a, b, (((1,), (0,)), ((), ())), preferred_element_type=jnp.float32)


def dot_across(a, b):
    return lax.dot_general(a, b, (((0,), (0,)), ((), ())), preferred_element_type=jnp.float32)


def dot_back(a, b):
    return lax.dot_general(a, b, (((1,), (1,)), ((), ())), preferred_element_type=jnp.float32)


def row_stats(rows):
    center = rows - jnp.mean(rows, axis=-1, keepdims=True)
    spread = jnp.mean(center * center, axis=-1, keepdims=True)
    rate = lax.rsqrt(spread + EPSILON)
    return center * rate, rate


def fold(rows):
    return jnp.sum(rows.reshape(rows.shape[0] // 8, 8, rows.shape[1]), axis=0)


def strips(count, body):
    for index in range(count // STRIP):
        body(pl.ds(index * STRIP, STRIP))


def place_chunk(target, mine_ref, other_ref, value, rows=slice(None)):
    @pl.when(target < 8)
    def _():
        mine_ref[target, rows, :] = value

    @pl.when(target >= 8)
    def _():
        other_ref[target - 8, rows, :] = value


def put_halves(small_ref, row, vector):
    half = vector.shape[1] // 2
    width = small_ref.shape[2]
    for side in range(2):
        for piece in range(half // width):
            start = side * half + piece * width
            small_ref[side, row + piece : row + piece + 1, :] = vector[:, start : start + width]


def feed_kernel(
    order_ref,
    tokens_ref,
    context_0_ref,
    context_1_ref,
    context_2_ref,
    cot_ref,
    w_out_ref,
    b_out_ref,
    gain_ref,
    shift_ref,
    w_in_ref,
    b_in_ref,
    w_back_ref,
    b_back_ref,
    out_ref,
    d_middle_ref,
    d_branch_ref,
    d_context_ref,
    back_mine_ref,
    back_other_ref,
    in_mine_ref,
    in_other_ref,
    small_ref,
    middle_ref,
    normed_ref,
    turned_ref,
    pre_ref,
    d_act_ref,
    act_ref,
    d_pre_ref,
    total_ref,
    d_normed_ref,
    sums_ref,
    in_sum_ref,
):
    step = pl.program_id(0)
    last = pl.num_programs(0) - 1
    rows = tokens_ref.shape[0]
    block = w_in_ref.shape[1]

    @pl.when(step == 0)
    def _():
        part = context_0_ref.shape[1]
        middle_ref[...] = (
            dot_plain(context_0_ref[...], w_out_ref[:part])
            + dot_plain(context_1_ref[...], w_out_ref[part : 2 * part])
            + dot_plain(context_2_ref[...], w_out_ref[2 * part :])
        )
        sums_ref[...] = jnp.zeros_like(sums_ref)
        small_ref[...] = jnp.zeros_like(small_ref)
        total_ref[...] = jnp.zeros_like(total_ref)
        d_normed_ref[...] = jnp.zeros_like(d_normed_ref)

        def first(at):
            value = middle_ref[at, :] + tokens_ref[at, :].astype(jnp.float32) + b_out_ref[...]
            middle_ref[at, :] = value
            hat, _ = row_stats(value)
            normed_ref[at, :] = (hat * gain_ref[...] + shift_ref[...]).astype(jnp.bfloat16)
            sums_ref[0] += fold(cot_ref[at, :].astype(jnp.float32))

        strips(rows, first)
        turned_ref[...] = normed_ref[...].T

    pre_ref[...] = dot_plain(normed_ref[...], w_in_ref[...])
    d_act_ref[...] = dot_back(cot_ref[...], w_back_ref[...])
    in_sum_ref[...] = jnp.zeros_like(in_sum_ref)

    def middle_part(at):
        value = pre_ref[at, :] + b_in_ref[...]
        chance = 0.5 + 0.5 * lax.erf(value * ROOT_HALF)
        slope = chance + value * (DENSITY * jnp.exp(-0.5 * value * value))
        act_ref[at, :] = (value * chance).astype(jnp.bfloat16)
        d_pre = (d_act_ref[at, :] * slope).astype(jnp.bfloat16)
        d_pre_ref[at, :] = d_pre
        in_sum_ref[...] += fold(d_pre.astype(jnp.float32))

    strips(rows, middle_part)
    total_ref[...] += dot_plain(act_ref[...], w_back_ref[...])
    d_normed_ref[...] += dot_back(d_pre_ref[...], w_in_ref[...])
    per_block = block // 192
    back = dot_across(act_ref[...], cot_ref[...]).astype(jnp.bfloat16)
    for piece in range(per_block):
        place_chunk(
            order_ref[step * per_block + piece],
            back_mine_ref,
            back_other_ref,
            back[piece * 192 : piece * 192 + 192],
        )
    inward = dot_plain(turned_ref[...], d_pre_ref[...]).astype(jnp.bfloat16)
    at_rows = pl.ds(pl.multiple_of(step * 48, 16), 48)
    for piece in range(16):
        place_chunk(
            order_ref[piece], in_mine_ref, in_other_ref, inward[piece * 48 : piece * 48 + 48], at_rows
        )
    in_sum = jnp.sum(in_sum_ref[...], axis=0, keepdims=True)
    side = step // 2
    row = 8 + 2 * (step % 2)
    small_ref[side, pl.ds(row, 1), :] = in_sum[:, :384]
    small_ref[side, pl.ds(row + 1, 1), :] = in_sum[:, 384:]

    @pl.when(step == last)
    def _():
        def final(at):
            value = middle_ref[at, :]
            out_ref[at, :] = (value + total_ref[at, :] + b_back_ref[...]).astype(jnp.bfloat16)
            hat, rate = row_stats(value)
            d_normed = d_normed_ref[at, :]
            sums_ref[1] += fold(d_normed * hat)
            sums_ref[2] += fold(d_normed)
            scaled = d_normed * gain_ref[...]
            inner = (
                scaled
                - jnp.mean(scaled, axis=-1, keepdims=True)
                - hat * jnp.mean(scaled * hat, axis=-1, keepdims=True)
            )
            d_middle = cot_ref[at, :].astype(jnp.float32) + rate * inner
            d_middle_ref[at, :] = d_middle
            branch = d_middle.astype(jnp.bfloat16)
            d_branch_ref[at, :] = branch
            sums_ref[3] += fold(branch.astype(jnp.float32))

        strips(rows, final)
        d_context_ref[...] = dot_back(d_branch_ref[...], w_out_ref[...]).astype(jnp.bfloat16)
        for index, row in ((0, 7), (1, 5), (2, 6), (3, 4)):
            put_halves(small_ref, row, jnp.sum(sums_ref[index], axis=0, keepdims=True))


def feed_call(order, tokens, contexts, cot, w_out, b_out, gain, shift, w_in, b_in, w_back, b_back):
    rows, width = tokens.shape
    inner = w_in.shape[1]
    block = 768
    fixed = lambda shape: pl.BlockSpec(shape, lambda j, o: (0,) * len(shape), pipeline_mode=pl.Buffered(1))
    wide = lambda dtype: jax.ShapeDtypeStruct((rows, width), dtype)
    ring = jax.ShapeDtypeStruct((8, 192, width), jnp.bfloat16)
    f32, bf16 = jnp.float32, jnp.bfloat16
    vmem = pltpu.VMEM
    return pl.pallas_call(
        feed_kernel,
        out_shape=(wide(bf16), wide(f32), wide(bf16), wide(bf16), ring, ring, ring, ring,
                   jax.ShapeDtypeStruct((2, 24, 384), f32)),
        grid_spec=pltpu.PrefetchScalarGridSpec(
            num_scalar_prefetch=1,
            grid=(inner // block,),
            in_specs=[
                fixed((rows, width)),
                fixed((rows, width // GROUPS)), fixed((rows, width // GROUPS)), fixed((rows, width // GROUPS)),
                fixed((rows, width)),
                fixed((width, width)), fixed((1, width)), fixed((1, width)), fixed((1, width)),
                pl.BlockSpec((width, block), lambda j, o: (0, j)),
                pl.BlockSpec((1, block), lambda j, o: (0, j)),
                pl.BlockSpec((block, width), lambda j, o: (j, 0)),
                fixed((1, width)),
            ],
            out_specs=[fixed((rows, width))] * 4 + [fixed((8, 192, width))] * 4 + [fixed((2, 24, 384))],
            scratch_shapes=[
                vmem((rows, width), f32), vmem((rows, width), bf16), vmem((width, rows), bf16),
                vmem((rows, block), f32), vmem((rows, block), f32),
                vmem((rows, block), bf16), vmem((rows, block), bf16),
                vmem((rows, width), f32), vmem((rows, width), f32),
                vmem((4, 8, width), f32), vmem((8, block), f32),
            ],
        ),
        compiler_params=pltpu.CompilerParams(vmem_limit_bytes=60 << 20),
        name="feed",
    )(order, tokens, *contexts, cot, w_out, b_out, gain, shift, w_in, b_in, w_back, b_back)


def first_kernel(tokens_ref, gain_ref, shift_ref, w_ref, bias_ref, normed_ref, *sent_refs):
    rows, width = tokens_ref.shape

    def norm(at):
        hat, _ = row_stats(tokens_ref[at, :].astype(jnp.float32))
        normed_ref[at, :] = (hat * gain_ref[...] + shift_ref[...]).astype(jnp.bfloat16)

    strips(rows, norm)
    part = width // GROUPS
    for group, sent_ref in enumerate(sent_refs):
        at = group * part
        sent_ref[0] = dot_plain(normed_ref[...], w_ref[:, width + at : width + at + part]).astype(jnp.bfloat16)
        sent_ref[1] = (
            dot_plain(normed_ref[...], w_ref[:, 2 * width + at : 2 * width + at + part])
            + bias_ref[:, at : at + part]
        ).astype(jnp.bfloat16)


def whole_specs(count):
    return [pl.BlockSpec(memory_space=pltpu.VMEM)] * count


def kernel_call(kernel, name, outs, *args, scratch=(), smem=0, aliases={}):
    specs = [pl.BlockSpec(memory_space=pltpu.SMEM)] * smem + whole_specs(len(args) - smem)
    return pl.pallas_call(
        kernel,
        out_shape=tuple(outs),
        in_specs=specs,
        out_specs=tuple(whole_specs(len(outs))),
        scratch_shapes=list(scratch),
        input_output_aliases=aliases,
        compiler_params=pltpu.CompilerParams(vmem_limit_bytes=60 << 20),
        name=name,
    )(*args)


def first_call(tokens, gain, shift, w_qkv, bias_v):
    rows, width = tokens.shape
    outs = [jax.ShapeDtypeStruct((rows, width), jnp.bfloat16)]
    outs += [jax.ShapeDtypeStruct((2, rows, width // GROUPS), jnp.bfloat16)] * GROUPS
    return kernel_call(first_kernel, "first", outs, tokens, gain, shift, w_qkv, bias_v)


def code_columns(rows_of_codes, rows):
    blank = jnp.zeros((5, rows), jnp.float32)
    return jnp.concatenate([r.astype(jnp.float32) for r in rows_of_codes] + [blank], axis=0).T


def prep_kernel(
    stream_ref, box_ref, segment_ref, mask_ref, normed_ref, w_ref, bias_ref, table_ref,
    queries_ref, hot_ref, turned_hot_ref, key_hot_ref, live_ref, tiles_ref,
):
    rows = normed_ref.shape[0]
    own = stream_ref[0]
    far = 1 - own
    queries_ref[...] = (dot_plain(normed_ref[...], w_ref[:, : normed_ref.shape[1]]) + bias_ref[...]).astype(jnp.bfloat16)
    live_ref[...] = mask_ref[far]
    own_codes = code_columns([box_ref[own, 0], box_ref[own, 1], segment_ref[own]], rows)
    far_codes = code_columns([box_ref[far, 0], box_ref[far, 1], segment_ref[far]], rows)
    levels = lax.broadcasted_iota(jnp.int32, (rows, BINS), 1).astype(jnp.float32)
    for axis in range(3):
        lanes = slice(axis * BINS, axis * BINS + BINS)
        column = own_codes[:, axis : axis + 1]
        hot_ref[:, lanes] = jnp.where(column == levels, 1.0, 0.0).astype(jnp.bfloat16)
        turned_hot_ref[:, lanes] = jnp.where(BINS - 1 - column == levels, 1.0, 0.0).astype(jnp.bfloat16)
        key_hot_ref[:, lanes] = jnp.where(far_codes[:, axis : axis + 1] == levels, 1.0, 0.0).astype(jnp.bfloat16)
    half = BINS // 2
    entry = lax.broadcasted_iota(jnp.int32, (BINS, 2 * BINS), 0)
    gap = lax.broadcasted_iota(jnp.int32, (BINS, 2 * BINS), 1)
    gap = jnp.where(gap < BINS, -gap, 2 * BINS - gap)
    pick = jnp.where(jnp.clip(gap, -half, half - 1) + half == entry, 1.0, 0.0).astype(jnp.bfloat16)
    spread = dot_plain(table_ref[...].astype(jnp.bfloat16), pick)
    for index in range(3 * HEADS):
        wide = jnp.broadcast_to(spread[index : index + 1, :], (BINS, 2 * BINS))
        rolled = pltpu.roll(wide, 0, 1, stride=1, stride_axis=0)
        tiles_ref[index] = rolled[:, :BINS].astype(jnp.bfloat16)


def prep_call(stream, box_bins, segment_ids, key_mask, normed, w_qkv, bias_q, table):
    rows, width = normed.shape
    hot = jax.ShapeDtypeStruct((rows, 3 * BINS), jnp.bfloat16)
    outs = [
        jax.ShapeDtypeStruct((rows, width), jnp.bfloat16), hot, hot, hot,
        jax.ShapeDtypeStruct((1, rows), jnp.int32),
        jax.ShapeDtypeStruct((3 * HEADS, BINS, BINS), jnp.bfloat16),
    ]
    return kernel_call(prep_kernel, "prep", outs, stream, box_bins, segment_ids, key_mask, normed, w_qkv, bias_q, table, smem=1)


def half_of(slab, odd):
    lane = lax.broadcasted_iota(jnp.int32, slab.shape, 1)
    keep = (lane >= 64) if odd else (lane < 64)
    return jnp.where(keep, slab, jnp.zeros_like(slab))


def attend_kernel(group, queries_ref, pair_ref, hot_ref, key_hot_ref, live_ref, tiles_ref,
                  context_ref, probs_ref, left_ref, right_ref, scores_ref):
    rows = queries_ref.shape[0]
    part = pair_ref.shape[2]
    for slab in range(part // 128):
        lanes = slice(slab * 128, slab * 128 + 128)
        wide = slice(group * part + slab * 128, group * part + slab * 128 + 128)
        right_ref[slab, :, :128] = pair_ref[0, :, lanes]
        right_ref[slab, :, 128:] = key_hot_ref[...]
        halves = []
        for odd in range(2):
            head = slab * 2 + odd
            left_ref[head, :, :128] = half_of(queries_ref[:, wide].astype(jnp.float32) * 0.125, odd).astype(jnp.bfloat16)
            for axis in range(3):
                cut = slice(axis * BINS, axis * BINS + BINS)
                tile = tiles_ref[axis * HEADS + group * (part // 64) + head]
                left_ref[head, :, 128 + axis * BINS : 256 + axis * BINS] = dot_plain(hot_ref[:, cut], tile).astype(jnp.bfloat16)
            scores_ref[head] = dot_back(left_ref[head], right_ref[slab])

            def soft(at):
                scores = jnp.where(live_ref[...] > 0, scores_ref[head, at, :], NEGATIVE)
                top = jnp.max(scores, axis=-1, keepdims=True)
                weights = jnp.exp(scores - top)
                rate = 1.0 / jnp.sum(weights, axis=-1, keepdims=True)
                probs_ref[head, at, :] = (weights * rate).astype(jnp.bfloat16)

            strips(rows, soft)
            halves.append(half_of(dot_plain(probs_ref[head], pair_ref[1, :, lanes]), odd))
        context_ref[:, lanes] = (halves[0] + halves[1]).astype(jnp.bfloat16)


def attend_call(group, queries, pair, hot, key_hot, live, tiles):
    rows = queries.shape[0]
    part = pair.shape[2]
    heads = part // 64
    outs = [
        jax.ShapeDtypeStruct((rows, part), jnp.bfloat16),
        jax.ShapeDtypeStruct((heads, rows, rows), jnp.bfloat16),
    ]
    scratch = [
        pltpu.VMEM((heads, rows, 512), jnp.bfloat16),
        pltpu.VMEM((part // 128, rows, 512), jnp.bfloat16),
        pltpu.VMEM((heads, rows, rows), jnp.float32),
    ]
    return kernel_call(functools.partial(attend_kernel, group), f"attend_{group}", outs,
                       queries, pair, hot, key_hot, live, tiles, scratch=scratch)


def attend_back_kernel(group, queries_ref, pair_ref, turned_hot_ref, key_hot_ref, probs_ref, d_context_ref,
                       d_queries_ref, d_pair_ref, diagonal_ref, right_ref, slope_ref, d_scores_ref):
    rows = queries_ref.shape[0]
    part = pair_ref.shape[2]
    for slab in range(part // 128):
        lanes = slice(slab * 128, slab * 128 + 128)
        wide = slice(group * part + slab * 128, group * part + slab * 128 + 128)
        right_ref[slab, :, :128] = pair_ref[0, :, lanes]
        right_ref[slab, :, 128:] = key_hot_ref[...]
        d_query = d_key = d_value = 0.0
        for odd in range(2):
            head = slab * 2 + odd
            query = half_of(queries_ref[:, wide], odd)
            d_context = half_of(d_context_ref[:, wide], odd)
            slope_ref[head] = dot_back(d_context, pair_ref[1, :, lanes])

            def soft(at):
                probs = probs_ref[head, at, :].astype(jnp.float32)
                slope = slope_ref[head, at, :]
                centre = jnp.sum(probs * slope, axis=-1, keepdims=True)
                d_scores_ref[head, at, :] = (probs * (slope - centre)).astype(jnp.bfloat16)

            strips(rows, soft)
            d_value = d_value + dot_across(probs_ref[head], d_context)
            d_key = d_key + dot_across(d_scores_ref[head], query)
            both = dot_plain(d_scores_ref[head], right_ref[slab])
            d_query = d_query + half_of(both[:, :128], odd)
            spread = both[:, 128:].astype(jnp.bfloat16)
            for axis in range(3):
                cut = slice(axis * BINS, axis * BINS + BINS)
                tile = dot_across(turned_hot_ref[:, cut], spread[:, cut])
                padded = jnp.concatenate([tile, jnp.zeros_like(tile)], axis=1)
                rolled = pltpu.roll(padded, 0, 1, stride=1, stride_axis=0)
                diagonal_ref[axis, head : head + 1, :] = jnp.sum(rolled, axis=0, keepdims=True)
        d_queries_ref[:, lanes] = (d_query * 0.125).astype(jnp.bfloat16)
        d_pair_ref[0, :, lanes] = (d_key * 0.125).astype(jnp.bfloat16)
        d_pair_ref[1, :, lanes] = d_value.astype(jnp.bfloat16)


def attend_back_call(group, queries, pair, turned_hot, key_hot, probs, d_context):
    rows = queries.shape[0]
    part = pair.shape[2]
    heads = part // 64
    outs = [
        jax.ShapeDtypeStruct((rows, part), jnp.bfloat16),
        jax.ShapeDtypeStruct((2, rows, part), jnp.bfloat16),
        jax.ShapeDtypeStruct((3, heads, 2 * BINS), jnp.float32),
    ]
    scratch = [
        pltpu.VMEM((part // 128, rows, 512), jnp.bfloat16),
        pltpu.VMEM((heads, rows, rows), jnp.float32),
        pltpu.VMEM((heads, rows, rows), jnp.bfloat16),
    ]
    return kernel_call(functools.partial(attend_back_kernel, group), f"attend_back_{group}", outs,
                       queries, pair, turned_hot, key_hot, probs, d_context, scratch=scratch)


def last_kernel(
    order_ref, tokens_ref, gain_ref, shift_ref, w_ref, d_middle_ref, d_branch_ref,
    context_0_ref, context_1_ref, context_2_ref, d_query_0_ref, d_query_1_ref, d_query_2_ref,
    back_0_ref, back_1_ref, back_2_ref, diagonal_0_ref, diagonal_1_ref, diagonal_2_ref, start_ref,
    g_tokens_ref, mine_ref, other_ref, small_ref,
    normed_ref, joined_ref, d_normed_ref, sums_ref,
):
    rows, width = tokens_ref.shape
    part = width // GROUPS
    small_ref[...] = start_ref[...]
    sums_ref[...] = jnp.zeros_like(sums_ref)

    def norm(at):
        hat, _ = row_stats(tokens_ref[at, :].astype(jnp.float32))
        normed_ref[at, :] = (hat * gain_ref[...] + shift_ref[...]).astype(jnp.bfloat16)

    strips(rows, norm)
    queries = (d_query_0_ref, d_query_1_ref, d_query_2_ref)
    backs = (back_0_ref, back_1_ref, back_2_ref)
    contexts = (context_0_ref, context_1_ref, context_2_ref)
    for group in range(GROUPS):
        lanes = slice(group * part, group * part + part)
        joined_ref[0, :, lanes] = queries[group][...]
        joined_ref[1, :, lanes] = backs[group][0]
        joined_ref[2, :, lanes] = backs[group][1]
        joined_ref[3, :, lanes] = contexts[group][...]
    for block in range(4):
        if block < 3:
            value = dot_across(normed_ref[...], joined_ref[block]).astype(jnp.bfloat16)
        else:
            value = dot_across(joined_ref[3], d_branch_ref[...]).astype(jnp.bfloat16)
        for piece in range(16):
            place_chunk(
                order_ref[piece], mine_ref, other_ref, value[piece * 48 : piece * 48 + 48],
                slice(block * 48, block * 48 + 48),
            )
    d_normed_ref[...] = (
        dot_back(joined_ref[0], w_ref[:, :width])
        + dot_back(joined_ref[1], w_ref[:, width : 2 * width])
        + dot_back(joined_ref[2], w_ref[:, 2 * width :])
    )

    def final(at):
        hat, rate = row_stats(tokens_ref[at, :].astype(jnp.float32))
        d_normed = d_normed_ref[at, :]
        sums_ref[0] += fold(d_normed * hat)
        sums_ref[1] += fold(d_normed)
        sums_ref[2] += fold(joined_ref[0, at, :].astype(jnp.float32))
        sums_ref[3] += fold(joined_ref[2, at, :].astype(jnp.float32))
        scaled = d_normed * gain_ref[...]
        inner = (
            scaled
            - jnp.mean(scaled, axis=-1, keepdims=True)
            - hat * jnp.mean(scaled * hat, axis=-1, keepdims=True)
        )
        g_tokens_ref[at, :] = (d_middle_ref[at, :] + rate * inner).astype(jnp.bfloat16)

    strips(rows, final)
    for row in range(4):
        put_halves(small_ref, row, jnp.sum(sums_ref[row], axis=0, keepdims=True))
    half = BINS // 2
    gap = BINS - 1 - lax.broadcasted_iota(jnp.int32, (2 * BINS, BINS), 0)
    entry = lax.broadcasted_iota(jnp.int32, (2 * BINS, BINS), 1)
    pick = jnp.where(jnp.clip(gap, -half, half - 1) + half == entry, 1.0, 0.0)
    for group, diagonal_ref in enumerate((diagonal_0_ref, diagonal_1_ref, diagonal_2_ref)):
        for axis in range(3):
            table = lax.dot_general(
                diagonal_ref[axis], pick, (((1,), (0,)), ((), ())),
                precision=HIGHEST, preferred_element_type=jnp.float32,
            )
            for head in range(part // 64):
                index = axis * HEADS + group * (part // 64) + head
                side, place = divmod(index, 18)
                row, lane = divmod(place, 3)
                small_ref[side, 12 + row : 13 + row, lane * BINS : lane * BINS + BINS] = table[head : head + 1, :]


def last_call(order, tokens, gain, shift, w_qkv, d_middle, d_branch, contexts, d_queries, backs, diagonals, start):
    rows, width = tokens.shape
    ring = jax.ShapeDtypeStruct((RING, 192, width), jnp.bfloat16)
    outs = [jax.ShapeDtypeStruct((rows, width), jnp.bfloat16), ring, ring, jax.ShapeDtypeStruct(start.shape, jnp.float32)]
    scratch = [
        pltpu.VMEM((rows, width), jnp.bfloat16),
        pltpu.VMEM((4, rows, width), jnp.bfloat16),
        pltpu.VMEM((rows, width), jnp.float32),
        pltpu.VMEM((4, 8, width), jnp.float32),
    ]
    return kernel_call(last_kernel, "last", outs, order, tokens, gain, shift, w_qkv, d_middle, d_branch,
                       *contexts, *d_queries, *backs, *diagonals, start, scratch=scratch, smem=1)


def open_back_kernel(place_ref, *refs):
    for index in range(RING):
        at = pl.ds(pl.multiple_of(place_ref[index] * 192, 192), 192)
        refs[RING][at, :] = refs[index][...].astype(jnp.float32)


def open_in_kernel(place_ref, *refs):
    width = refs[0].shape[1]
    for index in range(RING):
        at = pl.ds(pl.multiple_of(place_ref[index] * 48, 48), 48)
        for block in range(4):
            refs[RING][at, block * width : block * width + width] = refs[index][block * 48 : block * 48 + 48, :].astype(jnp.float32)


def open_rest_kernel(place_ref, *refs):
    width = refs[0].shape[1]
    for index in range(RING):
        at = pl.ds(pl.multiple_of(place_ref[index] * 48, 48), 48)
        for block in range(3):
            refs[RING][at, block * width : block * width + width] = refs[index][block * 48 : block * 48 + 48, :].astype(jnp.float32)
        refs[RING + 1][at, :] = refs[index][144:192, :].astype(jnp.float32)


def open_small_kernel(side_ref, small_ref, *outs):
    side = side_ref[0]
    for row in range(8):
        outs[row][...] = small_ref[side, row : row + 1, :]
    for row in range(4):
        outs[8][:, row * 384 : row * 384 + 384] = small_ref[side, 8 + row : 9 + row, :]
    for row in range(6):
        outs[9][:, row * 384 : row * 384 + 384] = small_ref[side, 12 + row : 13 + row, :]


def open_call(kernel, name, places, chunks, shapes):
    outs = [jax.ShapeDtypeStruct(shape, jnp.float32) for shape in shapes]
    return kernel_call(kernel, name, outs, places, *chunks, smem=1)


def partner_2(shard, axis, distance):
    return lax.ppermute(shard, axis, [(i, i ^ 1 << distance) for i in range(lax.axis_size(axis))])


def ring_send(chunk):
    pairs = []
    for place in range(RING):
        ahead = RING_ORDER[(place + 1) % RING]
        behind = RING_ORDER[(place - 1) % RING]
        pairs.append((RING_ORDER[place] * 2, ahead * 2))
        pairs.append((RING_ORDER[place] * 2 + 1, behind * 2 + 1))
    return lax.ppermute(chunk, ("group", "dp"), pairs)


def ring_place():
    group = lax.axis_index("group")
    place = jnp.int32(0)
    for position, member in enumerate(RING_ORDER):
        place = jnp.where(group == member, position, place)
    return place


def ring_plan(ringed):
    index = lax.iota(jnp.int32, 2 * RING)
    steps = lax.iota(jnp.int32, RING)
    if not ringed:
        return index, steps
    dp = lax.axis_index("dp")
    place = ring_place()
    side = index // RING
    start = jnp.where(side == 0, place, RING - place)
    order = (start - index % RING + RING) % RING + jnp.where(side == dp, 0, RING)
    start = jnp.where(dp == 0, place, RING - place)
    return order, (start + 1 - steps + RING) % RING


def add_low(*terms):
    return sum(term.astype(jnp.float32) for term in terms).astype(jnp.bfloat16)


def unringed_total(mine, other):
    return lax.psum(jnp.concatenate([mine, other]).astype(jnp.float32), ("group", "dp"))


def unringed_rows(packed):
    blocks = packed.shape[1] // 48
    rows = packed.reshape(2 * RING, blocks, 48, packed.shape[2])
    return jnp.swapaxes(rows, 1, 2).reshape(2 * RING * 48, blocks * packed.shape[2])


def own_share(whole):
    share = whole.shape[0] // lax.axis_size("dp")
    return lax.dynamic_slice_in_dim(whole, lax.axis_index("dp") * share, share, 0)[None]


def unringed_grads(back, inward, rest, small):
    back = unringed_total(*back)
    inward = unringed_total(*inward)
    rest = unringed_total(*rest)
    small = lax.psum(small, ("group", "dp"))
    vectors = [small[:, row].reshape(-1) for row in range(8)]
    vectors += [small[:, 8:12].reshape(-1), small[:, 12:18].reshape(-1)]
    weights = (
        back.reshape(-1, back.shape[2]),
        unringed_rows(inward),
        unringed_rows(rest[:, :144]),
        unringed_rows(rest[:, 144:]),
    )
    return [own_share(weight) for weight in weights], [own_share(vector) for vector in vectors]


def ring_totals(mine, other):
    met = lax.ppermute(other, "dp", [(0, 1), (1, 0)])
    held = add_low(mine[0], met[0])
    for step in range(1, RING):
        held = add_low(ring_send(held), mine[step], met[step])
    chunks = [held]
    for step in range(1, RING):
        chunks.append(ring_send(chunks[-1]))
    return chunks


def small_totals(small):
    small = small + lax.ppermute(small, "dp", [(0, 1), (1, 0)])
    for distance in range(3):
        small = small + partner_2(small, "group", distance)
    return small


def on_device(
    tokens, cotangent, box_bins, segment_ids, key_mask, ln1_gain, ln1_bias, w_qkv, bias_q, bias_v,
    w_out, bias_out, ln2_gain, ln2_bias, w_in, bias_in, w_back, bias_back, rel_table,
):
    ringed = lax.axis_size("group") == RING and lax.axis_size("dp") == 2
    width = tokens.shape[2]
    order, places = ring_plan(ringed)
    stream = lax.axis_index("stream").reshape(1)
    normed, *sent = first_call(tokens[0], ln1_gain, ln1_bias, w_qkv[0], bias_v)
    pairs = [partner_2(pair, "stream", 0) for pair in sent]
    queries, hot, turned_hot, key_hot, live, tiles = prep_call(
        stream, box_bins, segment_ids, key_mask, normed, w_qkv[0], bias_q, rel_table.reshape(3 * HEADS, BINS)
    )
    contexts, probs = [], []
    for group in range(GROUPS):
        context, prob = attend_call(group, queries, pairs[group], hot, key_hot, live, tiles)
        contexts.append(context)
        probs.append(prob)
    output, d_middle, d_branch, d_context, back_mine, back_other, in_mine, in_other, small = feed_call(
        order, tokens[0], contexts, cotangent[0], w_out[0], bias_out, ln2_gain, ln2_bias,
        w_in[0], bias_in, w_back[0], bias_back,
    )
    if ringed:
        back_chunks = ring_totals(back_mine, back_other)
        in_chunks = ring_totals(in_mine, in_other)
    d_queries, backs, diagonals = [], [], []
    for group in range(GROUPS):
        d_query, d_pair, diagonal = attend_back_call(
            group, queries, pairs[group], turned_hot, key_hot, probs[group], d_context
        )
        d_queries.append(d_query)
        backs.append(partner_2(d_pair, "stream", 0))
        diagonals.append(diagonal)
    g_tokens, rest_mine, rest_other, small = last_call(
        order, tokens[0], ln1_gain, ln1_bias, w_qkv[0], d_middle, d_branch, contexts, d_queries, backs, diagonals, small
    )
    if ringed:
        rest_chunks = ring_totals(rest_mine, rest_other)
        small = small_totals(small)
        half = width // 2
        (g_w_back,) = open_call(open_back_kernel, "open_back", places, back_chunks, [(2 * width, width)])
        (g_w_in,) = open_call(open_in_kernel, "open_in", places, in_chunks, [(half, 4 * width)])
        g_w_qkv, g_w_out = open_call(
            open_rest_kernel, "open_rest", places, rest_chunks, [(half, 3 * width), (half, width)]
        )
        weights = [value[None] for value in (g_w_back, g_w_in, g_w_qkv, g_w_out)]
        side = lax.axis_index("dp").reshape(1)
        vectors = open_call(
            open_small_kernel, "open_small", side, [small], [(1, half)] * 8 + [(1, 2 * width), (1, 3 * width)]
        )
    else:
        weights, vectors = unringed_grads(
            (back_mine, back_other), (in_mine, in_other), (rest_mine, rest_other), small
        )
    g_w_back, g_w_in, g_w_qkv, g_w_out = weights
    (
        g_ln1_gain, g_ln1_bias, g_bias_q, g_bias_v, g_bias_out, g_ln2_gain, g_ln2_bias, g_bias_back, g_bias_in, g_rel_table,
    ) = vectors
    return (
        output[None], g_tokens[None], g_ln1_gain, g_ln1_bias, g_w_qkv, g_bias_q, g_bias_v, g_w_out,
        g_bias_out, g_ln2_gain, g_ln2_bias, g_w_in, g_bias_in, g_w_back, g_bias_back, g_rel_table,
    )


def solution(mesh):
    placed = (
        P("stream", ("group", "dp"), None),
        P("stream", ("group", "dp"), None),
        P(None, None, ("group", "dp"), None),
        P(None, ("group", "dp"), None),
        P(None, ("group", "dp"), None),
        P("stream", None),
        P("stream", None),
        P("stream", None, None),
        P("stream", None),
        P("stream", None),
        P("stream", None, None),
        P("stream", None),
        P("stream", None),
        P("stream", None),
        P("stream", None, None),
        P("stream", None),
        P("stream", None, None),
        P("stream", None),
        P("stream", None),
    )
    return jax.shard_map(
        on_device,
        mesh=mesh,
        in_specs=placed,
        out_specs=(
            P("stream", ("group", "dp"), None),
            P("stream", ("group", "dp"), None),
            P("stream", "dp"),
            P("stream", "dp"),
            P("stream", "dp", None),
            P("stream", "dp"),
            P("stream", "dp"),
            P("stream", "dp", None),
            P("stream", "dp"),
            P("stream", "dp"),
            P("stream", "dp"),
            P("stream", "dp", None),
            P("stream", "dp"),
            P("stream", "dp", None),
            P("stream", "dp"),
            P("stream", "dp"),
        ),
        check_vma=False,
    )
```

```python
import functools
import jax
import jax.numpy as jnp
from jax import lax
from jax.experimental import pallas as pl
from jax.experimental.pallas import tpu as pltpu
from jax.sharding import PartitionSpec as P

EPSILON = 1e-05
STRIP = 64
HEADS = 12
BINS = 128
GROUPS = 3
NEGATIVE = -1000000000.0
HIGHEST = lax.Precision.HIGHEST
RING = 8
RING_ORDER = (0, 2, 4, 6, 7, 5, 3, 1)
ROOT_HALF = 0.7071067811865476
DENSITY = 0.3989422804014327


def dot_plain(a, b):
    return lax.dot_general(a, b, (((1,), (0,)), ((), ())), preferred_element_type=jnp.float32)


def dot_across(a, b):
    return lax.dot_general(a, b, (((0,), (0,)), ((), ())), preferred_element_type=jnp.float32)


def dot_back(a, b):
    return lax.dot_general(a, b, (((1,), (1,)), ((), ())), preferred_element_type=jnp.float32)


def row_stats(rows):
    center = rows - jnp.mean(rows, axis=-1, keepdims=True)
    spread = jnp.mean(center * center, axis=-1, keepdims=True)
    rate = lax.rsqrt(spread + EPSILON)
    return center * rate, rate


def fold(rows):
    return jnp.sum(rows.reshape(rows.shape[0] // 8, 8, rows.shape[1]), axis=0)


def strips(count, body):
    for index in range(count // STRIP):
        body(pl.ds(index * STRIP, STRIP))


def place_chunk(target, mine_ref, other_ref, value, rows=slice(None)):
    @pl.when(target < 8)
    def _():
        mine_ref[target, rows, :] = value

    @pl.when(target >= 8)
    def _():
        other_ref[target - 8, rows, :] = value


def put_halves(small_ref, row, vector):
    half = vector.shape[1] // 2
    width = small_ref.shape[2]
    for side in range(2):
        for piece in range(half // width):
            start = side * half + piece * width
            small_ref[side, row + piece : row + piece + 1, :] = vector[:, start : start + width]


def feed_kernel(
    order_ref,
    tokens_ref,
    context_0_ref,
    context_1_ref,
    context_2_ref,
    cot_ref,
    w_out_ref,
    b_out_ref,
    gain_ref,
    shift_ref,
    w_in_ref,
    b_in_ref,
    w_back_ref,
    b_back_ref,
    out_ref,
    d_middle_ref,
    d_branch_ref,
    d_context_ref,
    mine_ref,
    other_ref,
    small_ref,
    middle_ref,
    normed_ref,
    turned_ref,
    pre_ref,
    d_act_ref,
    act_ref,
    d_pre_ref,
    total_ref,
    d_normed_ref,
    sums_ref,
    in_sum_ref,
):
    step = pl.program_id(0)
    last = pl.num_programs(0) - 1
    rows = tokens_ref.shape[0]
    block = w_in_ref.shape[1]

    @pl.when(step == 0)
    def _():
        part = context_0_ref.shape[1]
        middle_ref[...] = (
            dot_plain(context_0_ref[...], w_out_ref[:part])
            + dot_plain(context_1_ref[...], w_out_ref[part : 2 * part])
            + dot_plain(context_2_ref[...], w_out_ref[2 * part :])
        )
        sums_ref[...] = jnp.zeros_like(sums_ref)
        small_ref[...] = jnp.zeros_like(small_ref)
        total_ref[...] = jnp.zeros_like(total_ref)
        d_normed_ref[...] = jnp.zeros_like(d_normed_ref)

        def first(at):
            value = middle_ref[at, :] + tokens_ref[at, :].astype(jnp.float32) + b_out_ref[...]
            middle_ref[at, :] = value
            hat, _ = row_stats(value)
            normed_ref[at, :] = (hat * gain_ref[...] + shift_ref[...]).astype(jnp.bfloat16)
            sums_ref[0] += fold(cot_ref[at, :].astype(jnp.float32))

        strips(rows, first)
        turned_ref[...] = normed_ref[...].T

    pre_ref[...] = dot_plain(normed_ref[...], w_in_ref[...])
    d_act_ref[...] = dot_back(cot_ref[...], w_back_ref[...])
    in_sum_ref[...] = jnp.zeros_like(in_sum_ref)

    def middle_part(at):
        value = pre_ref[at, :] + b_in_ref[...]
        chance = 0.5 + 0.5 * lax.erf(value * ROOT_HALF)
        slope = chance + value * (DENSITY * jnp.exp(-0.5 * value * value))
        act_ref[at, :] = (value * chance).astype(jnp.bfloat16)
        d_pre = (d_act_ref[at, :] * slope).astype(jnp.bfloat16)
        d_pre_ref[at, :] = d_pre
        in_sum_ref[...] += fold(d_pre.astype(jnp.float32))

    strips(rows, middle_part)
    total_ref[...] += dot_plain(act_ref[...], w_back_ref[...])
    d_normed_ref[...] += dot_back(d_pre_ref[...], w_in_ref[...])
    per_block = block // 192
    back = dot_across(act_ref[...], cot_ref[...]).astype(jnp.bfloat16)
    for piece in range(per_block):
        place_chunk(
            order_ref[step * per_block + piece],
            mine_ref,
            other_ref,
            back[piece * 192 : piece * 192 + 192],
            slice(0, 192),
        )
    inward = dot_plain(turned_ref[...], d_pre_ref[...]).astype(jnp.bfloat16)
    at_rows = pl.ds(pl.multiple_of(192 + step * 48, 16), 48)
    for piece in range(16):
        place_chunk(
            order_ref[piece], mine_ref, other_ref, inward[piece * 48 : piece * 48 + 48], at_rows
        )
    in_sum = jnp.sum(in_sum_ref[...], axis=0, keepdims=True)
    side = step // 2
    row = 8 + 2 * (step % 2)
    small_ref[side, pl.ds(row, 1), :] = in_sum[:, :384]
    small_ref[side, pl.ds(row + 1, 1), :] = in_sum[:, 384:]

    @pl.when(step == last)
    def _():
        def final(at):
            value = middle_ref[at, :]
            out_ref[at, :] = (value + total_ref[at, :] + b_back_ref[...]).astype(jnp.bfloat16)
            hat, rate = row_stats(value)
            d_normed = d_normed_ref[at, :]
            sums_ref[1] += fold(d_normed * hat)
            sums_ref[2] += fold(d_normed)
            scaled = d_normed * gain_ref[...]
            inner = (
                scaled
                - jnp.mean(scaled, axis=-1, keepdims=True)
                - hat * jnp.mean(scaled * hat, axis=-1, keepdims=True)
            )
            d_middle = cot_ref[at, :].astype(jnp.float32) + rate * inner
            d_middle_ref[at, :] = d_middle
            branch = d_middle.astype(jnp.bfloat16)
            d_branch_ref[at, :] = branch
            sums_ref[3] += fold(branch.astype(jnp.float32))

        strips(rows, final)
        d_context_ref[...] = dot_back(d_branch_ref[...], w_out_ref[...]).astype(jnp.bfloat16)
        for index, row in ((0, 7), (1, 5), (2, 6), (3, 4)):
            put_halves(small_ref, row, jnp.sum(sums_ref[index], axis=0, keepdims=True))


def feed_call(order, tokens, contexts, cot, w_out, b_out, gain, shift, w_in, b_in, w_back, b_back):
    rows, width = tokens.shape
    inner = w_in.shape[1]
    block = 768
    fixed = lambda shape: pl.BlockSpec(shape, lambda j, o: (0,) * len(shape), pipeline_mode=pl.Buffered(1))
    wide = lambda dtype: jax.ShapeDtypeStruct((rows, width), dtype)
    ring = jax.ShapeDtypeStruct((RING, 384, width), jnp.bfloat16)
    f32, bf16 = jnp.float32, jnp.bfloat16
    vmem = pltpu.VMEM
    return pl.pallas_call(
        feed_kernel,
        out_shape=(wide(bf16), wide(f32), wide(bf16), wide(bf16), ring, ring,
                   jax.ShapeDtypeStruct((2, 24, 384), f32)),
        grid_spec=pltpu.PrefetchScalarGridSpec(
            num_scalar_prefetch=1,
            grid=(inner // block,),
            in_specs=[
                fixed((rows, width)),
                fixed((rows, width // GROUPS)), fixed((rows, width // GROUPS)), fixed((rows, width // GROUPS)),
                fixed((rows, width)),
                fixed((width, width)), fixed((1, width)), fixed((1, width)), fixed((1, width)),
                pl.BlockSpec((width, block), lambda j, o: (0, j)),
                pl.BlockSpec((1, block), lambda j, o: (0, j)),
                pl.BlockSpec((block, width), lambda j, o: (j, 0)),
                fixed((1, width)),
            ],
            out_specs=[fixed((rows, width))] * 4 + [fixed((RING, 384, width))] * 2 + [fixed((2, 24, 384))],
            scratch_shapes=[
                vmem((rows, width), f32), vmem((rows, width), bf16), vmem((width, rows), bf16),
                vmem((rows, block), f32), vmem((rows, block), f32),
                vmem((rows, block), bf16), vmem((rows, block), bf16),
                vmem((rows, width), f32), vmem((rows, width), f32),
                vmem((4, 8, width), f32), vmem((8, block), f32),
            ],
        ),
        compiler_params=pltpu.CompilerParams(vmem_limit_bytes=60 << 20),
        cost_estimate=price(30),
        name="feed",
    )(order, tokens, *contexts, cot, w_out, b_out, gain, shift, w_in, b_in, w_back, b_back)


def first_kernel(tokens_ref, gain_ref, shift_ref, w_ref, bias_ref, normed_ref, *sent_refs):
    rows, width = tokens_ref.shape

    def norm(at):
        hat, _ = row_stats(tokens_ref[at, :].astype(jnp.float32))
        normed_ref[at, :] = (hat * gain_ref[...] + shift_ref[...]).astype(jnp.bfloat16)

    strips(rows, norm)
    part = width // GROUPS
    for group, sent_ref in enumerate(sent_refs):
        at = group * part
        sent_ref[0] = dot_plain(normed_ref[...], w_ref[:, width + at : width + at + part]).astype(jnp.bfloat16)
        sent_ref[1] = (
            dot_plain(normed_ref[...], w_ref[:, 2 * width + at : 2 * width + at + part])
            + bias_ref[:, at : at + part]
        ).astype(jnp.bfloat16)


def whole_specs(count):
    return [pl.BlockSpec(memory_space=pltpu.VMEM)] * count


def price(micros):
    return pl.CostEstimate(flops=int(micros * 1e9), transcendentals=0, bytes_accessed=0)


def kernel_call(kernel, name, micros, outs, *args, scratch=(), smem=0, aliases={}):
    specs = [pl.BlockSpec(memory_space=pltpu.SMEM)] * smem + whole_specs(len(args) - smem)
    return pl.pallas_call(
        kernel,
        out_shape=tuple(outs),
        in_specs=specs,
        out_specs=tuple(whole_specs(len(outs))),
        scratch_shapes=list(scratch),
        input_output_aliases=aliases,
        cost_estimate=price(micros),
        compiler_params=pltpu.CompilerParams(vmem_limit_bytes=60 << 20),
        name=name,
    )(*args)


def first_call(tokens, gain, shift, w_qkv, bias_v):
    rows, width = tokens.shape
    outs = [jax.ShapeDtypeStruct((rows, width), jnp.bfloat16)]
    outs += [jax.ShapeDtypeStruct((2, rows, width // GROUPS), jnp.bfloat16)] * GROUPS
    return kernel_call(first_kernel, "first", 5, outs, tokens, gain, shift, w_qkv, bias_v)


def code_columns(rows_of_codes, rows):
    blank = jnp.zeros((5, rows), jnp.float32)
    return jnp.concatenate([r.astype(jnp.float32) for r in rows_of_codes] + [blank], axis=0).T


def prep_kernel(
    stream_ref, box_ref, segment_ref, mask_ref, normed_ref, w_ref, bias_ref, table_ref,
    queries_ref, hot_ref, turned_hot_ref, key_hot_ref, live_ref, tiles_ref,
):
    rows = normed_ref.shape[0]
    own = stream_ref[0]
    far = 1 - own
    queries_ref[...] = (dot_plain(normed_ref[...], w_ref[:, : normed_ref.shape[1]]) + bias_ref[...]).astype(jnp.bfloat16)
    live_ref[...] = mask_ref[far]
    own_codes = code_columns([box_ref[own, 0], box_ref[own, 1], segment_ref[own]], rows)
    far_codes = code_columns([box_ref[far, 0], box_ref[far, 1], segment_ref[far]], rows)
    levels = lax.broadcasted_iota(jnp.int32, (rows, BINS), 1).astype(jnp.float32)
    for axis in range(3):
        lanes = slice(axis * BINS, axis * BINS + BINS)
        column = own_codes[:, axis : axis + 1]
        hot_ref[:, lanes] = jnp.where(column == levels, 1.0, 0.0).astype(jnp.bfloat16)
        turned_hot_ref[:, lanes] = jnp.where(BINS - 1 - column == levels, 1.0, 0.0).astype(jnp.bfloat16)
        key_hot_ref[:, lanes] = jnp.where(far_codes[:, axis : axis + 1] == levels, 1.0, 0.0).astype(jnp.bfloat16)
    half = BINS // 2
    entry = lax.broadcasted_iota(jnp.int32, (BINS, 2 * BINS), 0)
    gap = lax.broadcasted_iota(jnp.int32, (BINS, 2 * BINS), 1)
    gap = jnp.where(gap < BINS, -gap, 2 * BINS - gap)
    pick = jnp.where(jnp.clip(gap, -half, half - 1) + half == entry, 1.0, 0.0).astype(jnp.bfloat16)
    spread = dot_plain(table_ref[...].astype(jnp.bfloat16), pick)
    for index in range(3 * HEADS):
        wide = jnp.broadcast_to(spread[index : index + 1, :], (BINS, 2 * BINS))
        rolled = pltpu.roll(wide, 0, 1, stride=1, stride_axis=0)
        tiles_ref[index] = rolled[:, :BINS].astype(jnp.bfloat16)


def prep_call(stream, box_bins, segment_ids, key_mask, normed, w_qkv, bias_q, table):
    rows, width = normed.shape
    hot = jax.ShapeDtypeStruct((rows, 3 * BINS), jnp.bfloat16)
    outs = [
        jax.ShapeDtypeStruct((rows, width), jnp.bfloat16), hot, hot, hot,
        jax.ShapeDtypeStruct((1, rows), jnp.int32),
        jax.ShapeDtypeStruct((3 * HEADS, BINS, BINS), jnp.bfloat16),
    ]
    return kernel_call(prep_kernel, "prep", 5, outs, stream, box_bins, segment_ids, key_mask, normed, w_qkv, bias_q, table, smem=1)


def half_of(slab, odd):
    lane = lax.broadcasted_iota(jnp.int32, slab.shape, 1)
    keep = (lane >= 64) if odd else (lane < 64)
    return jnp.where(keep, slab, jnp.zeros_like(slab))


def attend_kernel(group, queries_ref, pair_ref, hot_ref, key_hot_ref, live_ref, tiles_ref,
                  context_ref, probs_ref, left_ref, right_ref, scores_ref):
    rows = queries_ref.shape[0]
    part = pair_ref.shape[2]
    for slab in range(part // 128):
        lanes = slice(slab * 128, slab * 128 + 128)
        wide = slice(group * part + slab * 128, group * part + slab * 128 + 128)
        right_ref[slab, :, :128] = pair_ref[0, :, lanes]
        right_ref[slab, :, 128:] = key_hot_ref[...]
        halves = []
        for odd in range(2):
            head = slab * 2 + odd
            left_ref[head, :, :128] = half_of(queries_ref[:, wide].astype(jnp.float32) * 0.125, odd).astype(jnp.bfloat16)
            for axis in range(3):
                cut = slice(axis * BINS, axis * BINS + BINS)
                tile = tiles_ref[axis * HEADS + group * (part // 64) + head]
                left_ref[head, :, 128 + axis * BINS : 256 + axis * BINS] = dot_plain(hot_ref[:, cut], tile).astype(jnp.bfloat16)
            scores_ref[head] = dot_back(left_ref[head], right_ref[slab])

            def soft(at):
                scores = jnp.where(live_ref[...] > 0, scores_ref[head, at, :], NEGATIVE)
                top = jnp.max(scores, axis=-1, keepdims=True)
                weights = jnp.exp(scores - top)
                rate = 1.0 / jnp.sum(weights, axis=-1, keepdims=True)
                probs_ref[head, at, :] = (weights * rate).astype(jnp.bfloat16)

            strips(rows, soft)
            halves.append(half_of(dot_plain(probs_ref[head], pair_ref[1, :, lanes]), odd))
        context_ref[:, lanes] = (halves[0] + halves[1]).astype(jnp.bfloat16)


def attend_call(group, queries, pair, hot, key_hot, live, tiles):
    rows = queries.shape[0]
    part = pair.shape[2]
    heads = part // 64
    outs = [
        jax.ShapeDtypeStruct((rows, part), jnp.bfloat16),
        jax.ShapeDtypeStruct((heads, rows, rows), jnp.bfloat16),
    ]
    scratch = [
        pltpu.VMEM((heads, rows, 512), jnp.bfloat16),
        pltpu.VMEM((part // 128, rows, 512), jnp.bfloat16),
        pltpu.VMEM((heads, rows, rows), jnp.float32),
    ]
    return kernel_call(functools.partial(attend_kernel, group), f"attend_{group}", 7, outs,
                       queries, pair, hot, key_hot, live, tiles, scratch=scratch)


def attend_back_kernel(group, queries_ref, pair_ref, turned_hot_ref, key_hot_ref, probs_ref, d_context_ref,
                       d_queries_ref, d_pair_ref, diagonal_ref, right_ref, slope_ref, d_scores_ref):
    rows = queries_ref.shape[0]
    part = pair_ref.shape[2]
    for slab in range(part // 128):
        lanes = slice(slab * 128, slab * 128 + 128)
        wide = slice(group * part + slab * 128, group * part + slab * 128 + 128)
        right_ref[slab, :, :128] = pair_ref[0, :, lanes]
        right_ref[slab, :, 128:] = key_hot_ref[...]
        d_query = d_key = d_value = 0.0
        for odd in range(2):
            head = slab * 2 + odd
            query = half_of(queries_ref[:, wide], odd)
            d_context = half_of(d_context_ref[:, wide], odd)
            slope_ref[head] = dot_back(d_context, pair_ref[1, :, lanes])

            def soft(at):
                probs = probs_ref[head, at, :].astype(jnp.float32)
                slope = slope_ref[head, at, :]
                centre = jnp.sum(probs * slope, axis=-1, keepdims=True)
                d_scores_ref[head, at, :] = (probs * (slope - centre)).astype(jnp.bfloat16)

            strips(rows, soft)
            d_value = d_value + dot_across(probs_ref[head], d_context)
            d_key = d_key + dot_across(d_scores_ref[head], query)
            both = dot_plain(d_scores_ref[head], right_ref[slab])
            d_query = d_query + half_of(both[:, :128], odd)
            spread = both[:, 128:].astype(jnp.bfloat16)
            for axis in range(3):
                cut = slice(axis * BINS, axis * BINS + BINS)
                tile = dot_across(turned_hot_ref[:, cut], spread[:, cut])
                padded = jnp.concatenate([tile, jnp.zeros_like(tile)], axis=1)
                rolled = pltpu.roll(padded, 0, 1, stride=1, stride_axis=0)
                diagonal_ref[axis, head : head + 1, :] = jnp.sum(rolled, axis=0, keepdims=True)
        d_queries_ref[:, lanes] = (d_query * 0.125).astype(jnp.bfloat16)
        d_pair_ref[0, :, lanes] = (d_key * 0.125).astype(jnp.bfloat16)
        d_pair_ref[1, :, lanes] = d_value.astype(jnp.bfloat16)


def attend_back_call(group, queries, pair, turned_hot, key_hot, probs, d_context):
    rows = queries.shape[0]
    part = pair.shape[2]
    heads = part // 64
    outs = [
        jax.ShapeDtypeStruct((rows, part), jnp.bfloat16),
        jax.ShapeDtypeStruct((2, rows, part), jnp.bfloat16),
        jax.ShapeDtypeStruct((3, heads, 2 * BINS), jnp.float32),
    ]
    scratch = [
        pltpu.VMEM((part // 128, rows, 512), jnp.bfloat16),
        pltpu.VMEM((heads, rows, rows), jnp.float32),
        pltpu.VMEM((heads, rows, rows), jnp.bfloat16),
    ]
    return kernel_call(functools.partial(attend_back_kernel, group), f"attend_back_{group}", 8, outs,
                       queries, pair, turned_hot, key_hot, probs, d_context, scratch=scratch)


def weights_kernel(
    order_ref, normed_ref, d_branch_ref, context_0_ref, context_1_ref, context_2_ref,
    d_query_0_ref, d_query_1_ref, d_query_2_ref, back_0_ref, back_1_ref, back_2_ref,
    mine_ref, other_ref, joined_ref,
):
    part = context_0_ref.shape[1]
    queries = (d_query_0_ref, d_query_1_ref, d_query_2_ref)
    backs = (back_0_ref, back_1_ref, back_2_ref)
    contexts = (context_0_ref, context_1_ref, context_2_ref)
    for group in range(GROUPS):
        lanes = slice(group * part, group * part + part)
        joined_ref[0, :, lanes] = queries[group][...]
        joined_ref[1, :, lanes] = backs[group][0]
        joined_ref[2, :, lanes] = backs[group][1]
        joined_ref[3, :, lanes] = contexts[group][...]
    for block in range(4):
        if block < 3:
            value = dot_across(normed_ref[...], joined_ref[block]).astype(jnp.bfloat16)
        else:
            value = dot_across(joined_ref[3], d_branch_ref[...]).astype(jnp.bfloat16)
        for piece in range(16):
            place_chunk(
                order_ref[piece], mine_ref, other_ref, value[piece * 48 : piece * 48 + 48],
                slice(block * 48, block * 48 + 48),
            )


def weights_call(order, normed, d_branch, contexts, d_queries, backs):
    rows, width = normed.shape
    ring = jax.ShapeDtypeStruct((RING, 192, width), jnp.bfloat16)
    scratch = [pltpu.VMEM((4, rows, width), jnp.bfloat16)]
    return kernel_call(weights_kernel, "weights", 7, [ring, ring], order, normed, d_branch,
                       *contexts, *d_queries, *backs, scratch=scratch, smem=1)


def last_kernel(
    tokens_ref, gain_ref, w_ref, d_middle_ref, d_query_0_ref, d_query_1_ref, d_query_2_ref,
    back_0_ref, back_1_ref, back_2_ref, diagonal_0_ref, diagonal_1_ref, diagonal_2_ref, start_ref,
    g_tokens_ref, small_ref, d_normed_ref, sums_ref,
):
    rows, width = tokens_ref.shape
    part = width // GROUPS
    queries = (d_query_0_ref, d_query_1_ref, d_query_2_ref)
    backs = (back_0_ref, back_1_ref, back_2_ref)
    small_ref[...] = start_ref[...]
    sums_ref[...] = jnp.zeros_like(sums_ref)
    total = 0.0
    for group in range(GROUPS):
        at = group * part
        total = total + dot_back(queries[group][...], w_ref[:, at : at + part])
        total = total + dot_back(backs[group][0], w_ref[:, width + at : width + at + part])
        total = total + dot_back(backs[group][1], w_ref[:, 2 * width + at : 2 * width + at + part])
    d_normed_ref[...] = total

    def final(at):
        hat, rate = row_stats(tokens_ref[at, :].astype(jnp.float32))
        d_normed = d_normed_ref[at, :]
        sums_ref[0] += fold(d_normed * hat)
        sums_ref[1] += fold(d_normed)
        for group in range(GROUPS):
            lanes = slice(group * part, group * part + part)
            sums_ref[2, :, lanes] += fold(queries[group][at, :].astype(jnp.float32))
            sums_ref[3, :, lanes] += fold(backs[group][1, at, :].astype(jnp.float32))
        scaled = d_normed * gain_ref[...]
        inner = (
            scaled
            - jnp.mean(scaled, axis=-1, keepdims=True)
            - hat * jnp.mean(scaled * hat, axis=-1, keepdims=True)
        )
        g_tokens_ref[at, :] = (d_middle_ref[at, :] + rate * inner).astype(jnp.bfloat16)

    strips(rows, final)
    for row in range(4):
        put_halves(small_ref, row, jnp.sum(sums_ref[row], axis=0, keepdims=True))
    half = BINS // 2
    gap = BINS - 1 - lax.broadcasted_iota(jnp.int32, (2 * BINS, BINS), 0)
    entry = lax.broadcasted_iota(jnp.int32, (2 * BINS, BINS), 1)
    pick = jnp.where(jnp.clip(gap, -half, half - 1) + half == entry, 1.0, 0.0)
    for group, diagonal_ref in enumerate((diagonal_0_ref, diagonal_1_ref, diagonal_2_ref)):
        for axis in range(3):
            table = lax.dot_general(
                diagonal_ref[axis], pick, (((1,), (0,)), ((), ())),
                precision=HIGHEST, preferred_element_type=jnp.float32,
            )
            for head in range(part // 64):
                index = axis * HEADS + group * (part // 64) + head
                side, place = divmod(index, 18)
                row, lane = divmod(place, 3)
                small_ref[side, 12 + row : 13 + row, lane * BINS : lane * BINS + BINS] = table[head : head + 1, :]


def last_call(tokens, gain, w_qkv, d_middle, d_queries, backs, diagonals, start):
    rows, width = tokens.shape
    outs = [jax.ShapeDtypeStruct((rows, width), jnp.bfloat16), jax.ShapeDtypeStruct(start.shape, jnp.float32)]
    scratch = [pltpu.VMEM((rows, width), jnp.float32), pltpu.VMEM((4, 8, width), jnp.float32)]
    return kernel_call(last_kernel, "last", 8, outs, tokens, gain, w_qkv, d_middle,
                       *d_queries, *backs, *diagonals, start, scratch=scratch)


def open_kernel(layout, place_ref, *refs):
    width = refs[0].shape[1]
    for out_ref, (start, blocks) in zip(refs[RING:], layout):
        size = out_ref.shape[0] // RING
        for index in range(RING):
            to = pl.ds(pl.multiple_of(place_ref[index] * size, size), size)
            for block in range(blocks):
                at = start + block * size
                out_ref[to, block * width : block * width + width] = refs[index][at : at + size, :].astype(jnp.float32)


OPEN_LAYOUTS = {"back": ((0, 1),), "inward": ((0, 4),), "rest": ((0, 3), (144, 1))}


def open_call(name, places, chunks):
    layout = OPEN_LAYOUTS[name]
    width = chunks[0].shape[1]
    outs = [
        jax.ShapeDtypeStruct((RING * (192 if name == "back" else 48), blocks * width), jnp.float32)
        for _, blocks in layout
    ]
    return kernel_call(functools.partial(open_kernel, layout), f"open_{name}", 4, outs, places, *chunks, smem=1)


def open_small_kernel(side_ref, small_ref, *outs):
    side = side_ref[0]
    for row in range(8):
        outs[row][...] = small_ref[side, row : row + 1, :]
    for row in range(4):
        outs[8][:, row * 384 : row * 384 + 384] = small_ref[side, 8 + row : 9 + row, :]
    for row in range(6):
        outs[9][:, row * 384 : row * 384 + 384] = small_ref[side, 12 + row : 13 + row, :]


def partner_2(shard, axis, distance):
    return lax.ppermute(shard, axis, [(i, i ^ 1 << distance) for i in range(lax.axis_size(axis))])


def ring_send(chunk):
    pairs = []
    for place in range(RING):
        ahead = RING_ORDER[(place + 1) % RING]
        behind = RING_ORDER[(place - 1) % RING]
        pairs.append((RING_ORDER[place] * 2, ahead * 2))
        pairs.append((RING_ORDER[place] * 2 + 1, behind * 2 + 1))
    return lax.ppermute(chunk, ("group", "dp"), pairs)


def ring_place():
    group = lax.axis_index("group")
    place = jnp.int32(0)
    for position, member in enumerate(RING_ORDER):
        place = jnp.where(group == member, position, place)
    return place


def ring_plan(ringed):
    index = lax.iota(jnp.int32, 2 * RING)
    steps = lax.iota(jnp.int32, RING)
    if not ringed:
        return index, steps
    dp = lax.axis_index("dp")
    place = ring_place()
    side = index // RING
    start = jnp.where(side == 0, place, RING - place)
    order = (start - index % RING + RING) % RING + jnp.where(side == dp, 0, RING)
    start = jnp.where(dp == 0, place, RING - place)
    return order, (start + 1 - steps + RING) % RING


def add_low(*terms):
    return sum(term.astype(jnp.float32) for term in terms).astype(jnp.bfloat16)


def unringed_total(mine, other):
    return lax.psum(jnp.concatenate([mine, other]).astype(jnp.float32), ("group", "dp"))


def unringed_rows(packed):
    blocks = packed.shape[1] // 48
    rows = packed.reshape(2 * RING, blocks, 48, packed.shape[2])
    return jnp.swapaxes(rows, 1, 2).reshape(2 * RING * 48, blocks * packed.shape[2])


def own_share(whole):
    share = whole.shape[0] // lax.axis_size("dp")
    return lax.dynamic_slice_in_dim(whole, lax.axis_index("dp") * share, share, 0)[None]


def unringed_grads(feed, rest, small):
    feed = unringed_total(*feed)
    rest = unringed_total(*rest)
    small = lax.psum(small, ("group", "dp"))
    vectors = [small[:, row].reshape(-1) for row in range(8)]
    vectors += [small[:, 8:12].reshape(-1), small[:, 12:18].reshape(-1)]
    weights = (
        feed[:, :192].reshape(-1, feed.shape[2]),
        unringed_rows(feed[:, 192:]),
        unringed_rows(rest[:, :144]),
        unringed_rows(rest[:, 144:]),
    )
    return [own_share(weight) for weight in weights], [own_share(vector) for vector in vectors]


class Ordered:
    def __init__(self):
        self.mark = None
        self.free = False

    def after(self, value):
        if self.mark is None or self.free:
            return value
        return lax.optimization_barrier((value, self.mark))[0]

    def wait(self, *values):
        self.mark = (self.mark, *values)


class Ring:
    def __init__(self, order, mine, other):
        self.order, self.mine = order, mine
        self.met = lax.ppermute(order.after(other), "dp", [(0, 1), (1, 0)])
        self.arrived, self.step = None, 0

    def reduce(self):
        step, order = self.step, self.order
        if step == 0:
            held = add_low(self.mine[0], order.after(self.met)[0])
        else:
            held = add_low(order.after(self.arrived), self.mine[step], self.met[step])
        order.mark = held
        if step < RING - 1:
            self.arrived = ring_send(held)
        self.step += 1
        return held


def gather(held, waits={}):
    chunks = [held]
    for step in range(1, RING):
        held = ring_send(held)
        if step in waits:
            held = waits[step](held)
        chunks.append(held)
    return chunks


SMALL_EARLY = (4, 6)
SMALL_PAIRS = (("dp", 0), ("group", 0), ("group", 1), ("group", 2))


class Small:
    def __init__(self, order, small):
        self.order, self.small, self.step = order, small, 0
        self.send()

    def send(self):
        self.arrived = partner_2(self.small, *SMALL_PAIRS[self.step])

    def advance(self):
        self.small = self.small + self.order.after(self.arrived)
        self.order.mark = self.small
        self.step += 1
        if self.step < len(SMALL_PAIRS):
            self.send()


def on_device(
    tokens, cotangent, box_bins, segment_ids, key_mask, ln1_gain, ln1_bias, w_qkv, bias_q, bias_v,
    w_out, bias_out, ln2_gain, ln2_bias, w_in, bias_in, w_back, bias_back, rel_table,
):
    ringed = lax.axis_size("group") == RING and lax.axis_size("dp") == 2
    width = tokens.shape[2]
    order, places = ring_plan(ringed)
    queue = Ordered()
    stream = lax.axis_index("stream").reshape(1)
    normed, *sent = first_call(tokens[0], ln1_gain, ln1_bias, w_qkv[0], bias_v)
    pairs = [partner_2(pair, "stream", 0) for pair in sent]
    queries, hot, turned_hot, key_hot, live, tiles = prep_call(
        stream, box_bins, segment_ids, key_mask, normed, w_qkv[0], bias_q, rel_table.reshape(3 * HEADS, BINS)
    )
    contexts, probs = [], []
    for group in range(GROUPS):
        context, prob = attend_call(group, queries, queue.after(pairs[group]), hot, key_hot, live, tiles)
        queue.mark = context
        contexts.append(context)
        probs.append(prob)
    output, d_middle, d_branch, d_context, feed_mine, feed_other, small = feed_call(
        order, tokens[0], contexts, cotangent[0], w_out[0], bias_out, ln2_gain, ln2_bias,
        w_in[0], bias_in, w_back[0], bias_back,
    )
    if ringed:
        feed = Ring(queue, feed_mine, feed_other)
    d_queries, backs, diagonals = [None] * GROUPS, [None] * GROUPS, [None] * GROUPS
    for group in range(GROUPS):
        d_queries[group], d_pair, diagonals[group] = attend_back_call(
            group, queries, pairs[group], turned_hot, key_hot, probs[group], queue.after(d_context)
        )
        queue.mark = d_queries[group]
        if ringed:
            if group == GROUPS - 1:
                feed.reduce()
                d_pair = queue.after(d_pair)
            backs[group] = partner_2(d_pair, "stream", 0)
            if group < GROUPS - 1:
                feed.reduce()
            if group:
                queue.wait(backs[group - 1])
        else:
            backs[group] = partner_2(d_pair, "stream", 0)
    rest_mine, rest_other = weights_call(order, queue.after(normed), d_branch, contexts, d_queries, backs)
    if ringed:
        queue.mark = rest_mine
        feed.reduce()
        rest = Ring(queue, rest_mine, rest_other)
    g_tokens, small = last_call(
        tokens[0], ln1_gain, w_qkv[0], queue.after(d_middle), d_queries, backs, diagonals, small
    )
    if ringed:
        queue.mark = g_tokens
        feed.reduce()
        rest.reduce()
        queue.free = True
        minor = Small(queue, small)

        def small_turn(value):
            minor.advance()
            value, minor.small = lax.optimization_barrier((value, minor.small))
            return value

        while feed.step < RING:
            feed_held = feed.reduce()
        back_chunks = gather(feed_held[:192])
        in_chunks = gather(feed_held[192:])
        g_w_back = open_call("back", places, back_chunks)
        g_w_in = open_call("inward", places, in_chunks)
        opened = [*g_w_back, *g_w_in]

        def back_turn(value):
            value, opened[0] = lax.optimization_barrier((value, opened[0]))
            return value

        def in_turn(value):
            value, opened[1] = lax.optimization_barrier((value, opened[1]))
            return value

        while rest.step < RING:
            if rest.step in SMALL_EARLY:
                rest.arrived = small_turn(rest.arrived)
            rest_held = rest.reduce()
        rest_chunks = gather(rest_held, {1: small_turn, 3: small_turn, 6: back_turn, 7: in_turn})
        opened += open_call("rest", places, rest_chunks)
        weights = [value[None] for value in opened]
        half = width // 2
        side = lax.axis_index("dp").reshape(1)
        shapes = [(1, half)] * 8 + [(1, 2 * width), (1, 3 * width)]
        outs = [jax.ShapeDtypeStruct(shape, jnp.float32) for shape in shapes]
        vectors = kernel_call(open_small_kernel, "open_small", 1, outs, side, minor.small, smem=1)
    else:
        weights, vectors = unringed_grads(
            (feed_mine, feed_other), (rest_mine, rest_other), small
        )
    g_w_back, g_w_in, g_w_qkv, g_w_out = weights
    (
        g_ln1_gain, g_ln1_bias, g_bias_q, g_bias_v, g_bias_out, g_ln2_gain, g_ln2_bias, g_bias_back, g_bias_in, g_rel_table,
    ) = vectors
    return (
        output[None], g_tokens[None], g_ln1_gain, g_ln1_bias, g_w_qkv, g_bias_q, g_bias_v, g_w_out,
        g_bias_out, g_ln2_gain, g_ln2_bias, g_w_in, g_bias_in, g_w_back, g_bias_back, g_rel_table,
    )


def solution(mesh):
    placed = (
        P("stream", ("group", "dp"), None),
        P("stream", ("group", "dp"), None),
        P(None, None, ("group", "dp"), None),
        P(None, ("group", "dp"), None),
        P(None, ("group", "dp"), None),
        P("stream", None),
        P("stream", None),
        P("stream", None, None),
        P("stream", None),
        P("stream", None),
        P("stream", None, None),
        P("stream", None),
        P("stream", None),
        P("stream", None),
        P("stream", None, None),
        P("stream", None),
        P("stream", None, None),
        P("stream", None),
        P("stream", None),
    )
    return jax.shard_map(
        on_device,
        mesh=mesh,
        in_specs=placed,
        out_specs=(
            P("stream", ("group", "dp"), None),
            P("stream", ("group", "dp"), None),
            P("stream", "dp"),
            P("stream", "dp"),
            P("stream", "dp", None),
            P("stream", "dp"),
            P("stream", "dp"),
            P("stream", "dp", None),
            P("stream", "dp"),
            P("stream", "dp"),
            P("stream", "dp"),
            P("stream", "dp", None),
            P("stream", "dp"),
            P("stream", "dp", None),
            P("stream", "dp"),
            P("stream", "dp"),
        ),
        check_vma=False,
    )
```

```python
import functools
import jax
import jax.numpy as jnp
from jax import lax
from jax.experimental import pallas as pl
from jax.experimental.pallas import tpu as pltpu
from jax.sharding import PartitionSpec as P

EPSILON = 1e-05
STRIP = 64
HEADS = 12
BINS = 128
GROUPS = 3
NEGATIVE = -1000000000.0
HIGHEST = lax.Precision.HIGHEST
RING = 8
RING_ORDER = (0, 2, 4, 6, 7, 5, 3, 1)
ROOT_HALF = 0.7071067811865476
DENSITY = 0.3989422804014327


def dot_plain(a, b):
    return lax.dot_general(a, b, (((1,), (0,)), ((), ())), preferred_element_type=jnp.float32)


def dot_across(a, b):
    return lax.dot_general(a, b, (((0,), (0,)), ((), ())), preferred_element_type=jnp.float32)


def dot_back(a, b):
    return lax.dot_general(a, b, (((1,), (1,)), ((), ())), preferred_element_type=jnp.float32)


def row_stats(rows):
    center = rows - jnp.mean(rows, axis=-1, keepdims=True)
    spread = jnp.mean(center * center, axis=-1, keepdims=True)
    rate = lax.rsqrt(spread + EPSILON)
    return center * rate, rate


def fold(rows):
    return jnp.sum(rows.reshape(rows.shape[0] // 8, 8, rows.shape[1]), axis=0)


def strips(count, body):
    for index in range(count // STRIP):
        body(pl.ds(index * STRIP, STRIP))


def place_chunk(target, mine_ref, other_ref, value, rows=slice(None)):
    @pl.when(target < 8)
    def _():
        mine_ref[target, rows, :] = value

    @pl.when(target >= 8)
    def _():
        other_ref[target - 8, rows, :] = value


def put_halves(small_ref, row, vector):
    half = vector.shape[1] // 2
    width = small_ref.shape[2]
    for side in range(2):
        for piece in range(half // width):
            start = side * half + piece * width
            small_ref[side, row + piece : row + piece + 1, :] = vector[:, start : start + width]


def feed_kernel(
    order_ref,
    tokens_ref,
    context_0_ref,
    context_1_ref,
    context_2_ref,
    cot_ref,
    w_out_ref,
    b_out_ref,
    gain_ref,
    shift_ref,
    w_in_ref,
    b_in_ref,
    w_back_ref,
    b_back_ref,
    out_ref,
    d_middle_ref,
    d_branch_ref,
    d_context_ref,
    mine_ref,
    other_ref,
    small_ref,
    middle_ref,
    normed_ref,
    turned_ref,
    pre_ref,
    d_act_ref,
    act_ref,
    d_pre_ref,
    total_ref,
    d_normed_ref,
    sums_ref,
    in_sum_ref,
):
    step = pl.program_id(0)
    last = pl.num_programs(0) - 1
    rows = tokens_ref.shape[0]
    block = w_in_ref.shape[1]

    @pl.when(step == 0)
    def _():
        part = context_0_ref.shape[1]
        middle_ref[...] = (
            dot_plain(context_0_ref[...], w_out_ref[:part])
            + dot_plain(context_1_ref[...], w_out_ref[part : 2 * part])
            + dot_plain(context_2_ref[...], w_out_ref[2 * part :])
        )
        sums_ref[...] = jnp.zeros_like(sums_ref)
        small_ref[...] = jnp.zeros_like(small_ref)
        total_ref[...] = jnp.zeros_like(total_ref)
        d_normed_ref[...] = jnp.zeros_like(d_normed_ref)

        def first(at):
            value = middle_ref[at, :] + tokens_ref[at, :].astype(jnp.float32) + b_out_ref[...]
            middle_ref[at, :] = value
            hat, _ = row_stats(value)
            normed_ref[at, :] = (hat * gain_ref[...] + shift_ref[...]).astype(jnp.bfloat16)
            sums_ref[0] += fold(cot_ref[at, :].astype(jnp.float32))

        strips(rows, first)
        turned_ref[...] = normed_ref[...].T

    pre_ref[...] = dot_plain(normed_ref[...], w_in_ref[...])
    d_act_ref[...] = dot_back(cot_ref[...], w_back_ref[...])
    in_sum_ref[...] = jnp.zeros_like(in_sum_ref)

    def middle_part(at):
        value = pre_ref[at, :] + b_in_ref[...]
        chance = 0.5 + 0.5 * lax.erf(value * ROOT_HALF)
        slope = chance + value * (DENSITY * jnp.exp(-0.5 * value * value))
        act_ref[at, :] = (value * chance).astype(jnp.bfloat16)
        d_pre = (d_act_ref[at, :] * slope).astype(jnp.bfloat16)
        d_pre_ref[at, :] = d_pre
        in_sum_ref[...] += fold(d_pre.astype(jnp.float32))

    strips(rows, middle_part)
    total_ref[...] += dot_plain(act_ref[...], w_back_ref[...])
    d_normed_ref[...] += dot_back(d_pre_ref[...], w_in_ref[...])
    per_block = block // 192
    back = dot_across(act_ref[...], cot_ref[...]).astype(jnp.bfloat16)
    for piece in range(per_block):
        place_chunk(
            order_ref[step * per_block + piece],
            mine_ref,
            other_ref,
            back[piece * 192 : piece * 192 + 192],
            slice(0, 192),
        )
    inward = dot_plain(turned_ref[...], d_pre_ref[...]).astype(jnp.bfloat16)
    at_rows = pl.ds(pl.multiple_of(192 + step * 48, 16), 48)
    for piece in range(16):
        place_chunk(
            order_ref[piece], mine_ref, other_ref, inward[piece * 48 : piece * 48 + 48], at_rows
        )
    in_sum = jnp.sum(in_sum_ref[...], axis=0, keepdims=True)
    side = step // 2
    row = 8 + 2 * (step % 2)
    small_ref[side, pl.ds(row, 1), :] = in_sum[:, :384]
    small_ref[side, pl.ds(row + 1, 1), :] = in_sum[:, 384:]

    @pl.when(step == last)
    def _():
        def final(at):
            value = middle_ref[at, :]
            out_ref[at, :] = (value + total_ref[at, :] + b_back_ref[...]).astype(jnp.bfloat16)
            hat, rate = row_stats(value)
            d_normed = d_normed_ref[at, :]
            sums_ref[1] += fold(d_normed * hat)
            sums_ref[2] += fold(d_normed)
            scaled = d_normed * gain_ref[...]
            inner = (
                scaled
                - jnp.mean(scaled, axis=-1, keepdims=True)
                - hat * jnp.mean(scaled * hat, axis=-1, keepdims=True)
            )
            d_middle = cot_ref[at, :].astype(jnp.float32) + rate * inner
            d_middle_ref[at, :] = d_middle
            branch = d_middle.astype(jnp.bfloat16)
            d_branch_ref[at, :] = branch
            sums_ref[3] += fold(branch.astype(jnp.float32))

        strips(rows, final)
        d_context_ref[...] = dot_back(d_branch_ref[...], w_out_ref[...]).astype(jnp.bfloat16)
        for index, row in ((0, 7), (1, 5), (2, 6), (3, 4)):
            put_halves(small_ref, row, jnp.sum(sums_ref[index], axis=0, keepdims=True))


def feed_call(order, tokens, contexts, cot, w_out, b_out, gain, shift, w_in, b_in, w_back, b_back):
    rows, width = tokens.shape
    inner = w_in.shape[1]
    block = 768
    fixed = lambda shape: pl.BlockSpec(shape, lambda j, o: (0,) * len(shape), pipeline_mode=pl.Buffered(1))
    wide = lambda dtype: jax.ShapeDtypeStruct((rows, width), dtype)
    ring = jax.ShapeDtypeStruct((RING, 384, width), jnp.bfloat16)
    f32, bf16 = jnp.float32, jnp.bfloat16
    vmem = pltpu.VMEM
    return pl.pallas_call(
        feed_kernel,
        out_shape=(wide(bf16), wide(f32), wide(bf16), wide(bf16), ring, ring,
                   jax.ShapeDtypeStruct((2, 24, 384), f32)),
        grid_spec=pltpu.PrefetchScalarGridSpec(
            num_scalar_prefetch=1,
            grid=(inner // block,),
            in_specs=[
                fixed((rows, width)),
                fixed((rows, width // GROUPS)), fixed((rows, width // GROUPS)), fixed((rows, width // GROUPS)),
                fixed((rows, width)),
                fixed((width, width)), fixed((1, width)), fixed((1, width)), fixed((1, width)),
                pl.BlockSpec((width, block), lambda j, o: (0, j)),
                pl.BlockSpec((1, block), lambda j, o: (0, j)),
                pl.BlockSpec((block, width), lambda j, o: (j, 0)),
                fixed((1, width)),
            ],
            out_specs=[fixed((rows, width))] * 4 + [fixed((RING, 384, width))] * 2 + [fixed((2, 24, 384))],
            scratch_shapes=[
                vmem((rows, width), f32), vmem((rows, width), bf16), vmem((width, rows), bf16),
                vmem((rows, block), f32), vmem((rows, block), f32),
                vmem((rows, block), bf16), vmem((rows, block), bf16),
                vmem((rows, width), f32), vmem((rows, width), f32),
                vmem((4, 8, width), f32), vmem((8, block), f32),
            ],
        ),
        compiler_params=pltpu.CompilerParams(vmem_limit_bytes=60 << 20),
        cost_estimate=price(30),
        name="feed",
    )(order, tokens, *contexts, cot, w_out, b_out, gain, shift, w_in, b_in, w_back, b_back)


def first_kernel(tokens_ref, gain_ref, shift_ref, w_ref, bias_ref, normed_ref, *sent_refs):
    rows, width = tokens_ref.shape

    def norm(at):
        hat, _ = row_stats(tokens_ref[at, :].astype(jnp.float32))
        normed_ref[at, :] = (hat * gain_ref[...] + shift_ref[...]).astype(jnp.bfloat16)

    strips(rows, norm)
    part = width // GROUPS
    for group, sent_ref in enumerate(sent_refs):
        at = group * part
        sent_ref[0] = dot_plain(normed_ref[...], w_ref[:, width + at : width + at + part]).astype(jnp.bfloat16)
        sent_ref[1] = (
            dot_plain(normed_ref[...], w_ref[:, 2 * width + at : 2 * width + at + part])
            + bias_ref[:, at : at + part]
        ).astype(jnp.bfloat16)


def whole_specs(count):
    return [pl.BlockSpec(memory_space=pltpu.VMEM)] * count


def price(micros):
    return pl.CostEstimate(flops=int(micros * 1e9), transcendentals=0, bytes_accessed=0)


def kernel_call(kernel, name, micros, outs, *args, scratch=(), smem=0, aliases={}):
    specs = [pl.BlockSpec(memory_space=pltpu.SMEM)] * smem + whole_specs(len(args) - smem)
    return pl.pallas_call(
        kernel,
        out_shape=tuple(outs),
        in_specs=specs,
        out_specs=tuple(whole_specs(len(outs))),
        scratch_shapes=list(scratch),
        input_output_aliases=aliases,
        cost_estimate=price(micros),
        compiler_params=pltpu.CompilerParams(vmem_limit_bytes=60 << 20),
        name=name,
    )(*args)


def first_call(tokens, gain, shift, w_qkv, bias_v):
    rows, width = tokens.shape
    outs = [jax.ShapeDtypeStruct((rows, width), jnp.bfloat16)]
    outs += [jax.ShapeDtypeStruct((2, rows, width // GROUPS), jnp.bfloat16)] * GROUPS
    return kernel_call(first_kernel, "first", 5, outs, tokens, gain, shift, w_qkv, bias_v)


def code_columns(rows_of_codes, rows):
    blank = jnp.zeros((5, rows), jnp.float32)
    return jnp.concatenate([r.astype(jnp.float32) for r in rows_of_codes] + [blank], axis=0).T


def prep_kernel(
    stream_ref, box_ref, segment_ref, mask_ref, normed_ref, w_ref, bias_ref, table_ref,
    queries_ref, hot_ref, turned_hot_ref, key_hot_ref, live_ref, tiles_ref,
):
    rows = normed_ref.shape[0]
    own = stream_ref[0]
    far = 1 - own
    queries_ref[...] = (dot_plain(normed_ref[...], w_ref[:, : normed_ref.shape[1]]) + bias_ref[...]).astype(jnp.bfloat16)
    live_ref[...] = mask_ref[far]
    own_codes = code_columns([box_ref[own, 0], box_ref[own, 1], segment_ref[own]], rows)
    far_codes = code_columns([box_ref[far, 0], box_ref[far, 1], segment_ref[far]], rows)
    levels = lax.broadcasted_iota(jnp.int32, (rows, BINS), 1).astype(jnp.float32)
    for axis in range(3):
        lanes = slice(axis * BINS, axis * BINS + BINS)
        column = own_codes[:, axis : axis + 1]
        hot_ref[:, lanes] = jnp.where(column == levels, 1.0, 0.0).astype(jnp.bfloat16)
        turned_hot_ref[:, lanes] = jnp.where(BINS - 1 - column == levels, 1.0, 0.0).astype(jnp.bfloat16)
        key_hot_ref[:, lanes] = jnp.where(far_codes[:, axis : axis + 1] == levels, 1.0, 0.0).astype(jnp.bfloat16)
    half = BINS // 2
    entry = lax.broadcasted_iota(jnp.int32, (BINS, 2 * BINS), 0)
    gap = lax.broadcasted_iota(jnp.int32, (BINS, 2 * BINS), 1)
    gap = jnp.where(gap < BINS, -gap, 2 * BINS - gap)
    pick = jnp.where(jnp.clip(gap, -half, half - 1) + half == entry, 1.0, 0.0).astype(jnp.bfloat16)
    spread = dot_plain(table_ref[...].astype(jnp.bfloat16), pick)
    for index in range(3 * HEADS):
        wide = jnp.broadcast_to(spread[index : index + 1, :], (BINS, 2 * BINS))
        rolled = pltpu.roll(wide, 0, 1, stride=1, stride_axis=0)
        tiles_ref[index] = rolled[:, :BINS].astype(jnp.bfloat16)


def prep_call(stream, box_bins, segment_ids, key_mask, normed, w_qkv, bias_q, table):
    rows, width = normed.shape
    hot = jax.ShapeDtypeStruct((rows, 3 * BINS), jnp.bfloat16)
    outs = [
        jax.ShapeDtypeStruct((rows, width), jnp.bfloat16), hot, hot, hot,
        jax.ShapeDtypeStruct((1, rows), jnp.int32),
        jax.ShapeDtypeStruct((3 * HEADS, BINS, BINS), jnp.bfloat16),
    ]
    return kernel_call(prep_kernel, "prep", 5, outs, stream, box_bins, segment_ids, key_mask, normed, w_qkv, bias_q, table, smem=1)


def half_of(slab, odd):
    lane = lax.broadcasted_iota(jnp.int32, slab.shape, 1)
    keep = (lane >= 64) if odd else (lane < 64)
    return jnp.where(keep, slab, jnp.zeros_like(slab))


def attend_kernel(group, queries_ref, pair_ref, hot_ref, key_hot_ref, live_ref, tiles_ref,
                  context_ref, probs_ref, left_ref, right_ref, scores_ref):
    rows = queries_ref.shape[0]
    part = pair_ref.shape[2]
    def slab_step(slab, carry):
        lanes = pl.ds(pl.multiple_of(slab * 128, 128), 128)
        wide = pl.ds(pl.multiple_of(group * part + slab * 128, 128), 128)
        right_ref[slab, :, :128] = pair_ref[0, :, lanes]
        right_ref[slab, :, 128:] = key_hot_ref[...]
        halves = []
        for odd in range(2):
            head = slab * 2 + odd
            left_ref[head, :, :128] = half_of(queries_ref[:, wide].astype(jnp.float32) * 0.125, odd).astype(jnp.bfloat16)
            for axis in range(3):
                cut = slice(axis * BINS, axis * BINS + BINS)
                tile = tiles_ref[axis * HEADS + group * (part // 64) + head]
                left_ref[head, :, 128 + axis * BINS : 256 + axis * BINS] = dot_plain(hot_ref[:, cut], tile).astype(jnp.bfloat16)
            scores_ref[head] = dot_back(left_ref[head], right_ref[slab])

            def soft(at):
                scores = jnp.where(live_ref[...] > 0, scores_ref[head, at, :], NEGATIVE)
                top = jnp.max(scores, axis=-1, keepdims=True)
                weights = jnp.exp(scores - top)
                rate = 1.0 / jnp.sum(weights, axis=-1, keepdims=True)
                probs_ref[head, at, :] = (weights * rate).astype(jnp.bfloat16)

            strips(rows, soft)
            halves.append(half_of(dot_plain(probs_ref[head], pair_ref[1, :, lanes]), odd))
        context_ref[:, lanes] = (halves[0] + halves[1]).astype(jnp.bfloat16)
        return carry

    lax.fori_loop(0, part // 128, slab_step, 0)


def attend_call(group, queries, pair, hot, key_hot, live, tiles):
    rows = queries.shape[0]
    part = pair.shape[2]
    heads = part // 64
    outs = [
        jax.ShapeDtypeStruct((rows, part), jnp.bfloat16),
        jax.ShapeDtypeStruct((heads, rows, rows), jnp.bfloat16),
    ]
    scratch = [
        pltpu.VMEM((heads, rows, 512), jnp.bfloat16),
        pltpu.VMEM((part // 128, rows, 512), jnp.bfloat16),
        pltpu.VMEM((heads, rows, rows), jnp.float32),
    ]
    return kernel_call(functools.partial(attend_kernel, group), f"attend_{group}", 7, outs,
                       queries, pair, hot, key_hot, live, tiles, scratch=scratch)


def attend_back_kernel(group, queries_ref, pair_ref, turned_hot_ref, key_hot_ref, probs_ref, d_context_ref,
                       d_queries_ref, d_pair_ref, diagonal_ref, right_ref, slope_ref, d_scores_ref):
    rows = queries_ref.shape[0]
    part = pair_ref.shape[2]
    def slab_step(slab, carry):
        lanes = pl.ds(pl.multiple_of(slab * 128, 128), 128)
        wide = pl.ds(pl.multiple_of(group * part + slab * 128, 128), 128)
        right_ref[slab, :, :128] = pair_ref[0, :, lanes]
        right_ref[slab, :, 128:] = key_hot_ref[...]
        d_query = d_key = d_value = 0.0
        for odd in range(2):
            head = slab * 2 + odd
            query = half_of(queries_ref[:, wide], odd)
            d_context = half_of(d_context_ref[:, wide], odd)
            slope_ref[head] = dot_back(d_context, pair_ref[1, :, lanes])

            def soft(at):
                probs = probs_ref[head, at, :].astype(jnp.float32)
                slope = slope_ref[head, at, :]
                centre = jnp.sum(probs * slope, axis=-1, keepdims=True)
                d_scores_ref[head, at, :] = (probs * (slope - centre)).astype(jnp.bfloat16)

            strips(rows, soft)
            d_value = d_value + dot_across(probs_ref[head], d_context)
            d_key = d_key + dot_across(d_scores_ref[head], query)
            both = dot_plain(d_scores_ref[head], right_ref[slab])
            d_query = d_query + half_of(both[:, :128], odd)
            spread = both[:, 128:].astype(jnp.bfloat16)
            for axis in range(3):
                cut = slice(axis * BINS, axis * BINS + BINS)
                tile = dot_across(turned_hot_ref[:, cut], spread[:, cut])
                padded = jnp.concatenate([tile, jnp.zeros_like(tile)], axis=1)
                rolled = pltpu.roll(padded, 0, 1, stride=1, stride_axis=0)
                diagonal_ref[axis, pl.ds(head, 1), :] = jnp.sum(rolled, axis=0, keepdims=True)
        d_queries_ref[:, lanes] = (d_query * 0.125).astype(jnp.bfloat16)
        d_pair_ref[0, :, lanes] = (d_key * 0.125).astype(jnp.bfloat16)
        d_pair_ref[1, :, lanes] = d_value.astype(jnp.bfloat16)
        return carry

    lax.fori_loop(0, part // 128, slab_step, 0)


def attend_back_call(group, queries, pair, turned_hot, key_hot, probs, d_context):
    rows = queries.shape[0]
    part = pair.shape[2]
    heads = part // 64
    outs = [
        jax.ShapeDtypeStruct((rows, part), jnp.bfloat16),
        jax.ShapeDtypeStruct((2, rows, part), jnp.bfloat16),
        jax.ShapeDtypeStruct((3, heads, 2 * BINS), jnp.float32),
    ]
    scratch = [
        pltpu.VMEM((part // 128, rows, 512), jnp.bfloat16),
        pltpu.VMEM((heads, rows, rows), jnp.float32),
        pltpu.VMEM((heads, rows, rows), jnp.bfloat16),
    ]
    return kernel_call(functools.partial(attend_back_kernel, group), f"attend_back_{group}", 8, outs,
                       queries, pair, turned_hot, key_hot, probs, d_context, scratch=scratch)


def weights_kernel(
    order_ref, normed_ref, d_branch_ref, context_0_ref, context_1_ref, context_2_ref,
    d_query_0_ref, d_query_1_ref, d_query_2_ref, back_0_ref, back_1_ref, back_2_ref,
    mine_ref, other_ref, joined_ref, left_ref,
):
    part = context_0_ref.shape[1]
    queries = (d_query_0_ref, d_query_1_ref, d_query_2_ref)
    backs = (back_0_ref, back_1_ref, back_2_ref)
    contexts = (context_0_ref, context_1_ref, context_2_ref)
    for group in range(GROUPS):
        lanes = slice(group * part, group * part + part)
        joined_ref[0, :, lanes] = queries[group][...]
        joined_ref[1, :, lanes] = backs[group][0]
        joined_ref[2, :, lanes] = backs[group][1]
        joined_ref[3, :, lanes] = contexts[group][...]
    left_ref[0] = normed_ref[...]
    left_ref[1] = joined_ref[3]
    joined_ref[3] = d_branch_ref[...]

    def block_step(block, carry):
        value = dot_across(left_ref[block // 3], joined_ref[block]).astype(jnp.bfloat16)
        rows = pl.ds(pl.multiple_of(block * 48, 16), 48)
        for piece in range(16):
            place_chunk(order_ref[piece], mine_ref, other_ref, value[piece * 48 : piece * 48 + 48], rows)
        return carry

    lax.fori_loop(0, 4, block_step, 0)


def weights_call(order, normed, d_branch, contexts, d_queries, backs):
    rows, width = normed.shape
    ring = jax.ShapeDtypeStruct((RING, 192, width), jnp.bfloat16)
    scratch = [pltpu.VMEM((4, rows, width), jnp.bfloat16), pltpu.VMEM((2, rows, width), jnp.bfloat16)]
    return kernel_call(weights_kernel, "weights", 7, [ring, ring], order, normed, d_branch,
                       *contexts, *d_queries, *backs, scratch=scratch, smem=1)


def last_kernel(
    side_ref, tokens_ref, gain_ref, w_ref, d_middle_ref, d_query_0_ref, d_query_1_ref, d_query_2_ref,
    back_0_ref, back_1_ref, back_2_ref, diagonal_0_ref, diagonal_1_ref, diagonal_2_ref, start_ref,
    g_tokens_ref, mine_ref, other_ref, small_ref, d_normed_ref, sums_ref,
):
    rows, width = tokens_ref.shape
    part = width // GROUPS
    queries = (d_query_0_ref, d_query_1_ref, d_query_2_ref)
    backs = (back_0_ref, back_1_ref, back_2_ref)
    small_ref[...] = start_ref[...]
    sums_ref[...] = jnp.zeros_like(sums_ref)
    total = 0.0
    for group in range(GROUPS):
        at = group * part
        total = total + dot_back(queries[group][...], w_ref[:, at : at + part])
        total = total + dot_back(backs[group][0], w_ref[:, width + at : width + at + part])
        total = total + dot_back(backs[group][1], w_ref[:, 2 * width + at : 2 * width + at + part])
    d_normed_ref[...] = total

    def final(at):
        hat, rate = row_stats(tokens_ref[at, :].astype(jnp.float32))
        d_normed = d_normed_ref[at, :]
        sums_ref[0] += fold(d_normed * hat)
        sums_ref[1] += fold(d_normed)
        for group in range(GROUPS):
            lanes = slice(group * part, group * part + part)
            sums_ref[2, :, lanes] += fold(queries[group][at, :].astype(jnp.float32))
            sums_ref[3, :, lanes] += fold(backs[group][1, at, :].astype(jnp.float32))
        scaled = d_normed * gain_ref[...]
        inner = (
            scaled
            - jnp.mean(scaled, axis=-1, keepdims=True)
            - hat * jnp.mean(scaled * hat, axis=-1, keepdims=True)
        )
        g_tokens_ref[at, :] = (d_middle_ref[at, :] + rate * inner).astype(jnp.bfloat16)

    strips(rows, final)
    for row in range(4):
        put_halves(small_ref, row, jnp.sum(sums_ref[row], axis=0, keepdims=True))
    half = BINS // 2
    gap = BINS - 1 - lax.broadcasted_iota(jnp.int32, (2 * BINS, BINS), 0)
    entry = lax.broadcasted_iota(jnp.int32, (2 * BINS, BINS), 1)
    pick = jnp.where(jnp.clip(gap, -half, half - 1) + half == entry, 1.0, 0.0)
    for group, diagonal_ref in enumerate((diagonal_0_ref, diagonal_1_ref, diagonal_2_ref)):
        for axis in range(3):
            table = lax.dot_general(
                diagonal_ref[axis], pick, (((1,), (0,)), ((), ())),
                precision=HIGHEST, preferred_element_type=jnp.float32,
            )
            for head in range(part // 64):
                index = axis * HEADS + group * (part // 64) + head
                side, place = divmod(index, 18)
                row, lane = divmod(place, 3)
                small_ref[side, 12 + row : 13 + row, lane * BINS : lane * BINS + BINS] = table[head : head + 1, :]
    for out_ref, side in ((mine_ref, side_ref[0]), (other_ref, 1 - side_ref[0])):
        out_ref[...] = jnp.zeros_like(out_ref)
        out_ref[:12, :384] = small_ref[side, :12, :]
        out_ref[:12, 384:] = small_ref[side, 12:, :]


def last_call(side, tokens, gain, w_qkv, d_middle, d_queries, backs, diagonals, start):
    rows, width = tokens.shape
    packed = jax.ShapeDtypeStruct((16, width), jnp.float32)
    outs = [jax.ShapeDtypeStruct((rows, width), jnp.bfloat16), packed, packed]
    scratch = [pltpu.VMEM(start.shape, jnp.float32), pltpu.VMEM((rows, width), jnp.float32), pltpu.VMEM((4, 8, width), jnp.float32)]
    return kernel_call(last_kernel, "last", 8, outs, side, tokens, gain, w_qkv, d_middle,
                       *d_queries, *backs, *diagonals, start, scratch=scratch, smem=1)


def open_kernel(layout, place_ref, *refs):
    width = refs[0].shape[1]
    for out_ref, (start, blocks) in zip(refs[RING:], layout):
        size = out_ref.shape[0] // RING
        for index in range(RING):
            to = pl.ds(pl.multiple_of(place_ref[index] * size, size), size)
            for block in range(blocks):
                at = start + block * size
                out_ref[to, block * width : block * width + width] = refs[index][at : at + size, :].astype(jnp.float32)


def open_rest_kernel(place_ref, *refs):
    chunks, outs, parts_ref = refs[:RING], refs[RING:-1], refs[-1]
    open_kernel(((0, 3), (144, 1)), place_ref, *chunks, outs[0], outs[1])
    for index in range(RING):
        parts_ref[place_ref[index]] = chunks[index][192:, :].astype(jnp.float32)
    total = parts_ref[0]
    for index in range(1, RING):
        total = total + parts_ref[index]
    parts_ref[0] = total
    for row in range(8):
        outs[2 + row][...] = parts_ref[0, row : row + 1, :384]
    for row in range(4):
        outs[10][:, row * 384 : row * 384 + 384] = parts_ref[0, 8 + row : 9 + row, :384]
    for row in range(6):
        outs[11][:, row * 384 : row * 384 + 384] = parts_ref[0, row : row + 1, 384:]


def open_call(name, places, chunks):
    width = chunks[0].shape[1]
    half = width // 2
    if name == "rest":
        shapes = [(half, 3 * width), (half, width)] + [(1, half)] * 8 + [(1, 2 * width), (1, 3 * width)]
        kernel, scratch = open_rest_kernel, [pltpu.VMEM((RING, 16, width), jnp.float32)]
    else:
        shapes = [(2 * width, width)] if name == "back" else [(half, 4 * width)]
        kernel, scratch = functools.partial(open_kernel, ((0, shapes[0][1] // width),)), []
    outs = [jax.ShapeDtypeStruct(shape, jnp.float32) for shape in shapes]
    return kernel_call(kernel, f"open_{name}", 4, outs, places, *chunks, smem=1, scratch=scratch)


def partner_2(shard, axis, distance):
    return lax.ppermute(shard, axis, [(i, i ^ 1 << distance) for i in range(lax.axis_size(axis))])


def ring_send(chunk):
    pairs = []
    for place in range(RING):
        ahead = RING_ORDER[(place + 1) % RING]
        behind = RING_ORDER[(place - 1) % RING]
        pairs.append((RING_ORDER[place] * 2, ahead * 2))
        pairs.append((RING_ORDER[place] * 2 + 1, behind * 2 + 1))
    return lax.ppermute(chunk, ("group", "dp"), pairs)


def ring_place():
    group = lax.axis_index("group")
    place = jnp.int32(0)
    for position, member in enumerate(RING_ORDER):
        place = jnp.where(group == member, position, place)
    return place


def ring_plan(ringed):
    index = lax.iota(jnp.int32, 2 * RING)
    steps = lax.iota(jnp.int32, RING)
    if not ringed:
        return index, steps
    dp = lax.axis_index("dp")
    place = ring_place()
    side = index // RING
    start = jnp.where(side == 0, place, RING - place)
    order = (start - index % RING + RING) % RING + jnp.where(side == dp, 0, RING)
    start = jnp.where(dp == 0, place, RING - place)
    return order, (start + 1 - steps + RING) % RING


def add_low(*terms):
    return sum(term.astype(jnp.float32) for term in terms).astype(jnp.bfloat16)


def unringed_total(mine, other):
    return lax.psum(jnp.concatenate([mine, other]).astype(jnp.float32), ("group", "dp"))


def unringed_rows(packed):
    blocks = packed.shape[1] // 48
    rows = packed.reshape(2 * RING, blocks, 48, packed.shape[2])
    return jnp.swapaxes(rows, 1, 2).reshape(2 * RING * 48, blocks * packed.shape[2])


def own_share(whole):
    share = whole.shape[0] // lax.axis_size("dp")
    return lax.dynamic_slice_in_dim(whole, lax.axis_index("dp") * share, share, 0)[None]


def unringed_grads(feed, rest, small):
    feed = unringed_total(*feed)
    rest = unringed_total(*rest)
    small = lax.psum(jnp.stack(small)[:, :12], ("group", "dp"))
    small = jnp.concatenate([small[:, :, :384], small[:, :, 384:]], axis=1)
    vectors = [small[:, row].reshape(-1) for row in range(8)]
    vectors += [small[:, 8:12].reshape(-1), small[:, 12:18].reshape(-1)]
    weights = (
        feed[:, :192].reshape(-1, feed.shape[2]),
        unringed_rows(feed[:, 192:]),
        unringed_rows(rest[:, :144]),
        unringed_rows(rest[:, 144:]),
    )
    return [own_share(weight) for weight in weights], [own_share(vector) for vector in vectors]


class Ordered:
    def __init__(self):
        self.mark = None
        self.free = False

    def after(self, value):
        if self.mark is None or self.free:
            return value
        return lax.optimization_barrier((value, self.mark))[0]

    def wait(self, *values):
        self.mark = (self.mark, *values)


class Ring:
    def __init__(self, order, mine, other):
        self.order, self.mine = order, mine
        self.met = lax.ppermute(order.after(other), "dp", [(0, 1), (1, 0)])
        self.arrived, self.step = None, 0

    def reduce(self):
        step, order = self.step, self.order
        if step == 0:
            held = add_low(self.mine[0], order.after(self.met)[0])
        else:
            held = add_low(order.after(self.arrived), self.mine[step], self.met[step])
        order.mark = held
        if step < RING - 1:
            self.arrived = ring_send(held)
        self.step += 1
        return held

    def split(self, cuts):
        pieces = []
        for start, stop in zip(cuts, cuts[1:]):
            piece = Ring.__new__(Ring)
            piece.order, piece.step = self.order, self.step
            piece.mine, piece.met = self.mine[:, start:stop], self.met[:, start:stop]
            piece.arrived = None if self.arrived is None else self.arrived[start:stop]
            pieces.append(piece)
        return pieces


def gather(held, waits={}):
    chunks = [held]
    for step in range(1, RING):
        held = ring_send(held)
        if step in waits:
            held = waits[step](held)
        chunks.append(held)
    return chunks


def on_device(
    tokens, cotangent, box_bins, segment_ids, key_mask, ln1_gain, ln1_bias, w_qkv, bias_q, bias_v,
    w_out, bias_out, ln2_gain, ln2_bias, w_in, bias_in, w_back, bias_back, rel_table,
):
    ringed = lax.axis_size("group") == RING and lax.axis_size("dp") == 2
    width = tokens.shape[2]
    order, places = ring_plan(ringed)
    queue = Ordered()
    stream = lax.axis_index("stream").reshape(1)
    normed, *sent = first_call(tokens[0], ln1_gain, ln1_bias, w_qkv[0], bias_v)
    pairs = [partner_2(pair, "stream", 0) for pair in sent]
    queries, hot, turned_hot, key_hot, live, tiles = prep_call(
        stream, box_bins, segment_ids, key_mask, normed, w_qkv[0], bias_q, rel_table.reshape(3 * HEADS, BINS)
    )
    contexts, probs = [], []
    for group in range(GROUPS):
        context, prob = attend_call(group, queries, queue.after(pairs[group]), hot, key_hot, live, tiles)
        queue.mark = context
        contexts.append(context)
        probs.append(prob)
    output, d_middle, d_branch, d_context, feed_mine, feed_other, small = feed_call(
        order, tokens[0], contexts, cotangent[0], w_out[0], bias_out, ln2_gain, ln2_bias,
        w_in[0], bias_in, w_back[0], bias_back,
    )
    if ringed:
        feed = Ring(queue, feed_mine, feed_other)
    d_queries, backs, diagonals = [None] * GROUPS, [None] * GROUPS, [None] * GROUPS
    for group in range(GROUPS):
        d_queries[group], d_pair, diagonals[group] = attend_back_call(
            group, queries, pairs[group], turned_hot, key_hot, probs[group], queue.after(d_context)
        )
        queue.mark = d_queries[group]
        if ringed:
            if group == GROUPS - 1:
                feed.reduce()
                d_pair = queue.after(d_pair)
            backs[group] = partner_2(d_pair, "stream", 0)
            if group < GROUPS - 1:
                feed.reduce()
            if group:
                queue.wait(backs[group - 1])
        else:
            backs[group] = partner_2(d_pair, "stream", 0)
    rest_mine, rest_other = weights_call(order, queue.after(normed), d_branch, contexts, d_queries, backs)
    if ringed:
        queue.mark = rest_mine
        feed.reduce()
        rest = Ring(queue, rest_mine, rest_other)
    side = lax.axis_index("dp").reshape(1)
    g_tokens, *small = last_call(
        side if ringed else jnp.zeros_like(side), tokens[0], ln1_gain, w_qkv[0], queue.after(d_middle), d_queries, backs, diagonals, small
    )
    if ringed:
        queue.mark = g_tokens
        feed.reduce()
        rest.reduce()
        queue.free = True
        held_parts = []
        for piece in feed.split((0, 192, 384)):
            while piece.step < RING:
                held = piece.reduce()
            held_parts.append(held)
        back_chunks = gather(held_parts[0])
        in_chunks = gather(held_parts[1])
        g_w_back = open_call("back", places, back_chunks)
        g_w_in = open_call("inward", places, in_chunks)
        opened = [*g_w_back, *g_w_in]

        def back_turn(value):
            value, opened[0] = lax.optimization_barrier((value, opened[0]))
            return value

        def in_turn(value):
            value, opened[1] = lax.optimization_barrier((value, opened[1]))
            return value

        while rest.step < RING:
            rest_held = rest.reduce()
        small_held = add_low(small[0], lax.ppermute(small[1], "dp", [(0, 1), (1, 0)]))
        rest_held = jnp.concatenate([rest_held, small_held], axis=0)
        rest_chunks = gather(rest_held, {6: back_turn, 7: in_turn})
        opened += open_call("rest", places, rest_chunks)
        weights = [value[None] for value in opened[:4]]
        vectors = opened[4:]
    else:
        weights, vectors = unringed_grads(
            (feed_mine, feed_other), (rest_mine, rest_other), small
        )
    g_w_back, g_w_in, g_w_qkv, g_w_out = weights
    (
        g_ln1_gain, g_ln1_bias, g_bias_q, g_bias_v, g_bias_out, g_ln2_gain, g_ln2_bias, g_bias_back, g_bias_in, g_rel_table,
    ) = vectors
    return (
        output[None], g_tokens[None], g_ln1_gain, g_ln1_bias, g_w_qkv, g_bias_q, g_bias_v, g_w_out,
        g_bias_out, g_ln2_gain, g_ln2_bias, g_w_in, g_bias_in, g_w_back, g_bias_back, g_rel_table,
    )


def solution(mesh):
    placed = (
        P("stream", ("group", "dp"), None),
        P("stream", ("group", "dp"), None),
        P(None, None, ("group", "dp"), None),
        P(None, ("group", "dp"), None),
        P(None, ("group", "dp"), None),
        P("stream", None),
        P("stream", None),
        P("stream", None, None),
        P("stream", None),
        P("stream", None),
        P("stream", None, None),
        P("stream", None),
        P("stream", None),
        P("stream", None),
        P("stream", None, None),
        P("stream", None),
        P("stream", None, None),
        P("stream", None),
        P("stream", None),
    )
    return jax.shard_map(
        on_device,
        mesh=mesh,
        in_specs=placed,
        out_specs=(
            P("stream", ("group", "dp"), None),
            P("stream", ("group", "dp"), None),
            P("stream", "dp"),
            P("stream", "dp"),
            P("stream", "dp", None),
            P("stream", "dp"),
            P("stream", "dp"),
            P("stream", "dp", None),
            P("stream", "dp"),
            P("stream", "dp"),
            P("stream", "dp"),
            P("stream", "dp", None),
            P("stream", "dp"),
            P("stream", "dp", None),
            P("stream", "dp"),
            P("stream", "dp"),
        ),
        check_vma=False,
    )
```

```python
import functools
import jax
import jax.numpy as jnp
from jax import lax
from jax.experimental import pallas as pl
from jax.experimental.pallas import tpu as pltpu
from jax.sharding import PartitionSpec as P

EPSILON = 1e-05
STRIP = 64
HEADS = 12
BINS = 128
GROUPS = 3
NEGATIVE = -1000000000.0
HIGHEST = lax.Precision.HIGHEST
RING = 8
RING_ORDER = (0, 2, 4, 6, 7, 5, 3, 1)
ROOT_HALF = 0.7071067811865476
DENSITY = 0.3989422804014327


def dot_plain(a, b):
    return lax.dot_general(a, b, (((1,), (0,)), ((), ())), preferred_element_type=jnp.float32)


def dot_across(a, b):
    return lax.dot_general(a, b, (((0,), (0,)), ((), ())), preferred_element_type=jnp.float32)


def dot_back(a, b):
    return lax.dot_general(a, b, (((1,), (1,)), ((), ())), preferred_element_type=jnp.float32)


def row_stats(rows):
    center = rows - jnp.mean(rows, axis=-1, keepdims=True)
    spread = jnp.mean(center * center, axis=-1, keepdims=True)
    rate = lax.rsqrt(spread + EPSILON)
    return center * rate, rate


def fold(rows):
    return jnp.sum(rows.reshape(rows.shape[0] // 8, 8, rows.shape[1]), axis=0)


def strips(count, body):
    for index in range(count // STRIP):
        body(pl.ds(index * STRIP, STRIP))


def place_chunk(target, mine_ref, other_ref, value, rows=slice(None)):
    @pl.when(target < 8)
    def _():
        mine_ref[target, rows, :] = value

    @pl.when(target >= 8)
    def _():
        other_ref[target - 8, rows, :] = value


def put_halves(small_ref, row, vector):
    half = vector.shape[1] // 2
    width = small_ref.shape[2]
    for side in range(2):
        for piece in range(half // width):
            start = side * half + piece * width
            small_ref[side, row + piece : row + piece + 1, :] = vector[:, start : start + width]


def feed_kernel(
    order_ref,
    tokens_ref,
    context_0_ref,
    context_1_ref,
    context_2_ref,
    cot_ref,
    w_out_ref,
    b_out_ref,
    gain_ref,
    shift_ref,
    w_in_ref,
    b_in_ref,
    w_back_ref,
    b_back_ref,
    out_ref,
    d_middle_ref,
    d_branch_ref,
    d_context_ref,
    mine_ref,
    other_ref,
    small_ref,
    middle_ref,
    normed_ref,
    turned_ref,
    pre_ref,
    d_act_ref,
    act_ref,
    d_pre_ref,
    total_ref,
    d_normed_ref,
    sums_ref,
    in_sum_ref,
    stage_ref,
):
    step = pl.program_id(0)
    last = pl.num_programs(0) - 1
    rows = tokens_ref.shape[0]
    block = w_in_ref.shape[1]

    @pl.when(step == 0)
    def _():
        part = context_0_ref.shape[1]
        middle_ref[...] = (
            dot_plain(context_0_ref[...], w_out_ref[:part])
            + dot_plain(context_1_ref[...], w_out_ref[part : 2 * part])
            + dot_plain(context_2_ref[...], w_out_ref[2 * part :])
        )
        sums_ref[...] = jnp.zeros_like(sums_ref)
        small_ref[...] = jnp.zeros_like(small_ref)
        total_ref[...] = jnp.zeros_like(total_ref)
        d_normed_ref[...] = jnp.zeros_like(d_normed_ref)

        def first(at):
            value = middle_ref[at, :] + tokens_ref[at, :].astype(jnp.float32) + b_out_ref[...]
            middle_ref[at, :] = value
            hat, _ = row_stats(value)
            normed_ref[at, :] = (hat * gain_ref[...] + shift_ref[...]).astype(jnp.bfloat16)
            sums_ref[0] += fold(cot_ref[at, :].astype(jnp.float32))

        strips(rows, first)
        turned_ref[...] = normed_ref[...].T

    pre_ref[...] = dot_plain(normed_ref[...], w_in_ref[...])
    d_act_ref[...] = dot_back(cot_ref[...], w_back_ref[...])
    in_sum_ref[...] = jnp.zeros_like(in_sum_ref)

    def middle_part(at):
        value = pre_ref[at, :] + b_in_ref[...]
        chance = 0.5 + 0.5 * lax.erf(value * ROOT_HALF)
        slope = chance + value * (DENSITY * jnp.exp(-0.5 * value * value))
        act_ref[at, :] = (value * chance).astype(jnp.bfloat16)
        d_pre = (d_act_ref[at, :] * slope).astype(jnp.bfloat16)
        d_pre_ref[at, :] = d_pre
        in_sum_ref[...] += fold(d_pre.astype(jnp.float32))

    strips(rows, middle_part)
    total_ref[...] += dot_plain(act_ref[...], w_back_ref[...])
    d_normed_ref[...] += dot_back(d_pre_ref[...], w_in_ref[...])
    per_block = block // 192
    at_rows = pl.ds(pl.multiple_of(192 + step * 48, 16), 48)
    stage_ref[0] = dot_across(act_ref[...], cot_ref[...]).astype(jnp.bfloat16)
    stage_ref[1] = dot_plain(turned_ref[...], d_pre_ref[...]).astype(jnp.bfloat16)

    def place_back(piece, carry):
        value = stage_ref[0, pl.ds(pl.multiple_of(piece * 192, 16), 192), :]
        place_chunk(order_ref[step * per_block + piece], mine_ref, other_ref, value, slice(0, 192))
        return carry

    def place_in(piece, carry):
        value = stage_ref[1, pl.ds(pl.multiple_of(piece * 48, 16), 48), :]
        place_chunk(order_ref[piece], mine_ref, other_ref, value, at_rows)
        return carry

    lax.fori_loop(0, per_block, place_back, 0)
    lax.fori_loop(0, 16, place_in, 0)
    in_sum = jnp.sum(in_sum_ref[...], axis=0, keepdims=True)
    side = step // 2
    row = 8 + 2 * (step % 2)
    small_ref[side, pl.ds(row, 1), :] = in_sum[:, :384]
    small_ref[side, pl.ds(row + 1, 1), :] = in_sum[:, 384:]

    @pl.when(step == last)
    def _():
        def final(at):
            value = middle_ref[at, :]
            out_ref[at, :] = (value + total_ref[at, :] + b_back_ref[...]).astype(jnp.bfloat16)
            hat, rate = row_stats(value)
            d_normed = d_normed_ref[at, :]
            sums_ref[1] += fold(d_normed * hat)
            sums_ref[2] += fold(d_normed)
            scaled = d_normed * gain_ref[...]
            inner = (
                scaled
                - jnp.mean(scaled, axis=-1, keepdims=True)
                - hat * jnp.mean(scaled * hat, axis=-1, keepdims=True)
            )
            d_middle = cot_ref[at, :].astype(jnp.float32) + rate * inner
            d_middle_ref[at, :] = d_middle
            branch = d_middle.astype(jnp.bfloat16)
            d_branch_ref[at, :] = branch
            sums_ref[3] += fold(branch.astype(jnp.float32))

        strips(rows, final)
        d_context_ref[...] = dot_back(d_branch_ref[...], w_out_ref[...]).astype(jnp.bfloat16)
        for index, row in ((0, 7), (1, 5), (2, 6), (3, 4)):
            put_halves(small_ref, row, jnp.sum(sums_ref[index], axis=0, keepdims=True))


def feed_call(order, tokens, contexts, cot, w_out, b_out, gain, shift, w_in, b_in, w_back, b_back):
    rows, width = tokens.shape
    inner = w_in.shape[1]
    block = 768
    fixed = lambda shape: pl.BlockSpec(shape, lambda j, o: (0,) * len(shape), pipeline_mode=pl.Buffered(1))
    wide = lambda dtype: jax.ShapeDtypeStruct((rows, width), dtype)
    ring = jax.ShapeDtypeStruct((RING, 384, width), jnp.bfloat16)
    f32, bf16 = jnp.float32, jnp.bfloat16
    vmem = pltpu.VMEM
    return pl.pallas_call(
        feed_kernel,
        out_shape=(wide(bf16), wide(f32), wide(bf16), wide(bf16), ring, ring,
                   jax.ShapeDtypeStruct((2, 24, 384), f32)),
        grid_spec=pltpu.PrefetchScalarGridSpec(
            num_scalar_prefetch=1,
            grid=(inner // block,),
            in_specs=[
                fixed((rows, width)),
                fixed((rows, width // GROUPS)), fixed((rows, width // GROUPS)), fixed((rows, width // GROUPS)),
                fixed((rows, width)),
                fixed((width, width)), fixed((1, width)), fixed((1, width)), fixed((1, width)),
                pl.BlockSpec((width, block), lambda j, o: (0, j)),
                pl.BlockSpec((1, block), lambda j, o: (0, j)),
                pl.BlockSpec((block, width), lambda j, o: (j, 0)),
                fixed((1, width)),
            ],
            out_specs=[fixed((rows, width))] * 4 + [fixed((RING, 384, width))] * 2 + [fixed((2, 24, 384))],
            scratch_shapes=[
                vmem((rows, width), f32), vmem((rows, width), bf16), vmem((width, rows), bf16),
                vmem((rows, block), f32), vmem((rows, block), f32),
                vmem((rows, block), bf16), vmem((rows, block), bf16),
                vmem((rows, width), f32), vmem((rows, width), f32),
                vmem((4, 8, width), f32), vmem((8, block), f32), vmem((2, width, width), bf16),
            ],
        ),
        compiler_params=pltpu.CompilerParams(vmem_limit_bytes=60 << 20),
        cost_estimate=price(30),
        name="feed",
    )(order, tokens, *contexts, cot, w_out, b_out, gain, shift, w_in, b_in, w_back, b_back)


def first_kernel(tokens_ref, gain_ref, shift_ref, w_ref, bias_ref, normed_ref, *sent_refs):
    rows, width = tokens_ref.shape

    def norm(at):
        hat, _ = row_stats(tokens_ref[at, :].astype(jnp.float32))
        normed_ref[at, :] = (hat * gain_ref[...] + shift_ref[...]).astype(jnp.bfloat16)

    strips(rows, norm)
    part = width // GROUPS
    for group, sent_ref in enumerate(sent_refs):
        at = group * part
        sent_ref[0] = dot_plain(normed_ref[...], w_ref[:, width + at : width + at + part]).astype(jnp.bfloat16)
        sent_ref[1] = (
            dot_plain(normed_ref[...], w_ref[:, 2 * width + at : 2 * width + at + part])
            + bias_ref[:, at : at + part]
        ).astype(jnp.bfloat16)


def whole_specs(count):
    return [pl.BlockSpec(memory_space=pltpu.VMEM)] * count


def price(micros):
    return pl.CostEstimate(flops=int(micros * 1e9), transcendentals=0, bytes_accessed=0)


def kernel_call(kernel, name, micros, outs, *args, scratch=(), smem=0, aliases={}):
    specs = [pl.BlockSpec(memory_space=pltpu.SMEM)] * smem + whole_specs(len(args) - smem)
    return pl.pallas_call(
        kernel,
        out_shape=tuple(outs),
        in_specs=specs,
        out_specs=tuple(whole_specs(len(outs))),
        scratch_shapes=list(scratch),
        input_output_aliases=aliases,
        cost_estimate=price(micros),
        compiler_params=pltpu.CompilerParams(vmem_limit_bytes=60 << 20),
        name=name,
    )(*args)


def first_call(tokens, gain, shift, w_qkv, bias_v):
    rows, width = tokens.shape
    outs = [jax.ShapeDtypeStruct((rows, width), jnp.bfloat16)]
    outs += [jax.ShapeDtypeStruct((2, rows, width // GROUPS), jnp.bfloat16)] * GROUPS
    return kernel_call(first_kernel, "first", 5, outs, tokens, gain, shift, w_qkv, bias_v)


def code_columns(rows_of_codes, rows):
    blank = jnp.zeros((5, rows), jnp.float32)
    return jnp.concatenate([r.astype(jnp.float32) for r in rows_of_codes] + [blank], axis=0).T


def prep_kernel(
    stream_ref, box_ref, segment_ref, mask_ref, normed_ref, w_ref, bias_ref, table_ref,
    queries_ref, hot_ref, turned_hot_ref, key_hot_ref, live_ref, tiles_ref,
):
    rows = normed_ref.shape[0]
    own = stream_ref[0]
    far = 1 - own
    queries_ref[...] = (dot_plain(normed_ref[...], w_ref[:, : normed_ref.shape[1]]) + bias_ref[...]).astype(jnp.bfloat16)
    live_ref[...] = mask_ref[far]
    own_codes = code_columns([box_ref[own, 0], box_ref[own, 1], segment_ref[own]], rows)
    far_codes = code_columns([box_ref[far, 0], box_ref[far, 1], segment_ref[far]], rows)
    levels = lax.broadcasted_iota(jnp.int32, (rows, BINS), 1).astype(jnp.float32)
    for axis in range(3):
        lanes = slice(axis * BINS, axis * BINS + BINS)
        column = own_codes[:, axis : axis + 1]
        hot_ref[:, lanes] = jnp.where(column == levels, 1.0, 0.0).astype(jnp.bfloat16)
        turned_hot_ref[:, lanes] = jnp.where(BINS - 1 - column == levels, 1.0, 0.0).astype(jnp.bfloat16)
        key_hot_ref[:, lanes] = jnp.where(far_codes[:, axis : axis + 1] == levels, 1.0, 0.0).astype(jnp.bfloat16)
    half = BINS // 2
    entry = lax.broadcasted_iota(jnp.int32, (BINS, 2 * BINS), 0)
    gap = lax.broadcasted_iota(jnp.int32, (BINS, 2 * BINS), 1)
    gap = jnp.where(gap < BINS, -gap, 2 * BINS - gap)
    pick = jnp.where(jnp.clip(gap, -half, half - 1) + half == entry, 1.0, 0.0).astype(jnp.bfloat16)
    spread = dot_plain(table_ref[...].astype(jnp.bfloat16), pick)
    for index in range(3 * HEADS):
        wide = jnp.broadcast_to(spread[index : index + 1, :], (BINS, 2 * BINS))
        rolled = pltpu.roll(wide, 0, 1, stride=1, stride_axis=0)
        tiles_ref[index] = rolled[:, :BINS].astype(jnp.bfloat16)


def prep_call(stream, box_bins, segment_ids, key_mask, normed, w_qkv, bias_q, table):
    rows, width = normed.shape
    hot = jax.ShapeDtypeStruct((rows, 3 * BINS), jnp.bfloat16)
    outs = [
        jax.ShapeDtypeStruct((rows, width), jnp.bfloat16), hot, hot, hot,
        jax.ShapeDtypeStruct((1, rows), jnp.int32),
        jax.ShapeDtypeStruct((3 * HEADS, BINS, BINS), jnp.bfloat16),
    ]
    return kernel_call(prep_kernel, "prep", 5, outs, stream, box_bins, segment_ids, key_mask, normed, w_qkv, bias_q, table, smem=1)


def half_of(slab, odd):
    lane = lax.broadcasted_iota(jnp.int32, slab.shape, 1)
    keep = (lane >= 64) if odd else (lane < 64)
    return jnp.where(keep, slab, jnp.zeros_like(slab))


def attend_kernel(group, queries_ref, pair_ref, hot_ref, key_hot_ref, live_ref, tiles_ref,
                  context_ref, probs_ref, left_ref, right_ref, scores_ref):
    rows = queries_ref.shape[0]
    part = pair_ref.shape[2]
    def slab_step(slab, carry):
        lanes = pl.ds(pl.multiple_of(slab * 128, 128), 128)
        wide = pl.ds(pl.multiple_of(group * part + slab * 128, 128), 128)
        right_ref[slab, :, :128] = pair_ref[0, :, lanes]
        right_ref[slab, :, 128:] = key_hot_ref[...]
        halves = []
        for odd in range(2):
            head = slab * 2 + odd
            left_ref[head, :, :128] = half_of(queries_ref[:, wide].astype(jnp.float32) * 0.125, odd).astype(jnp.bfloat16)
            for axis in range(3):
                cut = slice(axis * BINS, axis * BINS + BINS)
                tile = tiles_ref[axis * HEADS + group * (part // 64) + head]
                left_ref[head, :, 128 + axis * BINS : 256 + axis * BINS] = dot_plain(hot_ref[:, cut], tile).astype(jnp.bfloat16)
            scores_ref[head] = dot_back(left_ref[head], right_ref[slab])

            def soft(at):
                scores = jnp.where(live_ref[...] > 0, scores_ref[head, at, :], NEGATIVE)
                top = jnp.max(scores, axis=-1, keepdims=True)
                weights = jnp.exp(scores - top)
                rate = 1.0 / jnp.sum(weights, axis=-1, keepdims=True)
                probs_ref[head, at, :] = (weights * rate).astype(jnp.bfloat16)

            strips(rows, soft)
            halves.append(half_of(dot_plain(probs_ref[head], pair_ref[1, :, lanes]), odd))
        context_ref[:, lanes] = (halves[0] + halves[1]).astype(jnp.bfloat16)
        return carry

    lax.fori_loop(0, part // 128, slab_step, 0)


def attend_call(group, queries, pair, hot, key_hot, live, tiles):
    rows = queries.shape[0]
    part = pair.shape[2]
    heads = part // 64
    outs = [
        jax.ShapeDtypeStruct((rows, part), jnp.bfloat16),
        jax.ShapeDtypeStruct((heads, rows, rows), jnp.bfloat16),
    ]
    scratch = [
        pltpu.VMEM((heads, rows, 512), jnp.bfloat16),
        pltpu.VMEM((part // 128, rows, 512), jnp.bfloat16),
        pltpu.VMEM((heads, rows, rows), jnp.float32),
    ]
    return kernel_call(functools.partial(attend_kernel, group), f"attend_{group}", 7, outs,
                       queries, pair, hot, key_hot, live, tiles, scratch=scratch)


def attend_back_kernel(group, queries_ref, pair_ref, turned_hot_ref, key_hot_ref, probs_ref, d_context_ref,
                       d_queries_ref, d_pair_ref, diagonal_ref, right_ref, slope_ref, d_scores_ref):
    rows = queries_ref.shape[0]
    part = pair_ref.shape[2]
    def slab_step(slab, carry):
        lanes = pl.ds(pl.multiple_of(slab * 128, 128), 128)
        wide = pl.ds(pl.multiple_of(group * part + slab * 128, 128), 128)
        right_ref[slab, :, :128] = pair_ref[0, :, lanes]
        right_ref[slab, :, 128:] = key_hot_ref[...]
        d_query = d_key = d_value = 0.0
        for odd in range(2):
            head = slab * 2 + odd
            query = half_of(queries_ref[:, wide], odd)
            d_context = half_of(d_context_ref[:, wide], odd)
            slope_ref[head] = dot_back(d_context, pair_ref[1, :, lanes])

            def soft(at):
                probs = probs_ref[head, at, :].astype(jnp.float32)
                slope = slope_ref[head, at, :]
                centre = jnp.sum(probs * slope, axis=-1, keepdims=True)
                d_scores_ref[head, at, :] = (probs * (slope - centre)).astype(jnp.bfloat16)

            strips(rows, soft)
            d_value = d_value + dot_across(probs_ref[head], d_context)
            d_key = d_key + dot_across(d_scores_ref[head], query)
            both = dot_plain(d_scores_ref[head], right_ref[slab])
            d_query = d_query + half_of(both[:, :128], odd)
            spread = both[:, 128:].astype(jnp.bfloat16)
            for axis in range(3):
                cut = slice(axis * BINS, axis * BINS + BINS)
                tile = dot_across(turned_hot_ref[:, cut], spread[:, cut])
                padded = jnp.concatenate([tile, jnp.zeros_like(tile)], axis=1)
                rolled = pltpu.roll(padded, 0, 1, stride=1, stride_axis=0)
                diagonal_ref[axis, pl.ds(head, 1), :] = jnp.sum(rolled, axis=0, keepdims=True)
        d_queries_ref[:, lanes] = (d_query * 0.125).astype(jnp.bfloat16)
        d_pair_ref[0, :, lanes] = (d_key * 0.125).astype(jnp.bfloat16)
        d_pair_ref[1, :, lanes] = d_value.astype(jnp.bfloat16)
        return carry

    lax.fori_loop(0, part // 128, slab_step, 0)


def attend_back_call(group, queries, pair, turned_hot, key_hot, probs, d_context):
    rows = queries.shape[0]
    part = pair.shape[2]
    heads = part // 64
    outs = [
        jax.ShapeDtypeStruct((rows, part), jnp.bfloat16),
        jax.ShapeDtypeStruct((2, rows, part), jnp.bfloat16),
        jax.ShapeDtypeStruct((3, heads, 2 * BINS), jnp.float32),
    ]
    scratch = [
        pltpu.VMEM((part // 128, rows, 512), jnp.bfloat16),
        pltpu.VMEM((heads, rows, rows), jnp.float32),
        pltpu.VMEM((heads, rows, rows), jnp.bfloat16),
    ]
    return kernel_call(functools.partial(attend_back_kernel, group), f"attend_back_{group}", 8, outs,
                       queries, pair, turned_hot, key_hot, probs, d_context, scratch=scratch)


def weights_kernel(
    order_ref, normed_ref, d_branch_ref, context_0_ref, context_1_ref, context_2_ref,
    d_query_0_ref, d_query_1_ref, d_query_2_ref, back_0_ref, back_1_ref, back_2_ref,
    mine_ref, other_ref, joined_ref, left_ref,
):
    part = context_0_ref.shape[1]
    queries = (d_query_0_ref, d_query_1_ref, d_query_2_ref)
    backs = (back_0_ref, back_1_ref, back_2_ref)
    contexts = (context_0_ref, context_1_ref, context_2_ref)
    for group in range(GROUPS):
        lanes = slice(group * part, group * part + part)
        joined_ref[0, :, lanes] = queries[group][...]
        joined_ref[1, :, lanes] = backs[group][0]
        joined_ref[2, :, lanes] = backs[group][1]
        joined_ref[3, :, lanes] = contexts[group][...]
    left_ref[0] = normed_ref[...]
    left_ref[1] = joined_ref[3]
    joined_ref[3] = d_branch_ref[...]

    def block_step(block, carry):
        value = dot_across(left_ref[block // 3], joined_ref[block]).astype(jnp.bfloat16)
        rows = pl.ds(pl.multiple_of(block * 48, 16), 48)
        for piece in range(16):
            place_chunk(order_ref[piece], mine_ref, other_ref, value[piece * 48 : piece * 48 + 48], rows)
        return carry

    lax.fori_loop(0, 4, block_step, 0)


def weights_call(order, normed, d_branch, contexts, d_queries, backs):
    rows, width = normed.shape
    ring = jax.ShapeDtypeStruct((RING, 192, width), jnp.bfloat16)
    scratch = [pltpu.VMEM((4, rows, width), jnp.bfloat16), pltpu.VMEM((2, rows, width), jnp.bfloat16)]
    return kernel_call(weights_kernel, "weights", 7, [ring, ring], order, normed, d_branch,
                       *contexts, *d_queries, *backs, scratch=scratch, smem=1)


def last_kernel(
    side_ref, tokens_ref, gain_ref, w_ref, d_middle_ref, d_query_0_ref, d_query_1_ref, d_query_2_ref,
    back_0_ref, back_1_ref, back_2_ref, diagonal_0_ref, diagonal_1_ref, diagonal_2_ref, start_ref,
    g_tokens_ref, mine_ref, other_ref, small_ref, d_normed_ref, sums_ref,
):
    rows, width = tokens_ref.shape
    part = width // GROUPS
    queries = (d_query_0_ref, d_query_1_ref, d_query_2_ref)
    backs = (back_0_ref, back_1_ref, back_2_ref)
    small_ref[...] = start_ref[...]
    sums_ref[...] = jnp.zeros_like(sums_ref)
    total = 0.0
    for group in range(GROUPS):
        at = group * part
        total = total + dot_back(queries[group][...], w_ref[:, at : at + part])
        total = total + dot_back(backs[group][0], w_ref[:, width + at : width + at + part])
        total = total + dot_back(backs[group][1], w_ref[:, 2 * width + at : 2 * width + at + part])
    d_normed_ref[...] = total

    def final(at):
        hat, rate = row_stats(tokens_ref[at, :].astype(jnp.float32))
        d_normed = d_normed_ref[at, :]
        sums_ref[0] += fold(d_normed * hat)
        sums_ref[1] += fold(d_normed)
        for group in range(GROUPS):
            lanes = slice(group * part, group * part + part)
            sums_ref[2, :, lanes] += fold(queries[group][at, :].astype(jnp.float32))
            sums_ref[3, :, lanes] += fold(backs[group][1, at, :].astype(jnp.float32))
        scaled = d_normed * gain_ref[...]
        inner = (
            scaled
            - jnp.mean(scaled, axis=-1, keepdims=True)
            - hat * jnp.mean(scaled * hat, axis=-1, keepdims=True)
        )
        g_tokens_ref[at, :] = (d_middle_ref[at, :] + rate * inner).astype(jnp.bfloat16)

    strips(rows, final)
    for row in range(4):
        put_halves(small_ref, row, jnp.sum(sums_ref[row], axis=0, keepdims=True))
    half = BINS // 2
    gap = BINS - 1 - lax.broadcasted_iota(jnp.int32, (2 * BINS, BINS), 0)
    entry = lax.broadcasted_iota(jnp.int32, (2 * BINS, BINS), 1)
    pick = jnp.where(jnp.clip(gap, -half, half - 1) + half == entry, 1.0, 0.0)
    for group, diagonal_ref in enumerate((diagonal_0_ref, diagonal_1_ref, diagonal_2_ref)):
        for axis in range(3):
            table = lax.dot_general(
                diagonal_ref[axis], pick, (((1,), (0,)), ((), ())),
                precision=HIGHEST, preferred_element_type=jnp.float32,
            )
            for head in range(part // 64):
                index = axis * HEADS + group * (part // 64) + head
                side, place = divmod(index, 18)
                row, lane = divmod(place, 3)
                small_ref[side, 12 + row : 13 + row, lane * BINS : lane * BINS + BINS] = table[head : head + 1, :]
    for out_ref, side in ((mine_ref, side_ref[0]), (other_ref, 1 - side_ref[0])):
        out_ref[...] = jnp.zeros_like(out_ref)
        out_ref[:12, :384] = small_ref[side, :12, :]
        out_ref[:12, 384:] = small_ref[side, 12:, :]


def last_call(side, tokens, gain, w_qkv, d_middle, d_queries, backs, diagonals, start):
    rows, width = tokens.shape
    packed = jax.ShapeDtypeStruct((16, width), jnp.float32)
    outs = [jax.ShapeDtypeStruct((rows, width), jnp.bfloat16), packed, packed]
    scratch = [pltpu.VMEM(start.shape, jnp.float32), pltpu.VMEM((rows, width), jnp.float32), pltpu.VMEM((4, 8, width), jnp.float32)]
    return kernel_call(last_kernel, "last", 8, outs, side, tokens, gain, w_qkv, d_middle,
                       *d_queries, *backs, *diagonals, start, scratch=scratch, smem=1)


def open_kernel(layout, place_ref, *refs):
    width = refs[0].shape[1]
    for out_ref, (start, blocks) in zip(refs[RING:], layout):
        size = out_ref.shape[0] // RING
        for index in range(RING):
            to = pl.ds(pl.multiple_of(place_ref[index] * size, size), size)
            for block in range(blocks):
                at = start + block * size
                out_ref[to, block * width : block * width + width] = refs[index][at : at + size, :].astype(jnp.float32)


def open_rest_kernel(place_ref, *refs):
    chunks, outs, parts_ref = refs[:RING], refs[RING:-1], refs[-1]
    open_kernel(((0, 3), (144, 1)), place_ref, *chunks, outs[0], outs[1])
    for index in range(RING):
        parts_ref[place_ref[index]] = chunks[index][192:, :].astype(jnp.float32)
    total = parts_ref[0]
    for index in range(1, RING):
        total = total + parts_ref[index]
    parts_ref[0] = total
    for row in range(8):
        outs[2 + row][...] = parts_ref[0, row : row + 1, :384]
    for row in range(4):
        outs[10][:, row * 384 : row * 384 + 384] = parts_ref[0, 8 + row : 9 + row, :384]
    for row in range(6):
        outs[11][:, row * 384 : row * 384 + 384] = parts_ref[0, row : row + 1, 384:]


def open_call(name, places, chunks):
    width = chunks[0].shape[1]
    half = width // 2
    if name == "rest":
        shapes = [(half, 3 * width), (half, width)] + [(1, half)] * 8 + [(1, 2 * width), (1, 3 * width)]
        kernel, scratch = open_rest_kernel, [pltpu.VMEM((RING, 16, width), jnp.float32)]
    else:
        shapes = [(2 * width, width)] if name == "back" else [(half, 4 * width)]
        kernel, scratch = functools.partial(open_kernel, ((0, shapes[0][1] // width),)), []
    outs = [jax.ShapeDtypeStruct(shape, jnp.float32) for shape in shapes]
    return kernel_call(kernel, f"open_{name}", 4, outs, places, *chunks, smem=1, scratch=scratch)


def partner_2(shard, axis, distance):
    return lax.ppermute(shard, axis, [(i, i ^ 1 << distance) for i in range(lax.axis_size(axis))])


def ring_send(chunk):
    pairs = []
    for place in range(RING):
        ahead = RING_ORDER[(place + 1) % RING]
        behind = RING_ORDER[(place - 1) % RING]
        pairs.append((RING_ORDER[place] * 2, ahead * 2))
        pairs.append((RING_ORDER[place] * 2 + 1, behind * 2 + 1))
    return lax.ppermute(chunk, ("group", "dp"), pairs)


def ring_place():
    group = lax.axis_index("group")
    place = jnp.int32(0)
    for position, member in enumerate(RING_ORDER):
        place = jnp.where(group == member, position, place)
    return place


def ring_plan(ringed):
    index = lax.iota(jnp.int32, 2 * RING)
    steps = lax.iota(jnp.int32, RING)
    if not ringed:
        return index, steps
    dp = lax.axis_index("dp")
    place = ring_place()
    side = index // RING
    start = jnp.where(side == 0, place, RING - place)
    order = (start - index % RING + RING) % RING + jnp.where(side == dp, 0, RING)
    start = jnp.where(dp == 0, place, RING - place)
    return order, (start + 1 - steps + RING) % RING


def add_low(*terms):
    return sum(term.astype(jnp.float32) for term in terms).astype(jnp.bfloat16)


def unringed_total(mine, other):
    return lax.psum(jnp.concatenate([mine, other]).astype(jnp.float32), ("group", "dp"))


def unringed_rows(packed):
    blocks = packed.shape[1] // 48
    rows = packed.reshape(2 * RING, blocks, 48, packed.shape[2])
    return jnp.swapaxes(rows, 1, 2).reshape(2 * RING * 48, blocks * packed.shape[2])


def own_share(whole):
    share = whole.shape[0] // lax.axis_size("dp")
    return lax.dynamic_slice_in_dim(whole, lax.axis_index("dp") * share, share, 0)[None]


def unringed_grads(feed, rest, small):
    feed = unringed_total(*feed)
    rest = unringed_total(*rest)
    small = lax.psum(jnp.stack(small)[:, :12], ("group", "dp"))
    small = jnp.concatenate([small[:, :, :384], small[:, :, 384:]], axis=1)
    vectors = [small[:, row].reshape(-1) for row in range(8)]
    vectors += [small[:, 8:12].reshape(-1), small[:, 12:18].reshape(-1)]
    weights = (
        feed[:, :192].reshape(-1, feed.shape[2]),
        unringed_rows(feed[:, 192:]),
        unringed_rows(rest[:, :144]),
        unringed_rows(rest[:, 144:]),
    )
    return [own_share(weight) for weight in weights], [own_share(vector) for vector in vectors]


LAST_STEP = 3
LAST_SPAN = 1


class Ordered:
    def __init__(self):
        self.mark = None
        self.free = False

    def after(self, value):
        if self.mark is None or self.free:
            return value
        return lax.optimization_barrier((value, self.mark))[0]

    def wait(self, *values):
        self.mark = (self.mark, *values)


class Ring:
    def __init__(self, order, mine, other):
        self.order, self.mine = order, mine
        self.met = lax.ppermute(order.after(other), "dp", [(0, 1), (1, 0)])
        self.arrived, self.step = None, 0

    def reduce(self):
        step, order = self.step, self.order
        if step == 0:
            held = add_low(self.mine[0], order.after(self.met)[0])
        else:
            held = add_low(order.after(self.arrived), self.mine[step], self.met[step])
        order.mark = held
        if step < RING - 1:
            self.arrived = ring_send(held)
        self.step += 1
        return held

    def split(self, cuts):
        pieces = []
        for start, stop in zip(cuts, cuts[1:]):
            piece = Ring.__new__(Ring)
            piece.order, piece.step = self.order, self.step
            piece.mine, piece.met = self.mine[:, start:stop], self.met[:, start:stop]
            piece.arrived = None if self.arrived is None else self.arrived[start:stop]
            pieces.append(piece)
        return pieces


def gather(held, waits={}):
    chunks = [held]
    for step in range(1, RING):
        held = ring_send(held)
        if step in waits:
            held = waits[step](held)
        chunks.append(held)
    return chunks


def on_device(
    tokens, cotangent, box_bins, segment_ids, key_mask, ln1_gain, ln1_bias, w_qkv, bias_q, bias_v,
    w_out, bias_out, ln2_gain, ln2_bias, w_in, bias_in, w_back, bias_back, rel_table,
):
    ringed = lax.axis_size("group") == RING and lax.axis_size("dp") == 2
    width = tokens.shape[2]
    order, places = ring_plan(ringed)
    queue = Ordered()
    stream = lax.axis_index("stream").reshape(1)
    normed, *sent = first_call(tokens[0], ln1_gain, ln1_bias, w_qkv[0], bias_v)
    pairs = [partner_2(pair, "stream", 0) for pair in sent]
    queries, hot, turned_hot, key_hot, live, tiles = prep_call(
        stream, box_bins, segment_ids, key_mask, normed, w_qkv[0], bias_q, rel_table.reshape(3 * HEADS, BINS)
    )
    contexts, probs = [], []
    for group in range(GROUPS):
        context, prob = attend_call(group, queries, queue.after(pairs[group]), hot, key_hot, live, tiles)
        queue.mark = context
        contexts.append(context)
        probs.append(prob)
    output, d_middle, d_branch, d_context, feed_mine, feed_other, small = feed_call(
        order, tokens[0], contexts, cotangent[0], w_out[0], bias_out, ln2_gain, ln2_bias,
        w_in[0], bias_in, w_back[0], bias_back,
    )
    if ringed:
        feed = Ring(queue, feed_mine, feed_other)
    d_queries, backs, diagonals = [None] * GROUPS, [None] * GROUPS, [None] * GROUPS
    for group in range(GROUPS):
        d_queries[group], d_pair, diagonals[group] = attend_back_call(
            group, queries, pairs[group], turned_hot, key_hot, probs[group], queue.after(d_context)
        )
        queue.mark = d_queries[group]
        if ringed:
            if group == GROUPS - 1:
                feed.reduce()
                d_pair = queue.after(d_pair)
            backs[group] = partner_2(d_pair, "stream", 0)
            if group < GROUPS - 1:
                feed.reduce()
            if group:
                queue.wait(backs[group - 1])
        else:
            backs[group] = partner_2(d_pair, "stream", 0)
    rest_mine, rest_other = weights_call(order, queue.after(normed), d_branch, contexts, d_queries, backs)
    if ringed:
        queue.mark = rest_mine
        feed.reduce()
        rest = Ring(queue, rest_mine, rest_other)
    side = lax.axis_index("dp").reshape(1)
    if not ringed:
        g_tokens, *small = last_call(
            jnp.zeros_like(side), tokens[0], ln1_gain, w_qkv[0], d_middle, d_queries, backs, diagonals, small
        )
    if ringed:
        rest.reduce()
        queue.free = True
        held_parts = []
        for piece in feed.split((0, 192, 384)):
            while piece.step < RING:
                held = piece.reduce()
            held_parts.append(held)
        back_chunks = gather(held_parts[0])
        in_chunks = gather(held_parts[1])
        g_w_back = open_call("back", places, back_chunks)
        g_w_in = open_call("inward", places, in_chunks)
        opened = [*g_w_back, *g_w_in]

        def back_turn(value):
            value, opened[0] = lax.optimization_barrier((value, opened[0]))
            return value

        def in_turn(value):
            value, opened[1] = lax.optimization_barrier((value, opened[1]))
            return value

        while rest.step < RING:
            if rest.step == LAST_STEP + LAST_SPAN:
                rest.arrived, g_tokens = lax.optimization_barrier((rest.arrived, g_tokens))
            rest_held = rest.reduce()
            if rest.step == LAST_STEP:
                ready = lax.optimization_barrier((d_middle, rest_held))[0]
                g_tokens, *small = last_call(
                    side, tokens[0], ln1_gain, w_qkv[0], ready, d_queries, backs, diagonals, small
                )
        small_held = add_low(small[0], lax.ppermute(small[1], "dp", [(0, 1), (1, 0)]))
        rest_held = jnp.concatenate([rest_held, small_held], axis=0)
        rest_chunks = gather(rest_held, {6: back_turn, 7: in_turn})
        opened += open_call("rest", places, rest_chunks)
        weights = [value[None] for value in opened[:4]]
        vectors = opened[4:]
    else:
        weights, vectors = unringed_grads(
            (feed_mine, feed_other), (rest_mine, rest_other), small
        )
    g_w_back, g_w_in, g_w_qkv, g_w_out = weights
    (
        g_ln1_gain, g_ln1_bias, g_bias_q, g_bias_v, g_bias_out, g_ln2_gain, g_ln2_bias, g_bias_back, g_bias_in, g_rel_table,
    ) = vectors
    return (
        output[None], g_tokens[None], g_ln1_gain, g_ln1_bias, g_w_qkv, g_bias_q, g_bias_v, g_w_out,
        g_bias_out, g_ln2_gain, g_ln2_bias, g_w_in, g_bias_in, g_w_back, g_bias_back, g_rel_table,
    )


def solution(mesh):
    placed = (
        P("stream", ("group", "dp"), None),
        P("stream", ("group", "dp"), None),
        P(None, None, ("group", "dp"), None),
        P(None, ("group", "dp"), None),
        P(None, ("group", "dp"), None),
        P("stream", None),
        P("stream", None),
        P("stream", None, None),
        P("stream", None),
        P("stream", None),
        P("stream", None, None),
        P("stream", None),
        P("stream", None),
        P("stream", None),
        P("stream", None, None),
        P("stream", None),
        P("stream", None, None),
        P("stream", None),
        P("stream", None),
    )
    return jax.shard_map(
        on_device,
        mesh=mesh,
        in_specs=placed,
        out_specs=(
            P("stream", ("group", "dp"), None),
            P("stream", ("group", "dp"), None),
            P("stream", "dp"),
            P("stream", "dp"),
            P("stream", "dp", None),
            P("stream", "dp"),
            P("stream", "dp"),
            P("stream", "dp", None),
            P("stream", "dp"),
            P("stream", "dp"),
            P("stream", "dp"),
            P("stream", "dp", None),
            P("stream", "dp"),
            P("stream", "dp", None),
            P("stream", "dp"),
            P("stream", "dp"),
        ),
        check_vma=False,
    )
```

```python
import functools
import jax
import jax.numpy as jnp
from jax import lax
from jax.experimental import pallas as pl
from jax.experimental.pallas import tpu as pltpu
from jax.sharding import PartitionSpec as P

EPSILON = 1e-05
STRIP = 64
HEADS = 12
BINS = 128
GROUPS = 3
NEGATIVE = -1000000000.0
HIGHEST = lax.Precision.HIGHEST
RING = 8
RING_ORDER = (0, 2, 4, 6, 7, 5, 3, 1)
ROOT_HALF = 0.7071067811865476
DENSITY = 0.3989422804014327


def dot_plain(a, b):
    return lax.dot_general(a, b, (((1,), (0,)), ((), ())), preferred_element_type=jnp.float32)


def dot_across(a, b):
    return lax.dot_general(a, b, (((0,), (0,)), ((), ())), preferred_element_type=jnp.float32)


def dot_back(a, b):
    return lax.dot_general(a, b, (((1,), (1,)), ((), ())), preferred_element_type=jnp.float32)


def row_stats(rows):
    center = rows - jnp.mean(rows, axis=-1, keepdims=True)
    spread = jnp.mean(center * center, axis=-1, keepdims=True)
    rate = lax.rsqrt(spread + EPSILON)
    return center * rate, rate


def fold(rows):
    return jnp.sum(rows.reshape(rows.shape[0] // 8, 8, rows.shape[1]), axis=0)


def strips(count, body):
    for index in range(count // STRIP):
        body(pl.ds(index * STRIP, STRIP))


def place_chunk(target, mine_ref, other_ref, value, rows=slice(None)):
    @pl.when(target < 8)
    def _():
        mine_ref[target, rows, :] = value

    @pl.when(target >= 8)
    def _():
        other_ref[target - 8, rows, :] = value


def put_halves(small_ref, row, vector):
    half = vector.shape[1] // 2
    width = small_ref.shape[2]
    for side in range(2):
        for piece in range(half // width):
            start = side * half + piece * width
            small_ref[side, row + piece : row + piece + 1, :] = vector[:, start : start + width]


def feed_kernel(
    order_ref,
    tokens_ref,
    context_0_ref,
    context_1_ref,
    context_2_ref,
    cot_ref,
    w_out_ref,
    b_out_ref,
    gain_ref,
    shift_ref,
    w_in_ref,
    b_in_ref,
    w_back_ref,
    b_back_ref,
    out_ref,
    d_middle_ref,
    d_branch_ref,
    d_context_ref,
    mine_ref,
    other_ref,
    small_ref,
    middle_ref,
    normed_ref,
    turned_ref,
    pre_ref,
    d_act_ref,
    act_ref,
    d_pre_ref,
    total_ref,
    d_normed_ref,
    sums_ref,
    in_sum_ref,
    stage_ref,
):
    step = pl.program_id(0)
    last = pl.num_programs(0) - 1
    rows = tokens_ref.shape[0]
    block = w_in_ref.shape[1]

    @pl.when(step == 0)
    def _():
        part = context_0_ref.shape[1]
        middle_ref[...] = (
            dot_plain(context_0_ref[...], w_out_ref[:part])
            + dot_plain(context_1_ref[...], w_out_ref[part : 2 * part])
            + dot_plain(context_2_ref[...], w_out_ref[2 * part :])
        )
        sums_ref[...] = jnp.zeros_like(sums_ref)
        small_ref[...] = jnp.zeros_like(small_ref)
        total_ref[...] = jnp.zeros_like(total_ref)
        d_normed_ref[...] = jnp.zeros_like(d_normed_ref)

        def first(at):
            value = middle_ref[at, :] + tokens_ref[at, :].astype(jnp.float32) + b_out_ref[...]
            middle_ref[at, :] = value
            hat, _ = row_stats(value)
            normed_ref[at, :] = (hat * gain_ref[...] + shift_ref[...]).astype(jnp.bfloat16)
            sums_ref[0] += fold(cot_ref[at, :].astype(jnp.float32))

        strips(rows, first)
        turned_ref[...] = normed_ref[...].T

    pre_ref[...] = dot_plain(normed_ref[...], w_in_ref[...])
    d_act_ref[...] = dot_back(cot_ref[...], w_back_ref[...])
    in_sum_ref[...] = jnp.zeros_like(in_sum_ref)

    def middle_part(at):
        value = pre_ref[at, :] + b_in_ref[...]
        chance = 0.5 + 0.5 * lax.erf(value * ROOT_HALF)
        slope = chance + value * (DENSITY * jnp.exp(-0.5 * value * value))
        act_ref[at, :] = (value * chance).astype(jnp.bfloat16)
        d_pre = (d_act_ref[at, :] * slope).astype(jnp.bfloat16)
        d_pre_ref[at, :] = d_pre
        in_sum_ref[...] += fold(d_pre.astype(jnp.float32))

    strips(rows, middle_part)
    total_ref[...] += dot_plain(act_ref[...], w_back_ref[...])
    d_normed_ref[...] += dot_back(d_pre_ref[...], w_in_ref[...])
    per_block = block // 192
    at_rows = pl.ds(pl.multiple_of(192 + step * 48, 16), 48)
    stage_ref[0] = dot_across(act_ref[...], cot_ref[...]).astype(jnp.bfloat16)
    stage_ref[1] = dot_plain(turned_ref[...], d_pre_ref[...]).astype(jnp.bfloat16)

    def place_back(piece, carry):
        value = stage_ref[0, pl.ds(pl.multiple_of(piece * 192, 16), 192), :]
        place_chunk(order_ref[step * per_block + piece], mine_ref, other_ref, value, slice(0, 192))
        return carry

    def place_in(piece, carry):
        value = stage_ref[1, pl.ds(pl.multiple_of(piece * 48, 16), 48), :]
        place_chunk(order_ref[piece], mine_ref, other_ref, value, at_rows)
        return carry

    lax.fori_loop(0, per_block, place_back, 0)
    lax.fori_loop(0, 16, place_in, 0)
    in_sum = jnp.sum(in_sum_ref[...], axis=0, keepdims=True)
    side = step // 2
    row = 8 + 2 * (step % 2)
    small_ref[side, pl.ds(row, 1), :] = in_sum[:, :384]
    small_ref[side, pl.ds(row + 1, 1), :] = in_sum[:, 384:]

    @pl.when(step == last)
    def _():
        def final(at):
            value = middle_ref[at, :]
            out_ref[at, :] = (value + total_ref[at, :] + b_back_ref[...]).astype(jnp.bfloat16)
            hat, rate = row_stats(value)
            d_normed = d_normed_ref[at, :]
            sums_ref[1] += fold(d_normed * hat)
            sums_ref[2] += fold(d_normed)
            scaled = d_normed * gain_ref[...]
            inner = (
                scaled
                - jnp.mean(scaled, axis=-1, keepdims=True)
                - hat * jnp.mean(scaled * hat, axis=-1, keepdims=True)
            )
            d_middle = cot_ref[at, :].astype(jnp.float32) + rate * inner
            d_middle_ref[at, :] = d_middle
            branch = d_middle.astype(jnp.bfloat16)
            d_branch_ref[at, :] = branch
            sums_ref[3] += fold(branch.astype(jnp.float32))

        strips(rows, final)
        d_context_ref[...] = dot_back(d_branch_ref[...], w_out_ref[...]).astype(jnp.bfloat16)
        for index, row in ((0, 7), (1, 5), (2, 6), (3, 4)):
            put_halves(small_ref, row, jnp.sum(sums_ref[index], axis=0, keepdims=True))


def feed_call(order, tokens, contexts, cot, w_out, b_out, gain, shift, w_in, b_in, w_back, b_back):
    rows, width = tokens.shape
    inner = w_in.shape[1]
    block = 768
    fixed = lambda shape: pl.BlockSpec(shape, lambda j, o: (0,) * len(shape), pipeline_mode=pl.Buffered(1))
    wide = lambda dtype: jax.ShapeDtypeStruct((rows, width), dtype)
    ring = jax.ShapeDtypeStruct((RING, 384, width), jnp.bfloat16)
    f32, bf16 = jnp.float32, jnp.bfloat16
    vmem = pltpu.VMEM
    return pl.pallas_call(
        feed_kernel,
        out_shape=(wide(bf16), wide(f32), wide(bf16), wide(bf16), ring, ring,
                   jax.ShapeDtypeStruct((2, 24, 384), f32)),
        grid_spec=pltpu.PrefetchScalarGridSpec(
            num_scalar_prefetch=1,
            grid=(inner // block,),
            in_specs=[
                fixed((rows, width)),
                fixed((rows, width // GROUPS)), fixed((rows, width // GROUPS)), fixed((rows, width // GROUPS)),
                fixed((rows, width)),
                fixed((width, width)), fixed((1, width)), fixed((1, width)), fixed((1, width)),
                pl.BlockSpec((width, block), lambda j, o: (0, j)),
                pl.BlockSpec((1, block), lambda j, o: (0, j)),
                pl.BlockSpec((block, width), lambda j, o: (j, 0)),
                fixed((1, width)),
            ],
            out_specs=[fixed((rows, width))] * 4 + [fixed((RING, 384, width))] * 2 + [fixed((2, 24, 384))],
            scratch_shapes=[
                vmem((rows, width), f32), vmem((rows, width), bf16), vmem((width, rows), bf16),
                vmem((rows, block), f32), vmem((rows, block), f32),
                vmem((rows, block), bf16), vmem((rows, block), bf16),
                vmem((rows, width), f32), vmem((rows, width), f32),
                vmem((4, 8, width), f32), vmem((8, block), f32), vmem((2, width, width), bf16),
            ],
        ),
        compiler_params=pltpu.CompilerParams(vmem_limit_bytes=60 << 20),
        cost_estimate=price(30),
        name="feed",
    )(order, tokens, *contexts, cot, w_out, b_out, gain, shift, w_in, b_in, w_back, b_back)


def first_kernel(tokens_ref, gain_ref, shift_ref, w_ref, bias_ref, normed_ref, *sent_refs):
    rows, width = tokens_ref.shape

    def norm(at):
        hat, _ = row_stats(tokens_ref[at, :].astype(jnp.float32))
        normed_ref[at, :] = (hat * gain_ref[...] + shift_ref[...]).astype(jnp.bfloat16)

    strips(rows, norm)
    part = width // GROUPS
    for group, sent_ref in enumerate(sent_refs):
        at = group * part
        sent_ref[0] = dot_plain(normed_ref[...], w_ref[:, width + at : width + at + part]).astype(jnp.bfloat16)
        sent_ref[1] = (
            dot_plain(normed_ref[...], w_ref[:, 2 * width + at : 2 * width + at + part])
            + bias_ref[:, at : at + part]
        ).astype(jnp.bfloat16)


def whole_specs(count):
    return [pl.BlockSpec(memory_space=pltpu.VMEM)] * count


def price(micros):
    return pl.CostEstimate(flops=int(micros * 1e9), transcendentals=0, bytes_accessed=0)


def kernel_call(kernel, name, micros, outs, *args, scratch=(), smem=0, aliases={}):
    specs = [pl.BlockSpec(memory_space=pltpu.SMEM)] * smem + whole_specs(len(args) - smem)
    return pl.pallas_call(
        kernel,
        out_shape=tuple(outs),
        in_specs=specs,
        out_specs=tuple(whole_specs(len(outs))),
        scratch_shapes=list(scratch),
        input_output_aliases=aliases,
        cost_estimate=price(micros),
        compiler_params=pltpu.CompilerParams(vmem_limit_bytes=60 << 20),
        name=name,
    )(*args)


def first_call(tokens, gain, shift, w_qkv, bias_v):
    rows, width = tokens.shape
    outs = [jax.ShapeDtypeStruct((rows, width), jnp.bfloat16)]
    outs += [jax.ShapeDtypeStruct((2, rows, width // GROUPS), jnp.bfloat16)] * GROUPS
    return kernel_call(first_kernel, "first", 5, outs, tokens, gain, shift, w_qkv, bias_v)


def code_columns(rows_of_codes, rows):
    blank = jnp.zeros((5, rows), jnp.float32)
    return jnp.concatenate([r.astype(jnp.float32) for r in rows_of_codes] + [blank], axis=0).T


def prep_kernel(
    stream_ref, box_ref, segment_ref, mask_ref, normed_ref, w_ref, bias_ref, table_ref,
    queries_ref, hot_ref, turned_hot_ref, key_hot_ref, live_ref, tiles_ref,
):
    rows = normed_ref.shape[0]
    own = stream_ref[0]
    far = 1 - own
    queries_ref[...] = (dot_plain(normed_ref[...], w_ref[:, : normed_ref.shape[1]]) + bias_ref[...]).astype(jnp.bfloat16)
    live_ref[...] = mask_ref[far]
    own_codes = code_columns([box_ref[own, 0], box_ref[own, 1], segment_ref[own]], rows)
    far_codes = code_columns([box_ref[far, 0], box_ref[far, 1], segment_ref[far]], rows)
    levels = lax.broadcasted_iota(jnp.int32, (rows, BINS), 1).astype(jnp.float32)
    for axis in range(3):
        lanes = slice(axis * BINS, axis * BINS + BINS)
        column = own_codes[:, axis : axis + 1]
        hot_ref[:, lanes] = jnp.where(column == levels, 1.0, 0.0).astype(jnp.bfloat16)
        turned_hot_ref[:, lanes] = jnp.where(BINS - 1 - column == levels, 1.0, 0.0).astype(jnp.bfloat16)
        key_hot_ref[:, lanes] = jnp.where(far_codes[:, axis : axis + 1] == levels, 1.0, 0.0).astype(jnp.bfloat16)
    half = BINS // 2
    entry = lax.broadcasted_iota(jnp.int32, (BINS, 2 * BINS), 0)
    gap = lax.broadcasted_iota(jnp.int32, (BINS, 2 * BINS), 1)
    gap = jnp.where(gap < BINS, -gap, 2 * BINS - gap)
    pick = jnp.where(jnp.clip(gap, -half, half - 1) + half == entry, 1.0, 0.0).astype(jnp.bfloat16)
    spread = dot_plain(table_ref[...].astype(jnp.bfloat16), pick)
    for index in range(3 * HEADS):
        wide = jnp.broadcast_to(spread[index : index + 1, :], (BINS, 2 * BINS))
        rolled = pltpu.roll(wide, 0, 1, stride=1, stride_axis=0)
        tiles_ref[index] = rolled[:, :BINS].astype(jnp.bfloat16)


def prep_call(stream, box_bins, segment_ids, key_mask, normed, w_qkv, bias_q, table):
    rows, width = normed.shape
    hot = jax.ShapeDtypeStruct((rows, 3 * BINS), jnp.bfloat16)
    outs = [
        jax.ShapeDtypeStruct((rows, width), jnp.bfloat16), hot, hot, hot,
        jax.ShapeDtypeStruct((1, rows), jnp.int32),
        jax.ShapeDtypeStruct((3 * HEADS, BINS, BINS), jnp.bfloat16),
    ]
    return kernel_call(prep_kernel, "prep", 5, outs, stream, box_bins, segment_ids, key_mask, normed, w_qkv, bias_q, table, smem=1)


def half_of(slab, odd):
    lane = lax.broadcasted_iota(jnp.int32, slab.shape, 1)
    keep = (lane >= 64) if odd else (lane < 64)
    return jnp.where(keep, slab, jnp.zeros_like(slab))


def attend_kernel(group, queries_ref, pair_ref, hot_ref, key_hot_ref, live_ref, tiles_ref,
                  context_ref, probs_ref, left_ref, right_ref, scores_ref):
    rows = queries_ref.shape[0]
    part = pair_ref.shape[2]
    def slab_step(slab, carry):
        lanes = pl.ds(pl.multiple_of(slab * 128, 128), 128)
        wide = pl.ds(pl.multiple_of(group * part + slab * 128, 128), 128)
        right_ref[slab, :, :128] = pair_ref[0, :, lanes]
        right_ref[slab, :, 128:] = key_hot_ref[...]
        halves = []
        for odd in range(2):
            head = slab * 2 + odd
            left_ref[head, :, :128] = half_of(queries_ref[:, wide].astype(jnp.float32) * 0.125, odd).astype(jnp.bfloat16)
            for axis in range(3):
                cut = slice(axis * BINS, axis * BINS + BINS)
                tile = tiles_ref[axis * HEADS + group * (part // 64) + head]
                left_ref[head, :, 128 + axis * BINS : 256 + axis * BINS] = dot_plain(hot_ref[:, cut], tile).astype(jnp.bfloat16)
            scores_ref[head] = dot_back(left_ref[head], right_ref[slab])

            def soft(at):
                scores = jnp.where(live_ref[...] > 0, scores_ref[head, at, :], NEGATIVE)
                top = jnp.max(scores, axis=-1, keepdims=True)
                weights = jnp.exp(scores - top)
                rate = 1.0 / jnp.sum(weights, axis=-1, keepdims=True)
                probs_ref[head, at, :] = (weights * rate).astype(jnp.bfloat16)

            strips(rows, soft)
            halves.append(half_of(dot_plain(probs_ref[head], pair_ref[1, :, lanes]), odd))
        context_ref[:, lanes] = (halves[0] + halves[1]).astype(jnp.bfloat16)
        return carry

    lax.fori_loop(0, part // 128, slab_step, 0)


def attend_call(group, queries, pair, hot, key_hot, live, tiles):
    rows = queries.shape[0]
    part = pair.shape[2]
    heads = part // 64
    outs = [
        jax.ShapeDtypeStruct((rows, part), jnp.bfloat16),
        jax.ShapeDtypeStruct((heads, rows, rows), jnp.bfloat16),
    ]
    scratch = [
        pltpu.VMEM((heads, rows, 512), jnp.bfloat16),
        pltpu.VMEM((part // 128, rows, 512), jnp.bfloat16),
        pltpu.VMEM((heads, rows, rows), jnp.float32),
    ]
    return kernel_call(functools.partial(attend_kernel, group), f"attend_{group}", 7, outs,
                       queries, pair, hot, key_hot, live, tiles, scratch=scratch)


def attend_back_kernel(group, queries_ref, pair_ref, turned_hot_ref, key_hot_ref, probs_ref, d_context_ref,
                       d_queries_ref, d_pair_ref, diagonal_ref, right_ref, slope_ref, d_scores_ref):
    rows = queries_ref.shape[0]
    part = pair_ref.shape[2]
    def slab_step(slab, carry):
        lanes = pl.ds(pl.multiple_of(slab * 128, 128), 128)
        wide = pl.ds(pl.multiple_of(group * part + slab * 128, 128), 128)
        right_ref[slab, :, :128] = pair_ref[0, :, lanes]
        right_ref[slab, :, 128:] = key_hot_ref[...]
        d_query = d_key = d_value = 0.0
        for odd in range(2):
            head = slab * 2 + odd
            query = half_of(queries_ref[:, wide], odd)
            d_context = half_of(d_context_ref[:, wide], odd)
            slope_ref[head] = dot_back(d_context, pair_ref[1, :, lanes])

            def soft(at):
                probs = probs_ref[head, at, :].astype(jnp.float32)
                slope = slope_ref[head, at, :]
                centre = jnp.sum(probs * slope, axis=-1, keepdims=True)
                d_scores_ref[head, at, :] = (probs * (slope - centre)).astype(jnp.bfloat16)

            strips(rows, soft)
            d_value = d_value + dot_across(probs_ref[head], d_context)
            d_key = d_key + dot_across(d_scores_ref[head], query)
            both = dot_plain(d_scores_ref[head], right_ref[slab])
            d_query = d_query + half_of(both[:, :128], odd)
            spread = both[:, 128:].astype(jnp.bfloat16)
            for axis in range(3):
                cut = slice(axis * BINS, axis * BINS + BINS)
                tile = dot_across(turned_hot_ref[:, cut], spread[:, cut])
                padded = jnp.concatenate([tile, jnp.zeros_like(tile)], axis=1)
                rolled = pltpu.roll(padded, 0, 1, stride=1, stride_axis=0)
                diagonal_ref[axis, pl.ds(head, 1), :] = jnp.sum(rolled, axis=0, keepdims=True)
        d_queries_ref[:, lanes] = (d_query * 0.125).astype(jnp.bfloat16)
        d_pair_ref[0, :, lanes] = (d_key * 0.125).astype(jnp.bfloat16)
        d_pair_ref[1, :, lanes] = d_value.astype(jnp.bfloat16)
        return carry

    lax.fori_loop(0, part // 128, slab_step, 0)


def attend_back_call(group, queries, pair, turned_hot, key_hot, probs, d_context):
    rows = queries.shape[0]
    part = pair.shape[2]
    heads = part // 64
    outs = [
        jax.ShapeDtypeStruct((rows, part), jnp.bfloat16),
        jax.ShapeDtypeStruct((2, rows, part), jnp.bfloat16),
        jax.ShapeDtypeStruct((3, heads, 2 * BINS), jnp.float32),
    ]
    scratch = [
        pltpu.VMEM((part // 128, rows, 512), jnp.bfloat16),
        pltpu.VMEM((heads, rows, rows), jnp.float32),
        pltpu.VMEM((heads, rows, rows), jnp.bfloat16),
    ]
    return kernel_call(functools.partial(attend_back_kernel, group), f"attend_back_{group}", 8, outs,
                       queries, pair, turned_hot, key_hot, probs, d_context, scratch=scratch)


def early_weights_kernel(
    order_ref, normed_ref, d_branch_ref, context_0_ref, context_1_ref, context_2_ref,
    d_query_0_ref, d_query_1_ref, d_query_2_ref, mine_ref, other_ref, left_ref, right_ref,
):
    part = context_0_ref.shape[1]
    left_ref[0] = normed_ref[...]
    right_ref[1] = d_branch_ref[...]
    pairs = zip((d_query_0_ref, d_query_1_ref, d_query_2_ref), (context_0_ref, context_1_ref, context_2_ref))
    for group, (query_ref, context_ref) in enumerate(pairs):
        lanes = slice(group * part, group * part + part)
        right_ref[0, :, lanes] = query_ref[...]
        left_ref[1, :, lanes] = context_ref[...]

    def block_step(block, carry):
        value = dot_across(left_ref[block], right_ref[block]).astype(jnp.bfloat16)
        rows = pl.ds(pl.multiple_of(block * 48, 16), 48)
        for piece in range(16):
            place_chunk(order_ref[piece], mine_ref, other_ref, value[piece * 48 : piece * 48 + 48], rows)
        return carry

    lax.fori_loop(0, 2, block_step, 0)


def weights_kernel(
    order_ref, normed_ref, back_0_ref, back_1_ref, back_2_ref, early_mine_ref, early_other_ref,
    mine_ref, other_ref, right_ref,
):
    part = back_0_ref.shape[2]
    for group, back_ref in enumerate((back_0_ref, back_1_ref, back_2_ref)):
        lanes = slice(group * part, group * part + part)
        right_ref[0, :, lanes] = back_ref[0]
        right_ref[1, :, lanes] = back_ref[1]
    for early_ref, out_ref in ((early_mine_ref, mine_ref), (early_other_ref, other_ref)):
        out_ref[:, 0:48, :] = early_ref[:, 0:48, :]
        out_ref[:, 144:192, :] = early_ref[:, 48:96, :]

    def block_step(block, carry):
        value = dot_across(normed_ref[...], right_ref[block]).astype(jnp.bfloat16)
        rows = pl.ds(pl.multiple_of(48 + block * 48, 16), 48)
        for piece in range(16):
            place_chunk(order_ref[piece], mine_ref, other_ref, value[piece * 48 : piece * 48 + 48], rows)
        return carry

    lax.fori_loop(0, 2, block_step, 0)


def early_weights_call(order, normed, d_branch, contexts, d_queries):
    rows, width = normed.shape
    ring = jax.ShapeDtypeStruct((RING, 96, width), jnp.bfloat16)
    scratch = [pltpu.VMEM((2, rows, width), jnp.bfloat16), pltpu.VMEM((2, rows, width), jnp.bfloat16)]
    return kernel_call(early_weights_kernel, "early_weights", 5, [ring, ring], order, normed, d_branch,
                       *contexts, *d_queries, scratch=scratch, smem=1)


def weights_call(order, normed, backs, early):
    rows, width = normed.shape
    ring = jax.ShapeDtypeStruct((RING, 192, width), jnp.bfloat16)
    scratch = [pltpu.VMEM((2, rows, width), jnp.bfloat16)]
    return kernel_call(weights_kernel, "weights", 5, [ring, ring], order, normed, *backs, *early,
                       scratch=scratch, smem=1)


def last_kernel(
    side_ref, tokens_ref, gain_ref, w_ref, d_middle_ref, d_query_0_ref, d_query_1_ref, d_query_2_ref,
    back_0_ref, back_1_ref, back_2_ref, diagonal_0_ref, diagonal_1_ref, diagonal_2_ref, start_ref,
    g_tokens_ref, mine_ref, other_ref, small_ref, d_normed_ref, sums_ref,
):
    rows, width = tokens_ref.shape
    part = width // GROUPS
    queries = (d_query_0_ref, d_query_1_ref, d_query_2_ref)
    backs = (back_0_ref, back_1_ref, back_2_ref)
    small_ref[...] = start_ref[...]
    sums_ref[...] = jnp.zeros_like(sums_ref)
    total = 0.0
    for group in range(GROUPS):
        at = group * part
        total = total + dot_back(queries[group][...], w_ref[:, at : at + part])
        total = total + dot_back(backs[group][0], w_ref[:, width + at : width + at + part])
        total = total + dot_back(backs[group][1], w_ref[:, 2 * width + at : 2 * width + at + part])
    d_normed_ref[...] = total

    def final(at):
        hat, rate = row_stats(tokens_ref[at, :].astype(jnp.float32))
        d_normed = d_normed_ref[at, :]
        sums_ref[0] += fold(d_normed * hat)
        sums_ref[1] += fold(d_normed)
        for group in range(GROUPS):
            lanes = slice(group * part, group * part + part)
            sums_ref[2, :, lanes] += fold(queries[group][at, :].astype(jnp.float32))
            sums_ref[3, :, lanes] += fold(backs[group][1, at, :].astype(jnp.float32))
        scaled = d_normed * gain_ref[...]
        inner = (
            scaled
            - jnp.mean(scaled, axis=-1, keepdims=True)
            - hat * jnp.mean(scaled * hat, axis=-1, keepdims=True)
        )
        g_tokens_ref[at, :] = (d_middle_ref[at, :] + rate * inner).astype(jnp.bfloat16)

    strips(rows, final)
    for row in range(4):
        put_halves(small_ref, row, jnp.sum(sums_ref[row], axis=0, keepdims=True))
    half = BINS // 2
    gap = BINS - 1 - lax.broadcasted_iota(jnp.int32, (2 * BINS, BINS), 0)
    entry = lax.broadcasted_iota(jnp.int32, (2 * BINS, BINS), 1)
    pick = jnp.where(jnp.clip(gap, -half, half - 1) + half == entry, 1.0, 0.0)
    for group, diagonal_ref in enumerate((diagonal_0_ref, diagonal_1_ref, diagonal_2_ref)):
        for axis in range(3):
            table = lax.dot_general(
                diagonal_ref[axis], pick, (((1,), (0,)), ((), ())),
                precision=HIGHEST, preferred_element_type=jnp.float32,
            )
            for head in range(part // 64):
                index = axis * HEADS + group * (part // 64) + head
                side, place = divmod(index, 18)
                row, lane = divmod(place, 3)
                small_ref[side, 12 + row : 13 + row, lane * BINS : lane * BINS + BINS] = table[head : head + 1, :]
    for out_ref, side in ((mine_ref, side_ref[0]), (other_ref, 1 - side_ref[0])):
        out_ref[...] = jnp.zeros_like(out_ref)
        out_ref[:12, :384] = small_ref[side, :12, :]
        out_ref[:12, 384:] = small_ref[side, 12:, :]


def last_call(side, tokens, gain, w_qkv, d_middle, d_queries, backs, diagonals, start):
    rows, width = tokens.shape
    packed = jax.ShapeDtypeStruct((16, width), jnp.float32)
    outs = [jax.ShapeDtypeStruct((rows, width), jnp.bfloat16), packed, packed]
    scratch = [pltpu.VMEM(start.shape, jnp.float32), pltpu.VMEM((rows, width), jnp.float32), pltpu.VMEM((4, 8, width), jnp.float32)]
    return kernel_call(last_kernel, "last", 8, outs, side, tokens, gain, w_qkv, d_middle,
                       *d_queries, *backs, *diagonals, start, scratch=scratch, smem=1)


def open_kernel(layout, place_ref, *refs):
    width = refs[0].shape[1]
    for out_ref, (start, blocks) in zip(refs[RING:], layout):
        size = out_ref.shape[0] // RING
        for index in range(RING):
            to = pl.ds(pl.multiple_of(place_ref[index] * size, size), size)
            for block in range(blocks):
                at = start + block * size
                out_ref[to, block * width : block * width + width] = refs[index][at : at + size, :].astype(jnp.float32)


def open_rest_kernel(place_ref, *refs):
    chunks, outs, parts_ref = refs[:RING], refs[RING:-1], refs[-1]
    open_kernel(((0, 3), (144, 1)), place_ref, *chunks, outs[0], outs[1])
    for index in range(RING):
        parts_ref[place_ref[index]] = chunks[index][192:, :].astype(jnp.float32)
    total = parts_ref[0]
    for index in range(1, RING):
        total = total + parts_ref[index]
    parts_ref[0] = total
    for row in range(8):
        outs[2 + row][...] = parts_ref[0, row : row + 1, :384]
    for row in range(4):
        outs[10][:, row * 384 : row * 384 + 384] = parts_ref[0, 8 + row : 9 + row, :384]
    for row in range(6):
        outs[11][:, row * 384 : row * 384 + 384] = parts_ref[0, row : row + 1, 384:]


def open_call(name, places, chunks):
    width = chunks[0].shape[1]
    half = width // 2
    if name == "rest":
        shapes = [(half, 3 * width), (half, width)] + [(1, half)] * 8 + [(1, 2 * width), (1, 3 * width)]
        kernel, scratch = open_rest_kernel, [pltpu.VMEM((RING, 16, width), jnp.float32)]
    else:
        shapes = [(2 * width, width)] if name == "back" else [(half, 4 * width)]
        kernel, scratch = functools.partial(open_kernel, ((0, shapes[0][1] // width),)), []
    outs = [jax.ShapeDtypeStruct(shape, jnp.float32) for shape in shapes]
    return kernel_call(kernel, f"open_{name}", 4, outs, places, *chunks, smem=1, scratch=scratch)


def partner_2(shard, axis, distance):
    return lax.ppermute(shard, axis, [(i, i ^ 1 << distance) for i in range(lax.axis_size(axis))])


def ring_send(chunk):
    pairs = []
    for place in range(RING):
        ahead = RING_ORDER[(place + 1) % RING]
        behind = RING_ORDER[(place - 1) % RING]
        pairs.append((RING_ORDER[place] * 2, ahead * 2))
        pairs.append((RING_ORDER[place] * 2 + 1, behind * 2 + 1))
    return lax.ppermute(chunk, ("group", "dp"), pairs)


def ring_place():
    group = lax.axis_index("group")
    place = jnp.int32(0)
    for position, member in enumerate(RING_ORDER):
        place = jnp.where(group == member, position, place)
    return place


def ring_plan(ringed):
    index = lax.iota(jnp.int32, 2 * RING)
    steps = lax.iota(jnp.int32, RING)
    if not ringed:
        return index, steps
    dp = lax.axis_index("dp")
    place = ring_place()
    side = index // RING
    start = jnp.where(side == 0, place, RING - place)
    order = (start - index % RING + RING) % RING + jnp.where(side == dp, 0, RING)
    start = jnp.where(dp == 0, place, RING - place)
    return order, (start + 1 - steps + RING) % RING


def add_low(*terms):
    return sum(term.astype(jnp.float32) for term in terms).astype(jnp.bfloat16)


def unringed_total(mine, other):
    return lax.psum(jnp.concatenate([mine, other]).astype(jnp.float32), ("group", "dp"))


def unringed_rows(packed):
    blocks = packed.shape[1] // 48
    rows = packed.reshape(2 * RING, blocks, 48, packed.shape[2])
    return jnp.swapaxes(rows, 1, 2).reshape(2 * RING * 48, blocks * packed.shape[2])


def own_share(whole):
    share = whole.shape[0] // lax.axis_size("dp")
    return lax.dynamic_slice_in_dim(whole, lax.axis_index("dp") * share, share, 0)[None]


def unringed_grads(feed, rest, small):
    feed = unringed_total(*feed)
    rest = unringed_total(*rest)
    small = lax.psum(jnp.stack(small)[:, :12], ("group", "dp"))
    small = jnp.concatenate([small[:, :, :384], small[:, :, 384:]], axis=1)
    vectors = [small[:, row].reshape(-1) for row in range(8)]
    vectors += [small[:, 8:12].reshape(-1), small[:, 12:18].reshape(-1)]
    weights = (
        feed[:, :192].reshape(-1, feed.shape[2]),
        unringed_rows(feed[:, 192:]),
        unringed_rows(rest[:, :144]),
        unringed_rows(rest[:, 144:]),
    )
    return [own_share(weight) for weight in weights], [own_share(vector) for vector in vectors]


LAST_STEP = 3
LAST_SPAN = 1


class Ordered:
    def __init__(self):
        self.mark = None
        self.free = False

    def after(self, value):
        if self.mark is None or self.free:
            return value
        return lax.optimization_barrier((value, self.mark))[0]

    def wait(self, *values):
        self.mark = (self.mark, *values)


class Ring:
    def __init__(self, order, mine, other):
        self.order, self.mine = order, mine
        self.met = lax.ppermute(order.after(other), "dp", [(0, 1), (1, 0)])
        self.arrived, self.step = None, 0

    def reduce(self):
        step, order = self.step, self.order
        if step == 0:
            held = add_low(self.mine[0], order.after(self.met)[0])
        else:
            held = add_low(order.after(self.arrived), self.mine[step], self.met[step])
        order.mark = held
        if step < RING - 1:
            self.arrived = ring_send(held)
        self.step += 1
        return held

    def split(self, cuts):
        pieces = []
        for start, stop in zip(cuts, cuts[1:]):
            piece = Ring.__new__(Ring)
            piece.order, piece.step = self.order, self.step
            piece.mine, piece.met = self.mine[:, start:stop], self.met[:, start:stop]
            piece.arrived = None if self.arrived is None else self.arrived[start:stop]
            pieces.append(piece)
        return pieces


def gather(held, waits={}):
    chunks = [held]
    for step in range(1, RING):
        held = ring_send(held)
        if step in waits:
            held = waits[step](held)
        chunks.append(held)
    return chunks


def on_device(
    tokens, cotangent, box_bins, segment_ids, key_mask, ln1_gain, ln1_bias, w_qkv, bias_q, bias_v,
    w_out, bias_out, ln2_gain, ln2_bias, w_in, bias_in, w_back, bias_back, rel_table,
):
    ringed = lax.axis_size("group") == RING and lax.axis_size("dp") == 2
    width = tokens.shape[2]
    order, places = ring_plan(ringed)
    queue = Ordered()
    stream = lax.axis_index("stream").reshape(1)
    normed, *sent = first_call(tokens[0], ln1_gain, ln1_bias, w_qkv[0], bias_v)
    pairs = [partner_2(pair, "stream", 0) for pair in sent]
    queries, hot, turned_hot, key_hot, live, tiles = prep_call(
        stream, box_bins, segment_ids, key_mask, normed, w_qkv[0], bias_q, rel_table.reshape(3 * HEADS, BINS)
    )
    contexts, probs = [], []
    for group in range(GROUPS):
        context, prob = attend_call(group, queries, queue.after(pairs[group]), hot, key_hot, live, tiles)
        queue.mark = context
        contexts.append(context)
        probs.append(prob)
    output, d_middle, d_branch, d_context, feed_mine, feed_other, small = feed_call(
        order, tokens[0], contexts, cotangent[0], w_out[0], bias_out, ln2_gain, ln2_bias,
        w_in[0], bias_in, w_back[0], bias_back,
    )
    if ringed:
        feed = Ring(queue, feed_mine, feed_other)
    d_queries, backs, diagonals = [None] * GROUPS, [None] * GROUPS, [None] * GROUPS
    for group in range(GROUPS):
        d_queries[group], d_pair, diagonals[group] = attend_back_call(
            group, queries, pairs[group], turned_hot, key_hot, probs[group], queue.after(d_context)
        )
        queue.mark = d_queries[group]
        if ringed:
            if group == GROUPS - 1:
                feed.reduce()
                d_pair = queue.after(d_pair)
            backs[group] = partner_2(d_pair, "stream", 0)
            if group < GROUPS - 1:
                feed.reduce()
            if group == 1:
                queue.wait(backs[0])
        else:
            backs[group] = partner_2(d_pair, "stream", 0)
    early = early_weights_call(order, queue.after(normed), d_branch, contexts, d_queries)
    rest_mine, rest_other = weights_call(order, normed, backs, early)
    if ringed:
        queue.mark = rest_mine
        feed.reduce()
        rest = Ring(queue, rest_mine, rest_other)
    side = lax.axis_index("dp").reshape(1)
    if not ringed:
        g_tokens, *small = last_call(
            jnp.zeros_like(side), tokens[0], ln1_gain, w_qkv[0], d_middle, d_queries, backs, diagonals, small
        )
    if ringed:
        rest.reduce()
        queue.free = True
        held_parts = []
        for piece in feed.split((0, 192, 384)):
            while piece.step < RING:
                held = piece.reduce()
            held_parts.append(held)
        back_chunks = gather(held_parts[0])
        in_chunks = gather(held_parts[1])
        g_w_back = open_call("back", places, back_chunks)
        g_w_in = open_call("inward", places, in_chunks)
        opened = [*g_w_back, *g_w_in]

        def back_turn(value):
            value, opened[0] = lax.optimization_barrier((value, opened[0]))
            return value

        def in_turn(value):
            value, opened[1] = lax.optimization_barrier((value, opened[1]))
            return value

        while rest.step < RING:
            if rest.step == LAST_STEP + LAST_SPAN:
                rest.arrived, g_tokens = lax.optimization_barrier((rest.arrived, g_tokens))
            rest_held = rest.reduce()
            if rest.step == LAST_STEP:
                ready = lax.optimization_barrier((d_middle, rest_held))[0]
                g_tokens, *small = last_call(
                    side, tokens[0], ln1_gain, w_qkv[0], ready, d_queries, backs, diagonals, small
                )
        small_held = add_low(small[0], lax.ppermute(small[1], "dp", [(0, 1), (1, 0)]))
        rest_held = jnp.concatenate([rest_held, small_held], axis=0)
        rest_chunks = gather(rest_held, {6: back_turn, 7: in_turn})
        opened += open_call("rest", places, rest_chunks)
        weights = [value[None] for value in opened[:4]]
        vectors = opened[4:]
    else:
        weights, vectors = unringed_grads(
            (feed_mine, feed_other), (rest_mine, rest_other), small
        )
    g_w_back, g_w_in, g_w_qkv, g_w_out = weights
    (
        g_ln1_gain, g_ln1_bias, g_bias_q, g_bias_v, g_bias_out, g_ln2_gain, g_ln2_bias, g_bias_back, g_bias_in, g_rel_table,
    ) = vectors
    return (
        output[None], g_tokens[None], g_ln1_gain, g_ln1_bias, g_w_qkv, g_bias_q, g_bias_v, g_w_out,
        g_bias_out, g_ln2_gain, g_ln2_bias, g_w_in, g_bias_in, g_w_back, g_bias_back, g_rel_table,
    )


def solution(mesh):
    placed = (
        P("stream", ("group", "dp"), None),
        P("stream", ("group", "dp"), None),
        P(None, None, ("group", "dp"), None),
        P(None, ("group", "dp"), None),
        P(None, ("group", "dp"), None),
        P("stream", None),
        P("stream", None),
        P("stream", None, None),
        P("stream", None),
        P("stream", None),
        P("stream", None, None),
        P("stream", None),
        P("stream", None),
        P("stream", None),
        P("stream", None, None),
        P("stream", None),
        P("stream", None, None),
        P("stream", None),
        P("stream", None),
    )
    return jax.shard_map(
        on_device,
        mesh=mesh,
        in_specs=placed,
        out_specs=(
            P("stream", ("group", "dp"), None),
            P("stream", ("group", "dp"), None),
            P("stream", "dp"),
            P("stream", "dp"),
            P("stream", "dp", None),
            P("stream", "dp"),
            P("stream", "dp"),
            P("stream", "dp", None),
            P("stream", "dp"),
            P("stream", "dp"),
            P("stream", "dp"),
            P("stream", "dp", None),
            P("stream", "dp"),
            P("stream", "dp", None),
            P("stream", "dp"),
            P("stream", "dp"),
        ),
        check_vma=False,
    )
```
